512 devices in a mesh: seq: 64 (over x, z), tp: 8 (over y, core).
Axes of the slice: x: 4, y: 4, z: 16, core: 2. Of those that a mesh axis runs over, the one named last changes fastest.
Arguments:
- queries: bfloat16 [4, 1024], P(None, 'tp'), may hold values from -6 to 6
- keys_new: bfloat16 [4, 1024], P(None, 'tp'), may hold values from -32 to 32
- values_new: bfloat16 [4, 1024], P(None, 'tp'), may hold values from -6 to 6
- key_cache: bfloat16 [4, 4096, 1024], P(None, 'seq', 'tp'), may hold values from -32 to 32
- value_cache: bfloat16 [4, 4096, 1024], P(None, 'seq', 'tp'), may hold values from -6 to 6
- buckets: int32 [4, 4096], P(None, 'seq'), may hold values from 0 to 31
- lengths: int32 [4], replicated, may hold values from 1 to 4096, as said below
- bias_table: float32 [32, 16], replicated, may hold values from -3 to 3
- out_proj: bfloat16 [1024, 1024], P('tp'), may hold values from -0.1875 to 0.1875
- decode_in: bfloat16 [4, 1024], replicated, may hold values from -6 to 6
- prefill_in: bfloat16 [32768, 1024], P(('seq', 'tp')), may hold values from -6 to 6
- routes: int32 [32768, 2], P(('seq', 'tp')), may hold values from 0 to 15, all different within a row; in each aligned block of 64 rows (0 to 63, 64 to 127, ...) at most 10 rows name the same one
- gates: float32 [32768, 2], P(('seq', 'tp')), may hold values from 0.2 to 1
- dec_routes: int32 [4, 2], replicated, may hold values from 0 to 15, as said below
- dec_gates: float32 [4, 2], replicated, may hold values from 0.2 to 1
- norm_gain: float32 [1024], replicated, may hold values from 0.1 to 1.9
- w_gate: bfloat16 [1024, 45056], P('tp', 'seq'), may hold values from -0.1875 to 0.1875
- w_up: bfloat16 [1024, 45056], P('tp', 'seq'), may hold values from -0.1875 to 0.1875
- w_down: bfloat16 [45056, 1024], P('seq', 'tp'), may hold values from -0.109375 to 0.109375
Outputs:
- decode_out: bfloat16 [4, 1024], replicated
- prefill_out: bfloat16 [32768, 1024], P(('seq', 'tp'))
The draws below stay inside these ranges and needn't reach their ends.
Inputs may be any that keep to these rules, and one draw needn't show every extreme that they name: `routes`: in the 64 rows of one device no expert is named by more than 10 rows, a bound that some block reaches. `dec_routes`: the two experts of a decode token differ; some decode token names expert 0 and some names expert 16 - 1. `lengths`: some request has all 4096 positions and some has exactly 1.
All inputs are finite; a program needn't handle non-finite values.
Results may differ from the reference program's by a relative error of at most 0.0075.
Values may be sent and summed in bfloat16 or wider, within the bound.
A program may use at most 64 MiB of HBM per device.

```python
import math
import jax
import jax.numpy as jnp
import numpy as np
from jax import lax

D = 1024
H = 16
HD = 64
EXPERTS = 16
FF = 2816
NB = 32
TOP = 2
DEC = 4
PRE_DEV = 64
PREFILL = 32768
CTX = 4096
HHD = 1024
SHARDS = 4
CAP = 10
DEVICES = 512


def draw_queries(key, part):
    drawn_draw = jnp.clip(jax.random.normal(jax.random.fold_in(key, 1), (DEC, HHD), jnp.float32), -6.0, 6.0)
    return drawn_draw.astype(jnp.bfloat16)


def draw_keys_new(key, part):
    drawn_draw = jnp.clip(jax.random.normal(jax.random.fold_in(key, 2), (DEC, HHD), jnp.float32), -6.0, 6.0)
    return drawn_draw.astype(jnp.bfloat16)


def draw_key_cache(key, part):
    drawn_draw = jnp.clip(jax.random.normal(jax.random.fold_in(key, 3), (DEC, CTX, HHD), jnp.float32), -6.0, 6.0)
    return drawn_draw.astype(jnp.bfloat16)


def draw_lengths(key, part):
    base_key = jax.random.fold_in(key, 202)
    key_left, key_right, key_long = jax.random.split(base_key, 3)
    left_draw = jax.random.randint(key_left, (DEC,), 0, CTX)
    right_draw = jax.random.randint(key_right, (DEC,), 0, CTX)
    lengths = 1 + left_draw * right_draw // CTX
    longest = jax.random.randint(key_long, (), 0, DEC)
    positions = jnp.arange(DEC)
    lengths = jnp.where(positions == longest, CTX, lengths)
    lengths = jnp.where(positions == (longest + 1) % DEC, 1, lengths)
    return lengths.astype(jnp.int32)


def draw_dec_routes(key, part):
    base_key = jax.random.fold_in(key, 303)
    key_first, key_step, key_row = jax.random.split(base_key, 3)
    first_choice = jax.random.randint(key_first, (DEC,), 0, EXPERTS)
    top_row = jax.random.randint(key_row, (), 0, DEC)
    rows = jnp.arange(DEC)
    first_choice = jnp.where(rows == top_row, EXPERTS - 1, first_choice)
    first_choice = jnp.where(rows == (top_row + 1) % DEC, 0, first_choice)
    step_choice = jax.random.randint(key_step, (DEC,), 1, EXPERTS)
    second_choice = (first_choice + step_choice) % EXPERTS
    return jnp.stack([first_choice, second_choice], axis=1).astype(jnp.int32)


def touch_ends(array, own_key, low, top_value):
    index_at = [jax.random.randint(jax.random.fold_in(own_key, axis), (), 0, length) for axis, length in enumerate(array.shape)]
    widest = array.shape.index(max(array.shape))
    neighbour = index_at[:widest] + [(index_at[widest] + 1) % array.shape[widest]] + index_at[widest + 1:]
    return array.at[tuple(index_at)].set(low).at[tuple(neighbour)].set(top_value)


def levels(rng, dims, cuts, low, largest):
    factor_of = 1.0
    for axis_at, shards_of in cuts:
        heights = jax.random.uniform(jax.random.fold_in(jax.random.fold_in(rng, 6), axis_at), (shards_of,), jnp.float32, low / len(cuts), largest / len(cuts))
        factor_of = factor_of * jnp.repeat(jnp.exp(heights), dims[axis_at] // shards_of).reshape((-1,) + (1,) * (len(dims) - 1 - axis_at))
    return factor_of


def assign_block(rng, own, number, rows, count, top, most, skew):
    ranking = jax.random.permutation(rng, count)
    crowded, common = load_shares(count, rows * top, most, skew, True), load_shares(count, rows * top, most, skew, False)
    places = jnp.arange(count)

    def named(sizes, offset_by):
        used = int((sizes > 0).sum())
        fixed = max(1, used // 4)
        moved = fixed + (places - fixed + offset_by * (used - fixed)) % max(1, count - fixed)
        return jnp.zeros((count,), jnp.int32).at[ranking[jnp.where(places < fixed, places, moved)]].set(jnp.asarray(sizes, jnp.int32))

    sizes = jnp.where(number % 4 == 0, named(crowded, number // 4), named(common, number - number // 4 - 1))
    mixed = jax.random.permutation(jax.random.fold_in(own, 3), count)
    source_of, sink = mixed[0:count // 2 * 2:2], mixed[1:count // 2 * 2:2]
    slack = jnp.minimum(sizes[source_of] - 1, most - sizes[sink]) // 2
    slack = jnp.where((source_of == ranking[0]) | (sink == ranking[0]) | (sizes[sink] == 0), 0, jnp.maximum(slack, 0))
    moved = jax.random.randint(jax.random.fold_in(own, 4), (count // 2,), 0, 1 << 20) % (slack + 1)
    sizes = sizes.at[source_of].add(-moved).at[sink].add(moved)
    items = jnp.searchsorted(jnp.cumsum(sizes), jnp.arange(rows * top), side="right").astype(jnp.int32)
    listing = items.reshape(top, rows).T
    listing = listing[jax.random.permutation(jax.random.fold_in(own, 1), rows)]
    offset_by = jax.random.randint(jax.random.fold_in(own, 2), (rows, 1), 0, top)
    return jnp.take_along_axis(listing, (jnp.arange(top)[None, :] + offset_by) % top, axis=1)


def load_shares(count, total, most, slope, full):
    portions = [(1 << 20) // math.isqrt(rank ** slope) + 1 for rank in range(1, count + 1)]
    largest = most if full else min(most, max(-(-total // count), total * portions[0] // sum(portions)))
    least = 1 if total - largest >= count - 1 else 0
    holding, rest = [largest] + [least] * (count - 1), total - largest - least * (count - 1)
    while rest > 0:
        movable = [i for i in range(1, count) if holding[i] < largest] or [i for i in range(1, count) if holding[i] < most]
        whole, remaining = sum([portions[i] for i in movable]), rest
        for i in movable:
            extra = min(most - holding[i], max(1, remaining * portions[i] // whole), rest)
            holding[i] = holding[i] + extra
            rest = rest - extra
    return np.array(holding)


def scatter_about(own_key, dims, deviation, reach, pieces=(), held_as=jnp.bfloat16):
    values = deviation * jax.random.normal(own_key, dims, jnp.float32)
    if pieces:
        values = values * levels(own_key, dims, pieces, -0.22, 0.18)
    return jnp.clip(values, -reach, reach).astype(held_as)


def setup_inputs(seed: int = 0) -> dict:
    key_list = jax.random.split(jax.random.key(seed), 20)
    queries = draw_queries(jax.random.fold_in(key_list[19], 71), 0)
    keys_new = draw_keys_new(jax.random.fold_in(key_list[19], 71), 0)
    values_new = scatter_about(key_list[2], (DEC, HHD), 1.0, 6.0, ((1, 8),))
    key_cache = draw_key_cache(jax.random.fold_in(key_list[19], 71), 0)
    value_cache = scatter_about(key_list[4], (DEC, CTX, HHD), 1.0, 6.0, ((1, 64), (2, 8)))
    buckets = touch_ends(jax.random.randint(key_list[5], (DEC, CTX), 0, NB), jax.random.fold_in(key_list[5], 1), 0, NB - 1).astype(jnp.int32)
    lengths = draw_lengths(jax.random.fold_in(key_list[19], 71), 0)
    bias_table = scatter_about(key_list[7], (NB, H), 0.5, 3.0, (), jnp.float32)
    out_proj = scatter_about(key_list[8], (HHD, D), HHD ** -0.5, 0.1875, ((0, 8),))
    decode_in = scatter_about(key_list[9], (DEC, D), 1.0, 6.0)
    prefill_in = scatter_about(key_list[10], (PREFILL, D), 1.0, 6.0, ((0, 512),))
    routes_keys = jax.random.split(jax.random.fold_in(key_list[11], 1), PREFILL // PRE_DEV)
    routes_turns = jax.random.permutation(jax.random.fold_in(key_list[11], 3), PREFILL // PRE_DEV)
    routes = jax.vmap(lambda own, number: assign_block(jax.random.fold_in(key_list[11], 2), own, number, PRE_DEV, EXPERTS, TOP, CAP, 1))(routes_keys, routes_turns).reshape((PREFILL, TOP))
    gates = jnp.clip(0.2 + 0.8 * jax.random.uniform(key_list[12], (PREFILL, TOP), jnp.float32) ** levels(key_list[12], (PREFILL, TOP), ((0, 512),), -0.2, 0.2), 0.2, 1.0)
    dec_routes = draw_dec_routes(jax.random.fold_in(key_list[19], 71), 0)
    dec_gates = jnp.clip(jax.random.uniform(key_list[14], (DEC, TOP), jnp.float32, 0.2, 1.0), 0.2, 1.0)
    norm_gain = jnp.clip(1.0 + 0.18 * jax.random.normal(key_list[15], (D,), jnp.float32), 0.1, 1.9)
    w_gate = scatter_about(key_list[16], (D, EXPERTS * FF), D ** -0.5, 0.1875, ((0, 8), (1, 64)))
    w_up = scatter_about(key_list[17], (D, EXPERTS * FF), D ** -0.5, 0.1875, ((0, 8), (1, 64)))
    w_down = scatter_about(key_list[18], (EXPERTS * FF, D), FF ** -0.5, 0.109375, ((0, 64), (1, 8)))
    return dict(queries=queries, keys_new=keys_new, values_new=values_new, key_cache=key_cache, value_cache=value_cache, buckets=buckets, lengths=lengths, bias_table=bias_table, out_proj=out_proj, decode_in=decode_in, prefill_in=prefill_in, routes=routes, gates=gates, dec_routes=dec_routes, dec_gates=dec_gates, norm_gain=norm_gain, w_gate=w_gate, w_up=w_up, w_down=w_down)


def route_slots(route_rows, capacity):
    flat_routes = route_rows.reshape(-1)
    onehot = (flat_routes[:, None] == jnp.arange(EXPERTS, dtype=jnp.int32)[None, :]).astype(jnp.int32)
    earlier = jnp.cumsum(onehot, axis=0) - onehot
    slot_rank = lax.optimization_barrier(jnp.sum(earlier * onehot, axis=1))
    return (flat_routes * capacity + slot_rank).astype(jnp.int32)

def rms_scale(hidden, norm_gain):
    values = hidden.astype(jnp.float32)
    meansq = lax.optimization_barrier(jnp.mean(values * values, axis=-1, keepdims=True))
    return (values * lax.rsqrt(meansq + 1e-06) * norm_gain).astype(jnp.bfloat16)

def expert_parts(rows, expert, w_gate, w_up, w_down):
    shard_width = FF // SHARDS
    gate_cols = lax.dynamic_slice_in_dim(w_gate, expert * FF, FF, 1)
    up_cols = lax.dynamic_slice_in_dim(w_up, expert * FF, FF, 1)
    down_rows = lax.dynamic_slice_in_dim(w_down, expert * FF, FF, 0)
    gate_pre = jnp.dot(rows, gate_cols, preferred_element_type=jnp.float32)
    up_pre = jnp.dot(rows, up_cols, preferred_element_type=jnp.float32)
    act = (jax.nn.gelu(gate_pre, approximate=True) * up_pre).astype(jnp.bfloat16)
    result = jnp.zeros((rows.shape[0], D), jnp.float32)
    for shard in range(SHARDS):
        part = jnp.dot(act[:, shard * shard_width:(shard + 1) * shard_width], down_rows[shard * shard_width:(shard + 1) * shard_width], preferred_element_type=jnp.float32).astype(jnp.bfloat16)
        part = lax.optimization_barrier(part)
        result = result + part.astype(jnp.float32)
    return result

def reference(queries, keys_new, values_new, key_cache, value_cache, buckets, lengths, bias_table, out_proj, decode_in, prefill_in, routes, gates, dec_routes, dec_gates, norm_gain, w_gate, w_up, w_down):
    score_scale = 1.0 / math.sqrt(HD)
    positions = jnp.arange(CTX, dtype=jnp.int32)
    query_f = queries.astype(jnp.float32).reshape(DEC, H, HD)
    key_f = key_cache.astype(jnp.float32).reshape(DEC, CTX, H, HD)
    value_f = value_cache.astype(jnp.float32).reshape(DEC, CTX, H, HD)
    bias_rows = jnp.transpose(bias_table[buckets], (0, 2, 1))
    scores = jnp.einsum('rhd,rchd->rhc', query_f, key_f, precision=lax.Precision.HIGHEST) * score_scale + bias_rows
    valid_mask = (positions[None, :] < lengths[:, None])[:, None, :]
    scores = jnp.where(valid_mask, scores, -1e+30)
    own_score = lax.optimization_barrier(jnp.sum(query_f * keys_new.astype(jnp.float32).reshape(DEC, H, HD), axis=-1)) * score_scale + bias_table[0][None, :]
    peak = jnp.maximum(lax.optimization_barrier(jnp.max(scores, axis=-1)), own_score)
    weights = jnp.where(valid_mask, jnp.exp(scores - peak[..., None]), 0.0)
    own_weight = jnp.exp(own_score - peak)
    weight_total = lax.optimization_barrier(jnp.sum(weights, axis=-1)) + own_weight
    weighted = jnp.einsum('rhc,rchd->rhd', weights, value_f, precision=lax.Precision.HIGHEST)
    weighted = weighted + own_weight[..., None] * values_new.astype(jnp.float32).reshape(DEC, H, HD)
    mixed_rows = (weighted / weight_total[..., None]).astype(jnp.bfloat16).reshape(DEC, HHD)
    attended = jnp.dot(mixed_rows, out_proj, preferred_element_type=jnp.float32)
    decode_hidden = (decode_in.astype(jnp.float32) + attended).astype(jnp.bfloat16)
    normed_dec = rms_scale(decode_hidden, norm_gain)

    def run_dec(expert):
        return expert_parts(normed_dec, expert, w_gate, w_up, w_down)
    dec_results = lax.map(run_dec, jnp.arange(EXPERTS, dtype=jnp.int32))
    row_ids = jnp.arange(DEC, dtype=jnp.int32)[:, None]
    dec_picked = dec_results[dec_routes, row_ids]
    decode_out = (decode_hidden.astype(jnp.float32) + lax.optimization_barrier(jnp.sum(dec_gates[..., None] * dec_picked, axis=1))).astype(jnp.bfloat16)
    normed = rms_scale(prefill_in, norm_gain).reshape(DEVICES, PRE_DEV, D)

    def block_slots(route_rows):
        return route_slots(route_rows, CAP)
    flat_index = jax.vmap(block_slots)(routes.reshape(DEVICES, PRE_DEV, TOP))

    def pack_block(normed_rows, index_rows):
        source = jnp.repeat(normed_rows, TOP, axis=0)
        return jnp.zeros((EXPERTS * CAP, D), normed_rows.dtype).at[index_rows].set(source)
    packed = jax.vmap(pack_block)(normed, flat_index)

    def run_expert(expert):
        expert_rows = lax.dynamic_slice_in_dim(packed, expert * CAP, CAP, 1).reshape(DEVICES * CAP, D)
        return expert_parts(expert_rows, expert, w_gate, w_up, w_down)
    results = lax.map(run_expert, jnp.arange(EXPERTS, dtype=jnp.int32)).reshape(EXPERTS, DEVICES, CAP, D)
    device_ids = jnp.arange(DEVICES, dtype=jnp.int32)[:, None]
    picked = results[flat_index // CAP, device_ids, flat_index % CAP]
    gate_rows = gates.reshape(DEVICES, PRE_DEV, TOP)
    combined = prefill_in.astype(jnp.float32).reshape(DEVICES, PRE_DEV, D) + lax.optimization_barrier(jnp.sum(gate_rows[..., None] * picked.reshape(DEVICES, PRE_DEV, TOP, D), axis=2))
    prefill_out = combined.astype(jnp.bfloat16).reshape(PREFILL, D)
    return (decode_out, prefill_out)
```

```python
import functools
import math

import jax
import jax.numpy as jnp
from jax import lax
from jax.experimental import pallas as pl
from jax.experimental.pallas import tpu as pltpu
from jax.sharding import PartitionSpec as P

HD = 64
EXPERTS = 16
TOP = 2
CAP = 10


def peer_device(axis, peer):
    if axis == "seq":
        return (peer, lax.axis_index("tp"))
    return (lax.axis_index("seq"), peer)


def gather_kernel(axis, count, x_ref, out_ref, landed, send_sem, recv_sem):
    me = lax.axis_index(axis)
    barrier = pltpu.get_barrier_semaphore()

    def greet(step, carry):
        pl.semaphore_signal(
            barrier,
            inc=1,
            device_id=peer_device(axis, lax.rem(me + step, count)),
            device_id_type=pl.DeviceIdType.MESH,
        )
        return carry

    lax.fori_loop(1, count, greet, 0)
    pl.semaphore_wait(barrier, count - 1)

    def transfer(step):
        return pltpu.make_async_remote_copy(
            src_ref=x_ref,
            dst_ref=landed.at[me],
            send_sem=send_sem.at[step],
            recv_sem=recv_sem.at[step],
            device_id=peer_device(axis, lax.rem(me + step, count)),
            device_id_type=pl.DeviceIdType.MESH,
        )

    def launch(step, carry):
        transfer(step).start()
        return carry

    lax.fori_loop(1, count, launch, 0)
    landed[me] = x_ref[...]

    def finish(step, carry):
        transfer(step).wait()
        return carry

    lax.fori_loop(1, count, finish, 0)
    out_ref[...] = landed[...]


def axis_gather(x, axis, count, collective_id):
    stacked = (count,) + x.shape
    return pl.pallas_call(
        functools.partial(gather_kernel, axis, count),
        out_shape=jax.ShapeDtypeStruct(stacked, x.dtype),
        in_specs=[pl.BlockSpec(memory_space=pltpu.VMEM)],
        out_specs=pl.BlockSpec(memory_space=pltpu.VMEM),
        scratch_shapes=[
            pltpu.VMEM(stacked, x.dtype),
            pltpu.SemaphoreType.DMA((count,)),
            pltpu.SemaphoreType.DMA((count,)),
        ],
        compiler_params=pltpu.CompilerParams(collective_id=collective_id, has_side_effects=True),
    )(x)


def rms_scale(hidden, norm_gain):
    values = hidden.astype(jnp.float32)
    meansq = jnp.mean(values * values, axis=-1, keepdims=True)
    return (values * lax.rsqrt(meansq + 1e-06) * norm_gain).astype(jnp.bfloat16)


def route_slots(route_rows, capacity):
    flat_routes = route_rows.reshape(-1)
    onehot = (flat_routes[:, None] == jnp.arange(EXPERTS, dtype=jnp.int32)[None, :]).astype(
        jnp.int32
    )
    earlier = jnp.cumsum(onehot, axis=0) - onehot
    slot_rank = jnp.sum(earlier * onehot, axis=1)
    return flat_routes * capacity + slot_rank


def pack_rows(normed, route_rows, capacity, shards):
    flat_index = route_slots(route_rows, capacity)
    source = jnp.repeat(normed, TOP, axis=0)
    feature_width = normed.shape[1]
    packed = jnp.zeros((EXPERTS * capacity, feature_width), jnp.bfloat16).at[flat_index].set(source)
    packed = packed.reshape(EXPERTS, capacity, feature_width)
    return (jnp.repeat(packed, shards, axis=0), flat_index)


def expert_block(row_block, weights):
    gate_full, up_full, down_full = weights
    gate_pre = jnp.dot(row_block, gate_full, preferred_element_type=jnp.float32)
    up_pre = jnp.dot(row_block, up_full, preferred_element_type=jnp.float32)
    act = (jax.nn.gelu(gate_pre, approximate=True) * up_pre).astype(jnp.bfloat16)
    return jnp.dot(act, down_full, preferred_element_type=jnp.float32).astype(jnp.bfloat16)


def expert_apply(received, weights):
    peer_count, slot_count, feature_width = received.shape
    partial_value = expert_block(received.reshape(peer_count * slot_count, feature_width), weights)
    return partial_value.reshape(peer_count, slot_count, feature_width)


def unpack_rows(returned, flat_index, shards, residual, gate_rows):
    peer_count, slot_count, feature_width = returned.shape
    summed = returned.astype(jnp.float32).reshape(EXPERTS, shards, slot_count, feature_width)
    summed = jnp.sum(summed, axis=1).reshape(EXPERTS * slot_count, feature_width)
    picked = jnp.take(summed, flat_index, axis=0).reshape(-1, TOP, feature_width)
    combined = residual.astype(jnp.float32) + jnp.sum(gate_rows[..., None] * picked, axis=1)
    return combined.astype(jnp.bfloat16)


def body(
    queries,
    keys_new,
    values_new,
    key_cache,
    value_cache,
    buckets,
    lengths,
    bias_table,
    out_proj,
    decode_in,
    prefill_in,
    routes,
    gates,
    dec_routes,
    dec_gates,
    norm_gain,
    w_gate,
    w_up,
    w_down,
):
    seq_count = lax.axis_size("seq")
    seq_index = lax.axis_index("seq")
    tp_index = lax.axis_index("tp")
    shards = seq_count // EXPERTS
    weights = (
        lax.all_gather(w_gate, "tp", axis=0, tiled=True),
        lax.all_gather(w_up, "tp", axis=0, tiled=True),
        lax.all_gather(w_down, "tp", axis=1, tiled=True),
    )
    normed_pre = rms_scale(prefill_in, norm_gain)
    request_count, heads_width = queries.shape
    heads_here = heads_width // HD
    ctx_local = key_cache.shape[1]
    score_scale = 1.0 / math.sqrt(HD)
    query_rows = queries.reshape(request_count, heads_here, HD)
    key_rows = key_cache.reshape(request_count, ctx_local, heads_here, HD)
    value_rows = value_cache.reshape(request_count, ctx_local, heads_here, HD).astype(jnp.float32)
    bias_here = lax.dynamic_slice_in_dim(bias_table, tp_index * heads_here, heads_here, 1)
    bucket_hot = (
        buckets[..., None] == jnp.arange(bias_table.shape[0], dtype=jnp.int32)[None, None, :]
    ).astype(jnp.float32)
    bias_rows = jnp.einsum("rcn,nh->rhc", bucket_hot, bias_here, precision=lax.Precision.HIGHEST)
    cache_scores = (
        jnp.einsum("rhd,rchd->rhc", query_rows, key_rows, preferred_element_type=jnp.float32)
        * score_scale
        + bias_rows
    )
    positions = seq_index * ctx_local + jnp.arange(ctx_local, dtype=jnp.int32)
    valid_mask = (positions[None, :] < lengths[:, None])[:, None, :]
    cache_scores = jnp.where(valid_mask, cache_scores, -1e30)
    local_max = jnp.max(cache_scores, axis=-1)
    local_weights = jnp.where(valid_mask, jnp.exp(cache_scores - local_max[..., None]), 0.0)
    local_sum = jnp.sum(local_weights, axis=-1)
    local_acc = jnp.einsum(
        "rhc,rchd->rhd", local_weights, value_rows, precision=lax.Precision.HIGHEST
    )
    tp_count = lax.axis_size("tp")
    packed_parts = jnp.concatenate(
        [
            local_acc.reshape(request_count, heads_here * HD),
            jnp.pad(
                jnp.stack([local_max.reshape(-1), local_sum.reshape(-1)]),
                ((0, 2), (0, heads_here * HD - request_count * heads_here)),
            ),
        ],
        axis=0,
    )
    gathered = axis_gather(packed_parts, "seq", seq_count, 1)
    slot_max = gathered[:, request_count, : request_count * heads_here].reshape(
        seq_count, request_count, heads_here
    )
    slot_sum = gathered[:, request_count + 1, : request_count * heads_here].reshape(
        seq_count, request_count, heads_here
    )
    slot_acc = gathered[:, :request_count, :].reshape(seq_count, request_count, heads_here, HD)
    part_max = jnp.max(slot_max, axis=0)
    slot_scale = jnp.exp(slot_max - part_max[None])
    part_sum = jnp.sum(slot_sum * slot_scale, axis=0)
    part_acc = jnp.sum(slot_acc * slot_scale[..., None], axis=0)
    own_key = keys_new.reshape(request_count, heads_here, HD).astype(jnp.float32)
    own_value = values_new.reshape(request_count, heads_here, HD).astype(jnp.float32)
    own_score = (
        jnp.sum(query_rows.astype(jnp.float32) * own_key, axis=-1) * score_scale
        + bias_here[0][None, :]
    )
    row_peak = jnp.maximum(part_max, own_score)
    keep_scale = jnp.exp(part_max - row_peak)
    own_weight = jnp.exp(own_score - row_peak)
    weight_total = part_sum * keep_scale + own_weight
    weighted = part_acc * keep_scale[..., None] + own_weight[..., None] * own_value
    mixed_rows = (
        (weighted / weight_total[..., None])
        .astype(jnp.bfloat16)
        .reshape(request_count, heads_width)
    )
    head_terms = jnp.dot(mixed_rows, out_proj, preferred_element_type=jnp.float32)
    attended = jnp.sum(axis_gather(head_terms, "tp", tp_count, 2), axis=0)
    decode_hidden = (decode_in.astype(jnp.float32) + attended).astype(jnp.bfloat16)
    normed_dec = rms_scale(decode_hidden, norm_gain)
    dec_parts = axis_gather(expert_block(normed_dec, weights), "seq", seq_count, 3)
    slot_expert = jnp.arange(seq_count, dtype=jnp.int32) // shards
    slot_gate = jnp.sum(
        jnp.where(dec_routes[:, :, None] == slot_expert[None, None, :], dec_gates[:, :, None], 0.0),
        axis=1,
    )
    dec_terms = jnp.sum(
        slot_gate.T[:, :, None] * dec_parts.astype(jnp.float32), axis=0
    )
    decode_out = (decode_hidden.astype(jnp.float32) + dec_terms).astype(jnp.bfloat16)
    send_all, index_all = pack_rows(normed_pre, routes, CAP, shards)
    back_all = lax.all_to_all(
        expert_apply(
            lax.all_to_all(send_all, "seq", split_axis=0, concat_axis=0, tiled=True), weights
        ),
        "seq",
        split_axis=0,
        concat_axis=0,
        tiled=True,
    )
    prefill_out = unpack_rows(back_all, index_all, shards, prefill_in, gates)
    return (decode_out, prefill_out)


def solution(mesh):
    placed = (
        P(None, "tp"),
        P(None, "tp"),
        P(None, "tp"),
        P(None, "seq", "tp"),
        P(None, "seq", "tp"),
        P(None, "seq"),
        P(),
        P(),
        P("tp", None),
        P(),
        P(("seq", "tp"), None),
        P(("seq", "tp"), None),
        P(("seq", "tp"), None),
        P(),
        P(),
        P(),
        P("tp", "seq"),
        P("tp", "seq"),
        P("seq", "tp"),
    )
    return jax.shard_map(
        body, mesh=mesh, in_specs=placed, out_specs=(P(), P(("seq", "tp"), None)), check_vma=False
    )
```

```python
import functools
import math

import jax
import jax.numpy as jnp
from jax import lax
from jax.experimental import pallas as pl
from jax.experimental.pallas import tpu as pltpu
from jax.sharding import PartitionSpec as P

HD = 64
EXPERTS = 16
TOP = 2
CAP = 10


def peer_device(axis, peer):
    if axis == "seq":
        return (peer, lax.axis_index("tp"))
    return (lax.axis_index("seq"), peer)


def gather_kernel(axis, count, stride, x_ref, out_ref, landed, send_sem, recv_sem):
    index = lax.axis_index(axis)
    me = lax.rem(index // stride, count)
    base = index - me * stride

    def peer_of(step):
        return peer_device(axis, base + lax.rem(me + step, count) * stride)

    barrier = pltpu.get_barrier_semaphore()

    def greet(step, carry):
        pl.semaphore_signal(
            barrier, inc=1, device_id=peer_of(step), device_id_type=pl.DeviceIdType.MESH
        )
        return carry

    lax.fori_loop(1, count, greet, 0)
    pl.semaphore_wait(barrier, count - 1)

    def transfer(step):
        return pltpu.make_async_remote_copy(
            src_ref=x_ref,
            dst_ref=landed.at[me],
            send_sem=send_sem.at[step],
            recv_sem=recv_sem.at[step],
            device_id=peer_of(step),
            device_id_type=pl.DeviceIdType.MESH,
        )

    def launch(step, carry):
        transfer(step).start()
        return carry

    lax.fori_loop(1, count, launch, 0)
    landed[me] = x_ref[...]

    def finish(step, carry):
        transfer(step).wait()
        return carry

    lax.fori_loop(1, count, finish, 0)
    out_ref[...] = landed[...]


def axis_gather(x, axis, count, stride, collective_id):
    stacked = (count,) + x.shape
    return pl.pallas_call(
        functools.partial(gather_kernel, axis, count, stride),
        out_shape=jax.ShapeDtypeStruct(stacked, x.dtype),
        in_specs=[pl.BlockSpec(memory_space=pltpu.VMEM)],
        out_specs=pl.BlockSpec(memory_space=pltpu.VMEM),
        scratch_shapes=[
            pltpu.VMEM(stacked, x.dtype),
            pltpu.SemaphoreType.DMA((count,)),
            pltpu.SemaphoreType.DMA((count,)),
        ],
        compiler_params=pltpu.CompilerParams(collective_id=collective_id, has_side_effects=True),
    )(x)


def merge_softmax(stacked, rows, width):
    slot_max = stacked[:, rows, :width]
    slot_sum = stacked[:, rows + 1, :width]
    joint_max = jnp.max(slot_max, axis=0)
    slot_scale = jnp.exp(slot_max - joint_max[None])
    joint_sum = jnp.sum(slot_sum * slot_scale, axis=0)
    lane_scale = jnp.repeat(slot_scale.reshape(slot_scale.shape[0], rows, -1), HD, axis=2)
    joint_acc = jnp.sum(stacked[:, :rows, :] * lane_scale, axis=0)
    return joint_max, joint_sum, joint_acc


def pack_softmax(joint_max, joint_sum, joint_acc):
    rows, lanes = joint_acc.shape
    stats = jnp.stack([joint_max, joint_sum])
    return jnp.concatenate([joint_acc, jnp.pad(stats, ((0, 2), (0, lanes - stats.shape[1])))], axis=0)


def rms_scale(hidden, norm_gain):
    values = hidden.astype(jnp.float32)
    meansq = jnp.mean(values * values, axis=-1, keepdims=True)
    return (values * lax.rsqrt(meansq + 1e-06) * norm_gain).astype(jnp.bfloat16)


def route_slots(route_rows, capacity):
    flat_routes = route_rows.reshape(-1)
    onehot = (flat_routes[:, None] == jnp.arange(EXPERTS, dtype=jnp.int32)[None, :]).astype(
        jnp.int32
    )
    earlier = jnp.cumsum(onehot, axis=0) - onehot
    slot_rank = jnp.sum(earlier * onehot, axis=1)
    return flat_routes * capacity + slot_rank


def pack_rows(normed, route_rows, capacity, shards):
    flat_index = route_slots(route_rows, capacity)
    source = jnp.repeat(normed, TOP, axis=0)
    feature_width = normed.shape[1]
    packed = jnp.zeros((EXPERTS * capacity, feature_width), jnp.bfloat16).at[flat_index].set(source)
    packed = packed.reshape(EXPERTS, capacity, feature_width)
    return (jnp.repeat(packed, shards, axis=0), flat_index)


def expert_block(row_block, weights):
    gate_full, up_full, down_full = weights
    gate_pre = jnp.dot(row_block, gate_full, preferred_element_type=jnp.float32)
    up_pre = jnp.dot(row_block, up_full, preferred_element_type=jnp.float32)
    act = (jax.nn.gelu(gate_pre, approximate=True) * up_pre).astype(jnp.bfloat16)
    return jnp.dot(act, down_full, preferred_element_type=jnp.float32).astype(jnp.bfloat16)


def expert_apply(received, weights):
    peer_count, slot_count, feature_width = received.shape
    partial_value = expert_block(received.reshape(peer_count * slot_count, feature_width), weights)
    return partial_value.reshape(peer_count, slot_count, feature_width)


def unpack_rows(returned, flat_index, shards, residual, gate_rows):
    peer_count, slot_count, feature_width = returned.shape
    summed = returned.astype(jnp.float32).reshape(EXPERTS, shards, slot_count, feature_width)
    summed = jnp.sum(summed, axis=1).reshape(EXPERTS * slot_count, feature_width)
    picked = jnp.take(summed, flat_index, axis=0).reshape(-1, TOP, feature_width)
    combined = residual.astype(jnp.float32) + jnp.sum(gate_rows[..., None] * picked, axis=1)
    return combined.astype(jnp.bfloat16)


def body(
    queries,
    keys_new,
    values_new,
    key_cache,
    value_cache,
    buckets,
    lengths,
    bias_table,
    out_proj,
    decode_in,
    prefill_in,
    routes,
    gates,
    dec_routes,
    dec_gates,
    norm_gain,
    w_gate,
    w_up,
    w_down,
):
    seq_count = lax.axis_size("seq")
    seq_index = lax.axis_index("seq")
    tp_index = lax.axis_index("tp")
    shards = seq_count // EXPERTS
    weights = (
        lax.all_gather(w_gate, "tp", axis=0, tiled=True),
        lax.all_gather(w_up, "tp", axis=0, tiled=True),
        lax.all_gather(w_down, "tp", axis=1, tiled=True),
    )
    normed_pre = rms_scale(prefill_in, norm_gain)
    request_count, heads_width = queries.shape
    heads_here = heads_width // HD
    ctx_local = key_cache.shape[1]
    score_scale = 1.0 / math.sqrt(HD)
    query_rows = queries.reshape(request_count, heads_here, HD)
    key_rows = key_cache.reshape(request_count, ctx_local, heads_here, HD)
    value_rows = value_cache.reshape(request_count, ctx_local, heads_here, HD).astype(jnp.float32)
    bias_here = lax.dynamic_slice_in_dim(bias_table, tp_index * heads_here, heads_here, 1)
    bucket_hot = (
        buckets[..., None] == jnp.arange(bias_table.shape[0], dtype=jnp.int32)[None, None, :]
    ).astype(jnp.float32)
    bias_rows = jnp.einsum("rcn,nh->rhc", bucket_hot, bias_here, precision=lax.Precision.HIGHEST)
    cache_scores = (
        jnp.einsum("rhd,rchd->rhc", query_rows, key_rows, preferred_element_type=jnp.float32)
        * score_scale
        + bias_rows
    )
    positions = seq_index * ctx_local + jnp.arange(ctx_local, dtype=jnp.int32)
    valid_mask = (positions[None, :] < lengths[:, None])[:, None, :]
    cache_scores = jnp.where(valid_mask, cache_scores, -1e30)
    local_max = jnp.max(cache_scores, axis=-1)
    local_weights = jnp.where(valid_mask, jnp.exp(cache_scores - local_max[..., None]), 0.0)
    local_sum = jnp.sum(local_weights, axis=-1)
    local_acc = jnp.einsum(
        "rhc,rchd->rhd", local_weights, value_rows, precision=lax.Precision.HIGHEST
    )
    tp_count = lax.axis_size("tp")
    z_count = 16 if seq_count % 16 == 0 else seq_count
    x_count = seq_count // z_count
    flat_width = request_count * heads_here
    packed_parts = pack_softmax(
        local_max.reshape(-1), local_sum.reshape(-1), local_acc.reshape(request_count, heads_here * HD)
    )
    stage = merge_softmax(axis_gather(packed_parts, "seq", z_count, 1, 1), request_count, flat_width)
    stage = merge_softmax(
        axis_gather(pack_softmax(*stage), "seq", x_count, z_count, 2), request_count, flat_width
    )
    part_max = stage[0].reshape(request_count, heads_here)
    part_sum = stage[1].reshape(request_count, heads_here)
    part_acc = stage[2].reshape(request_count, heads_here, HD)
    own_key = keys_new.reshape(request_count, heads_here, HD).astype(jnp.float32)
    own_value = values_new.reshape(request_count, heads_here, HD).astype(jnp.float32)
    own_score = (
        jnp.sum(query_rows.astype(jnp.float32) * own_key, axis=-1) * score_scale
        + bias_here[0][None, :]
    )
    row_peak = jnp.maximum(part_max, own_score)
    keep_scale = jnp.exp(part_max - row_peak)
    own_weight = jnp.exp(own_score - row_peak)
    weight_total = part_sum * keep_scale + own_weight
    weighted = part_acc * keep_scale[..., None] + own_weight[..., None] * own_value
    mixed_rows = (
        (weighted / weight_total[..., None])
        .astype(jnp.bfloat16)
        .reshape(request_count, heads_width)
    )
    head_terms = jnp.dot(mixed_rows, out_proj, preferred_element_type=jnp.float32)
    attended = jnp.sum(axis_gather(head_terms, "tp", tp_count, 1, 3), axis=0)
    send_all, index_all = pack_rows(normed_pre, routes, CAP, shards)
    received = lax.all_to_all(send_all, "seq", split_axis=0, concat_axis=0, tiled=True)
    received, attended = lax.optimization_barrier((received, attended))
    decode_hidden = (decode_in.astype(jnp.float32) + attended).astype(jnp.bfloat16)
    normed_dec = rms_scale(decode_hidden, norm_gain)
    expert_rows = expert_apply(received, weights)
    expert_rows, normed_dec = lax.optimization_barrier((expert_rows, normed_dec))
    back_all = lax.all_to_all(expert_rows, "seq", split_axis=0, concat_axis=0, tiled=True)
    dec_parts = axis_gather(expert_block(normed_dec, weights), "seq", z_count, 1, 4)
    z_base = (seq_index // z_count) * z_count
    slot_expert = (z_base + jnp.arange(z_count, dtype=jnp.int32)) // shards
    slot_gate = jnp.sum(
        jnp.where(dec_routes[:, :, None] == slot_expert[None, None, :], dec_gates[:, :, None], 0.0),
        axis=1,
    )
    z_terms = jnp.sum(slot_gate.T[:, :, None] * dec_parts.astype(jnp.float32), axis=0)
    dec_terms = jnp.sum(axis_gather(z_terms, "seq", x_count, z_count, 5), axis=0)
    decode_out = (decode_hidden.astype(jnp.float32) + dec_terms).astype(jnp.bfloat16)
    prefill_out = unpack_rows(back_all, index_all, shards, prefill_in, gates)
    return (decode_out, prefill_out)


def solution(mesh):
    placed = (
        P(None, "tp"),
        P(None, "tp"),
        P(None, "tp"),
        P(None, "seq", "tp"),
        P(None, "seq", "tp"),
        P(None, "seq"),
        P(),
        P(),
        P("tp", None),
        P(),
        P(("seq", "tp"), None),
        P(("seq", "tp"), None),
        P(("seq", "tp"), None),
        P(),
        P(),
        P(),
        P("tp", "seq"),
        P("tp", "seq"),
        P("seq", "tp"),
    )
    return jax.shard_map(
        body, mesh=mesh, in_specs=placed, out_specs=(P(), P(("seq", "tp"), None)), check_vma=False
    )
```

```python
import functools
import math

import jax
import jax.numpy as jnp
from jax import lax
from jax.experimental import pallas as pl
from jax.experimental.pallas import tpu as pltpu
from jax.sharding import PartitionSpec as P

HD = 64
EXPERTS = 16
TOP = 2
CAP = 10


def peer_device(axis, peer):
    if axis == "seq":
        return (peer, lax.axis_index("tp"))
    return (lax.axis_index("seq"), peer)


def gather_kernel(axis, count, stride, x_ref, out_ref, landed, send_sem, recv_sem):
    index = lax.axis_index(axis)
    me = lax.rem(index // stride, count)
    base = index - me * stride

    def peer_of(step):
        return peer_device(axis, base + lax.rem(me + step, count) * stride)

    barrier = pltpu.get_barrier_semaphore()

    def greet(step, carry):
        pl.semaphore_signal(
            barrier, inc=1, device_id=peer_of(step), device_id_type=pl.DeviceIdType.MESH
        )
        return carry

    lax.fori_loop(1, count, greet, 0)
    pl.semaphore_wait(barrier, count - 1)

    def transfer(step):
        return pltpu.make_async_remote_copy(
            src_ref=x_ref,
            dst_ref=landed.at[me],
            send_sem=send_sem.at[step],
            recv_sem=recv_sem.at[step],
            device_id=peer_of(step),
            device_id_type=pl.DeviceIdType.MESH,
        )

    def launch(step, carry):
        transfer(step).start()
        return carry

    lax.fori_loop(1, count, launch, 0)
    landed[me] = x_ref[...]

    def finish(step, carry):
        transfer(step).wait()
        return carry

    lax.fori_loop(1, count, finish, 0)
    out_ref[...] = landed[...]


def axis_gather(x, axis, count, stride, collective_id):
    stacked = (count,) + x.shape
    return pl.pallas_call(
        functools.partial(gather_kernel, axis, count, stride),
        out_shape=jax.ShapeDtypeStruct(stacked, x.dtype),
        in_specs=[pl.BlockSpec(memory_space=pltpu.VMEM)],
        out_specs=pl.BlockSpec(memory_space=pltpu.VMEM),
        scratch_shapes=[
            pltpu.VMEM(stacked, x.dtype),
            pltpu.SemaphoreType.DMA((count,)),
            pltpu.SemaphoreType.DMA((count,)),
        ],
        compiler_params=pltpu.CompilerParams(collective_id=collective_id, has_side_effects=True),
    )(x)


def exchange_kernel(axis, count, stride, x_ref, out_ref, landed, send_sem, recv_sem):
    index = lax.axis_index(axis)
    me = lax.rem(index // stride, count)
    base = index - me * stride

    def member(slot):
        return peer_device(axis, base + slot * stride)

    barrier = pltpu.get_barrier_semaphore()

    def greet(step, carry):
        pl.semaphore_signal(
            barrier,
            inc=1,
            device_id=member(lax.rem(me + step, count)),
            device_id_type=pl.DeviceIdType.MESH,
        )
        return carry

    lax.fori_loop(1, count, greet, 0)
    pl.semaphore_wait(barrier, count - 1)

    def outgoing(step):
        target = lax.rem(me + step, count)
        return pltpu.make_async_remote_copy(
            src_ref=x_ref.at[target],
            dst_ref=landed.at[me],
            send_sem=send_sem.at[step],
            recv_sem=recv_sem.at[step],
            device_id=member(target),
            device_id_type=pl.DeviceIdType.MESH,
        )

    def incoming(step):
        source = lax.rem(me - step + count, count)
        return pltpu.make_async_remote_copy(
            src_ref=x_ref.at[source],
            dst_ref=landed.at[source],
            send_sem=send_sem.at[step],
            recv_sem=recv_sem.at[step],
            device_id=member(source),
            device_id_type=pl.DeviceIdType.MESH,
        )

    def launch(step, carry):
        outgoing(step).start()
        return carry

    lax.fori_loop(1, count, launch, 0)
    landed[me] = x_ref[me]

    def finish(step, carry):
        outgoing(step).wait_send()
        incoming(step).wait_recv()
        return carry

    lax.fori_loop(1, count, finish, 0)
    out_ref[...] = landed[...]


def axis_exchange(x, axis, count, stride, collective_id):
    return pl.pallas_call(
        functools.partial(exchange_kernel, axis, count, stride),
        out_shape=jax.ShapeDtypeStruct(x.shape, x.dtype),
        in_specs=[pl.BlockSpec(memory_space=pltpu.VMEM)],
        out_specs=pl.BlockSpec(memory_space=pltpu.VMEM),
        scratch_shapes=[
            pltpu.VMEM(x.shape, x.dtype),
            pltpu.SemaphoreType.DMA((count,)),
            pltpu.SemaphoreType.DMA((count,)),
        ],
        compiler_params=pltpu.CompilerParams(collective_id=collective_id, has_side_effects=True),
    )(x)


def merge_softmax(stacked, rows, width):
    slot_max = stacked[:, rows, :width]
    slot_sum = stacked[:, rows + 1, :width]
    joint_max = jnp.max(slot_max, axis=0)
    slot_scale = jnp.exp(slot_max - joint_max[None])
    joint_sum = jnp.sum(slot_sum * slot_scale, axis=0)
    lane_scale = jnp.repeat(slot_scale.reshape(slot_scale.shape[0], rows, -1), HD, axis=2)
    joint_acc = jnp.sum(stacked[:, :rows, :] * lane_scale, axis=0)
    return joint_max, joint_sum, joint_acc


def pack_softmax(joint_max, joint_sum, joint_acc):
    rows, lanes = joint_acc.shape
    stats = jnp.stack([joint_max, joint_sum])
    return jnp.concatenate([joint_acc, jnp.pad(stats, ((0, 2), (0, lanes - stats.shape[1])))], axis=0)


def rms_scale(hidden, norm_gain):
    values = hidden.astype(jnp.float32)
    meansq = jnp.mean(values * values, axis=-1, keepdims=True)
    return (values * lax.rsqrt(meansq + 1e-06) * norm_gain).astype(jnp.bfloat16)


def route_slots(route_rows, capacity):
    flat_routes = route_rows.reshape(-1)
    onehot = (flat_routes[:, None] == jnp.arange(EXPERTS, dtype=jnp.int32)[None, :]).astype(
        jnp.int32
    )
    earlier = jnp.cumsum(onehot, axis=0) - onehot
    slot_rank = jnp.sum(earlier * onehot, axis=1)
    return flat_routes * capacity + slot_rank


def pack_rows(normed, route_rows, capacity, shards):
    flat_index = route_slots(route_rows, capacity)
    source = jnp.repeat(normed, TOP, axis=0)
    feature_width = normed.shape[1]
    packed = jnp.zeros((EXPERTS * capacity, feature_width), jnp.bfloat16).at[flat_index].set(source)
    packed = packed.reshape(EXPERTS, capacity, feature_width)
    return (jnp.repeat(packed, shards, axis=0), flat_index)


def expert_block(row_block, weights):
    gate_full, up_full, down_full = weights
    gate_pre = jnp.dot(row_block, gate_full, preferred_element_type=jnp.float32)
    up_pre = jnp.dot(row_block, up_full, preferred_element_type=jnp.float32)
    act = (jax.nn.gelu(gate_pre, approximate=True) * up_pre).astype(jnp.bfloat16)
    return jnp.dot(act, down_full, preferred_element_type=jnp.float32).astype(jnp.bfloat16)


def expert_apply(received, weights):
    peer_count, slot_count, feature_width = received.shape
    partial_value = expert_block(received.reshape(peer_count * slot_count, feature_width), weights)
    return partial_value.reshape(peer_count, slot_count, feature_width)


def unpack_rows(returned, flat_index, shards, residual, gate_rows):
    peer_count, slot_count, feature_width = returned.shape
    summed = returned.astype(jnp.float32).reshape(EXPERTS, shards, slot_count, feature_width)
    summed = jnp.sum(summed, axis=1).reshape(EXPERTS * slot_count, feature_width)
    picked = jnp.take(summed, flat_index, axis=0).reshape(-1, TOP, feature_width)
    combined = residual.astype(jnp.float32) + jnp.sum(gate_rows[..., None] * picked, axis=1)
    return combined.astype(jnp.bfloat16)


def body(
    queries,
    keys_new,
    values_new,
    key_cache,
    value_cache,
    buckets,
    lengths,
    bias_table,
    out_proj,
    decode_in,
    prefill_in,
    routes,
    gates,
    dec_routes,
    dec_gates,
    norm_gain,
    w_gate,
    w_up,
    w_down,
):
    seq_count = lax.axis_size("seq")
    seq_index = lax.axis_index("seq")
    tp_index = lax.axis_index("tp")
    shards = seq_count // EXPERTS
    weights = (
        lax.all_gather(w_gate, "tp", axis=0, tiled=True),
        lax.all_gather(w_up, "tp", axis=0, tiled=True),
        lax.all_gather(w_down, "tp", axis=1, tiled=True),
    )
    normed_pre = rms_scale(prefill_in, norm_gain)
    request_count, heads_width = queries.shape
    heads_here = heads_width // HD
    ctx_local = key_cache.shape[1]
    score_scale = 1.0 / math.sqrt(HD)
    query_rows = queries.reshape(request_count, heads_here, HD)
    key_rows = key_cache.reshape(request_count, ctx_local, heads_here, HD)
    value_rows = value_cache.reshape(request_count, ctx_local, heads_here, HD).astype(jnp.float32)
    bias_here = lax.dynamic_slice_in_dim(bias_table, tp_index * heads_here, heads_here, 1)
    bucket_hot = (
        buckets[..., None] == jnp.arange(bias_table.shape[0], dtype=jnp.int32)[None, None, :]
    ).astype(jnp.float32)
    bias_rows = jnp.einsum("rcn,nh->rhc", bucket_hot, bias_here, precision=lax.Precision.HIGHEST)
    cache_scores = (
        jnp.einsum("rhd,rchd->rhc", query_rows, key_rows, preferred_element_type=jnp.float32)
        * score_scale
        + bias_rows
    )
    positions = seq_index * ctx_local + jnp.arange(ctx_local, dtype=jnp.int32)
    valid_mask = (positions[None, :] < lengths[:, None])[:, None, :]
    cache_scores = jnp.where(valid_mask, cache_scores, -1e30)
    local_max = jnp.max(cache_scores, axis=-1)
    local_weights = jnp.where(valid_mask, jnp.exp(cache_scores - local_max[..., None]), 0.0)
    local_sum = jnp.sum(local_weights, axis=-1)
    local_acc = jnp.einsum(
        "rhc,rchd->rhd", local_weights, value_rows, precision=lax.Precision.HIGHEST
    )
    tp_count = lax.axis_size("tp")
    z_count = 16 if seq_count % 16 == 0 else seq_count
    x_count = seq_count // z_count
    flat_width = request_count * heads_here
    packed_parts = pack_softmax(
        local_max.reshape(-1), local_sum.reshape(-1), local_acc.reshape(request_count, heads_here * HD)
    )
    stage = merge_softmax(axis_gather(packed_parts, "seq", z_count, 1, 1), request_count, flat_width)
    stage = merge_softmax(
        axis_gather(pack_softmax(*stage), "seq", x_count, z_count, 2), request_count, flat_width
    )
    part_max = stage[0].reshape(request_count, heads_here)
    part_sum = stage[1].reshape(request_count, heads_here)
    part_acc = stage[2].reshape(request_count, heads_here, HD)
    own_key = keys_new.reshape(request_count, heads_here, HD).astype(jnp.float32)
    own_value = values_new.reshape(request_count, heads_here, HD).astype(jnp.float32)
    own_score = (
        jnp.sum(query_rows.astype(jnp.float32) * own_key, axis=-1) * score_scale
        + bias_here[0][None, :]
    )
    row_peak = jnp.maximum(part_max, own_score)
    keep_scale = jnp.exp(part_max - row_peak)
    own_weight = jnp.exp(own_score - row_peak)
    weight_total = part_sum * keep_scale + own_weight
    weighted = part_acc * keep_scale[..., None] + own_weight[..., None] * own_value
    mixed_rows = (
        (weighted / weight_total[..., None])
        .astype(jnp.bfloat16)
        .reshape(request_count, heads_width)
    )
    head_terms = jnp.dot(mixed_rows, out_proj, preferred_element_type=jnp.float32)
    attended = jnp.sum(axis_gather(head_terms, "tp", tp_count, 1, 3), axis=0)
    flat_index = route_slots(routes, CAP)
    slabs = (
        jnp.zeros((EXPERTS * CAP, normed_pre.shape[1]), jnp.bfloat16)
        .at[flat_index]
        .set(jnp.repeat(normed_pre, TOP, axis=0))
        .reshape(EXPERTS, CAP, normed_pre.shape[1])
    )
    group_count = seq_count // shards
    arrived = axis_exchange(slabs, "seq", group_count, shards, 6)
    arrived, attended = lax.optimization_barrier((arrived, attended))
    decode_hidden = (decode_in.astype(jnp.float32) + attended).astype(jnp.bfloat16)
    normed_dec = rms_scale(decode_hidden, norm_gain)
    block_rows = axis_gather(arrived, "seq", shards, 1, 7)
    block_out = expert_block(block_rows.reshape(-1, block_rows.shape[-1]), weights)
    block_out, normed_dec = lax.optimization_barrier((block_out, normed_dec))
    part_rows = axis_exchange(block_out.reshape(block_rows.shape), "seq", shards, 1, 8)
    summed = jnp.zeros(part_rows.shape[1:], jnp.float32)
    for part in range(shards):
        summed = summed + part_rows[part].astype(jnp.float32)
    returned = axis_exchange(summed, "seq", group_count, shards, 9)
    dec_parts = axis_gather(expert_block(normed_dec, weights), "seq", z_count, 1, 4)
    z_base = (seq_index // z_count) * z_count
    slot_expert = (z_base + jnp.arange(z_count, dtype=jnp.int32)) // shards
    slot_gate = jnp.sum(
        jnp.where(dec_routes[:, :, None] == slot_expert[None, None, :], dec_gates[:, :, None], 0.0),
        axis=1,
    )
    z_terms = jnp.sum(slot_gate.T[:, :, None] * dec_parts.astype(jnp.float32), axis=0)
    dec_terms = jnp.sum(axis_gather(z_terms, "seq", x_count, z_count, 5), axis=0)
    decode_out = (decode_hidden.astype(jnp.float32) + dec_terms).astype(jnp.bfloat16)
    picked = jnp.take(returned.reshape(EXPERTS * CAP, -1), flat_index, axis=0)
    picked = picked.reshape(-1, TOP, picked.shape[-1])
    prefill_out = (
        prefill_in.astype(jnp.float32) + jnp.sum(gates[..., None] * picked, axis=1)
    ).astype(jnp.bfloat16)
    return (decode_out, prefill_out)


def solution(mesh):
    placed = (
        P(None, "tp"),
        P(None, "tp"),
        P(None, "tp"),
        P(None, "seq", "tp"),
        P(None, "seq", "tp"),
        P(None, "seq"),
        P(),
        P(),
        P("tp", None),
        P(),
        P(("seq", "tp"), None),
        P(("seq", "tp"), None),
        P(("seq", "tp"), None),
        P(),
        P(),
        P(),
        P("tp", "seq"),
        P("tp", "seq"),
        P("seq", "tp"),
    )
    return jax.shard_map(
        body, mesh=mesh, in_specs=placed, out_specs=(P(), P(("seq", "tp"), None)), check_vma=False
    )
```

```python
import functools
import math

import jax
import jax.numpy as jnp
from jax import lax
from jax.experimental import pallas as pl
from jax.experimental.pallas import tpu as pltpu
from jax.sharding import PartitionSpec as P

HD = 64
EXPERTS = 16
TOP = 2
CAP = 10


def peer_device(axis, peer):
    if axis == "seq":
        return (peer, lax.axis_index("tp"))
    return (lax.axis_index("seq"), peer)


def share_kernel(axis, count, stride, modes, *refs):
    width = len(modes)
    sources = refs[:width]
    outputs = refs[width : 2 * width]
    landed = refs[2 * width : 3 * width]
    send_sems = refs[3 * width : 4 * width]
    recv_sems = refs[4 * width :]
    index = lax.axis_index(axis)
    me = lax.rem(index // stride, count)
    base = index - me * stride

    def member(slot):
        return peer_device(axis, base + slot * stride)

    def piece(which, slot):
        return sources[which].at[slot] if modes[which] else sources[which]

    barrier = pltpu.get_barrier_semaphore()

    def greet(step, carry):
        pl.semaphore_signal(
            barrier,
            inc=1,
            device_id=member(lax.rem(me + step, count)),
            device_id_type=pl.DeviceIdType.MESH,
        )
        return carry

    lax.fori_loop(1, count, greet, 0)
    pl.semaphore_wait(barrier, count - 1)

    def outgoing(which, step):
        target = lax.rem(me + step, count)
        return pltpu.make_async_remote_copy(
            src_ref=piece(which, target),
            dst_ref=landed[which].at[me],
            send_sem=send_sems[which].at[step],
            recv_sem=recv_sems[which].at[step],
            device_id=member(target),
            device_id_type=pl.DeviceIdType.MESH,
        )

    def incoming(which, step):
        source = lax.rem(me - step + count, count)
        return pltpu.make_async_remote_copy(
            src_ref=piece(which, source),
            dst_ref=landed[which].at[source],
            send_sem=send_sems[which].at[step],
            recv_sem=recv_sems[which].at[step],
            device_id=member(source),
            device_id_type=pl.DeviceIdType.MESH,
        )

    def launch(step, carry):
        for which in range(width):
            outgoing(which, step).start()
        return carry

    lax.fori_loop(1, count, launch, 0)
    for which in range(width):
        landed[which][me] = piece(which, me)[...]

    def finish(step, carry):
        for which in range(width):
            outgoing(which, step).wait_send()
            incoming(which, step).wait_recv()
        return carry

    lax.fori_loop(1, count, finish, 0)
    for which in range(width):
        outputs[which][...] = landed[which][...]


def axis_share(payloads, modes, axis, count, stride, collective_id):
    shapes = [x.shape if mode else (count,) + x.shape for x, mode in zip(payloads, modes)]
    width = len(payloads)
    return pl.pallas_call(
        functools.partial(share_kernel, axis, count, stride, tuple(modes)),
        out_shape=[jax.ShapeDtypeStruct(s, x.dtype) for s, x in zip(shapes, payloads)],
        in_specs=[pl.BlockSpec(memory_space=pltpu.VMEM)] * width,
        out_specs=[pl.BlockSpec(memory_space=pltpu.VMEM)] * width,
        scratch_shapes=[pltpu.VMEM(s, x.dtype) for s, x in zip(shapes, payloads)]
        + [pltpu.SemaphoreType.DMA((count,))] * (2 * width),
        compiler_params=pltpu.CompilerParams(collective_id=collective_id, has_side_effects=True),
    )(*payloads)


def merge_softmax(stacked, rows, width):
    slot_max = stacked[:, rows, :width]
    slot_sum = stacked[:, rows + 1, :width]
    joint_max = jnp.max(slot_max, axis=0)
    slot_scale = jnp.exp(slot_max - joint_max[None])
    joint_sum = jnp.sum(slot_sum * slot_scale, axis=0)
    lane_scale = jnp.repeat(slot_scale.reshape(slot_scale.shape[0], rows, -1), HD, axis=2)
    joint_acc = jnp.sum(stacked[:, :rows, :] * lane_scale, axis=0)
    return joint_max, joint_sum, joint_acc


def pack_softmax(joint_max, joint_sum, joint_acc):
    rows, lanes = joint_acc.shape
    stats = jnp.stack([joint_max, joint_sum])
    return jnp.concatenate([joint_acc, jnp.pad(stats, ((0, 2), (0, lanes - stats.shape[1])))], axis=0)


def rms_scale(hidden, norm_gain):
    values = hidden.astype(jnp.float32)
    meansq = jnp.mean(values * values, axis=-1, keepdims=True)
    return (values * lax.rsqrt(meansq + 1e-06) * norm_gain).astype(jnp.bfloat16)


def route_slots(route_rows, capacity):
    flat_routes = route_rows.reshape(-1)
    onehot = (flat_routes[:, None] == jnp.arange(EXPERTS, dtype=jnp.int32)[None, :]).astype(
        jnp.int32
    )
    earlier = jnp.cumsum(onehot, axis=0) - onehot
    slot_rank = jnp.sum(earlier * onehot, axis=1)
    return flat_routes * capacity + slot_rank


def expert_block(row_block, weights):
    gate_full, up_full, down_full = weights
    gate_pre = jnp.dot(row_block, gate_full, preferred_element_type=jnp.float32)
    up_pre = jnp.dot(row_block, up_full, preferred_element_type=jnp.float32)
    act = (jax.nn.gelu(gate_pre, approximate=True) * up_pre).astype(jnp.bfloat16)
    return jnp.dot(act, down_full, preferred_element_type=jnp.float32).astype(jnp.bfloat16)


def body(
    queries,
    keys_new,
    values_new,
    key_cache,
    value_cache,
    buckets,
    lengths,
    bias_table,
    out_proj,
    decode_in,
    prefill_in,
    routes,
    gates,
    dec_routes,
    dec_gates,
    norm_gain,
    w_gate,
    w_up,
    w_down,
):
    seq_count = lax.axis_size("seq")
    seq_index = lax.axis_index("seq")
    tp_index = lax.axis_index("tp")
    shards = seq_count // EXPERTS
    weights = (
        lax.all_gather(w_gate, "tp", axis=0, tiled=True),
        lax.all_gather(w_up, "tp", axis=0, tiled=True),
        lax.all_gather(w_down, "tp", axis=1, tiled=True),
    )
    normed_pre = rms_scale(prefill_in, norm_gain)
    request_count, heads_width = queries.shape
    heads_here = heads_width // HD
    ctx_local = key_cache.shape[1]
    score_scale = 1.0 / math.sqrt(HD)
    query_rows = queries.reshape(request_count, heads_here, HD)
    key_rows = key_cache.reshape(request_count, ctx_local, heads_here, HD)
    value_rows = value_cache.reshape(request_count, ctx_local, heads_here, HD).astype(jnp.float32)
    bias_here = lax.dynamic_slice_in_dim(bias_table, tp_index * heads_here, heads_here, 1)
    bucket_hot = (
        buckets[..., None] == jnp.arange(bias_table.shape[0], dtype=jnp.int32)[None, None, :]
    ).astype(jnp.float32)
    bias_rows = jnp.einsum("rcn,nh->rhc", bucket_hot, bias_here, precision=lax.Precision.HIGHEST)
    cache_scores = (
        jnp.einsum("rhd,rchd->rhc", query_rows, key_rows, preferred_element_type=jnp.float32)
        * score_scale
        + bias_rows
    )
    positions = seq_index * ctx_local + jnp.arange(ctx_local, dtype=jnp.int32)
    valid_mask = (positions[None, :] < lengths[:, None])[:, None, :]
    cache_scores = jnp.where(valid_mask, cache_scores, -1e30)
    local_max = jnp.max(cache_scores, axis=-1)
    local_weights = jnp.where(valid_mask, jnp.exp(cache_scores - local_max[..., None]), 0.0)
    local_sum = jnp.sum(local_weights, axis=-1)
    local_acc = jnp.einsum(
        "rhc,rchd->rhd", local_weights, value_rows, precision=lax.Precision.HIGHEST
    )
    tp_count = lax.axis_size("tp")
    flat_width = request_count * heads_here
    packed_parts = pack_softmax(
        local_max.reshape(-1), local_sum.reshape(-1), local_acc.reshape(request_count, heads_here * HD)
    )
    flat_index = route_slots(routes, CAP)
    feature_width = normed_pre.shape[1]
    slabs = (
        jnp.zeros((EXPERTS * CAP, feature_width), jnp.bfloat16)
        .at[flat_index]
        .set(jnp.repeat(normed_pre, TOP, axis=0))
        .reshape(EXPERTS, CAP, feature_width)
    )
    group_count = seq_count // shards
    arrived, group_parts = axis_share(
        [slabs, packed_parts], [True, False], "seq", group_count, shards, 1
    )
    group_merged = pack_softmax(*merge_softmax(group_parts, request_count, flat_width))
    block_rows, block_parts = axis_share(
        [arrived, group_merged], [False, False], "seq", shards, 1, 2
    )
    stage = merge_softmax(block_parts, request_count, flat_width)
    part_max = stage[0].reshape(request_count, heads_here)
    part_sum = stage[1].reshape(request_count, heads_here)
    part_acc = stage[2].reshape(request_count, heads_here, HD)
    own_key = keys_new.reshape(request_count, heads_here, HD).astype(jnp.float32)
    own_value = values_new.reshape(request_count, heads_here, HD).astype(jnp.float32)
    own_score = (
        jnp.sum(query_rows.astype(jnp.float32) * own_key, axis=-1) * score_scale
        + bias_here[0][None, :]
    )
    row_peak = jnp.maximum(part_max, own_score)
    keep_scale = jnp.exp(part_max - row_peak)
    own_weight = jnp.exp(own_score - row_peak)
    weight_total = part_sum * keep_scale + own_weight
    weighted = part_acc * keep_scale[..., None] + own_weight[..., None] * own_value
    mixed_rows = (
        (weighted / weight_total[..., None])
        .astype(jnp.bfloat16)
        .reshape(request_count, heads_width)
    )
    head_terms = jnp.dot(mixed_rows, out_proj, preferred_element_type=jnp.float32)
    (head_all,) = axis_share([head_terms], [False], "tp", tp_count, 1, 3)
    attended = jnp.sum(head_all, axis=0)
    decode_hidden = (decode_in.astype(jnp.float32) + attended).astype(jnp.bfloat16)
    normed_dec = rms_scale(decode_hidden, norm_gain)
    block_count = block_rows.shape[0] * block_rows.shape[1] * block_rows.shape[2]
    all_rows = jnp.concatenate([block_rows.reshape(block_count, feature_width), normed_dec], axis=0)
    all_out = expert_block(all_rows, weights)
    block_out = all_out[:block_count].reshape(block_rows.shape)
    dec_part = all_out[block_count:]
    part_rows, dec_block = axis_share(
        [block_out, dec_part], [True, False], "seq", shards, 1, 4
    )
    summed = jnp.zeros(part_rows.shape[1:], jnp.float32)
    dec_expert = jnp.zeros(dec_block.shape[1:], jnp.float32)
    for part in range(shards):
        summed = summed + part_rows[part].astype(jnp.float32)
        dec_expert = dec_expert + dec_block[part].astype(jnp.float32)
    my_expert = seq_index // shards
    gate_here = jnp.sum(jnp.where(dec_routes == my_expert, dec_gates, 0.0), axis=1)
    returned, dec_all = axis_share(
        [summed, gate_here[:, None] * dec_expert], [True, False], "seq", group_count, shards, 5
    )
    dec_terms = jnp.sum(dec_all, axis=0)
    decode_out = (decode_hidden.astype(jnp.float32) + dec_terms).astype(jnp.bfloat16)
    picked = jnp.take(returned.reshape(EXPERTS * CAP, -1), flat_index, axis=0)
    picked = picked.reshape(-1, TOP, picked.shape[-1])
    prefill_out = (
        prefill_in.astype(jnp.float32) + jnp.sum(gates[..., None] * picked, axis=1)
    ).astype(jnp.bfloat16)
    return (decode_out, prefill_out)


def solution(mesh):
    placed = (
        P(None, "tp"),
        P(None, "tp"),
        P(None, "tp"),
        P(None, "seq", "tp"),
        P(None, "seq", "tp"),
        P(None, "seq"),
        P(),
        P(),
        P("tp", None),
        P(),
        P(("seq", "tp"), None),
        P(("seq", "tp"), None),
        P(("seq", "tp"), None),
        P(),
        P(),
        P(),
        P("tp", "seq"),
        P("tp", "seq"),
        P("seq", "tp"),
    )
    return jax.shard_map(
        body, mesh=mesh, in_specs=placed, out_specs=(P(), P(("seq", "tp"), None)), check_vma=False
    )
```

```python
import functools
import math

import jax
import jax.numpy as jnp
from jax import lax
from jax.experimental import pallas as pl
from jax.experimental.pallas import tpu as pltpu
from jax.sharding import PartitionSpec as P

HD = 64
EXPERTS = 16
TOP = 2
CAP = 10


def peer_device(axis, peer):
    if axis == "seq":
        return (peer, lax.axis_index("tp"))
    return (lax.axis_index("seq"), peer)


def share_kernel(axis, count, stride, modes, *refs):
    width = len(modes)
    sources = refs[:width]
    outputs = refs[width : 2 * width]
    landed = refs[2 * width : 3 * width]
    send_sems = refs[3 * width : 4 * width]
    recv_sems = refs[4 * width :]
    index = lax.axis_index(axis)
    me = lax.rem(index // stride, count)
    base = index - me * stride

    def member(slot):
        return peer_device(axis, base + slot * stride)

    def piece(which, slot):
        return sources[which].at[slot] if modes[which] else sources[which]

    barrier = pltpu.get_barrier_semaphore()

    def greet(step, carry):
        pl.semaphore_signal(
            barrier,
            inc=1,
            device_id=member(lax.rem(me + step, count)),
            device_id_type=pl.DeviceIdType.MESH,
        )
        return carry

    lax.fori_loop(1, count, greet, 0)
    pl.semaphore_wait(barrier, count - 1)

    def outgoing(which, step):
        target = lax.rem(me + step, count)
        return pltpu.make_async_remote_copy(
            src_ref=piece(which, target),
            dst_ref=landed[which].at[me],
            send_sem=send_sems[which].at[step],
            recv_sem=recv_sems[which].at[step],
            device_id=member(target),
            device_id_type=pl.DeviceIdType.MESH,
        )

    def incoming(which, step):
        source = lax.rem(me - step + count, count)
        return pltpu.make_async_remote_copy(
            src_ref=piece(which, source),
            dst_ref=landed[which].at[source],
            send_sem=send_sems[which].at[step],
            recv_sem=recv_sems[which].at[step],
            device_id=member(source),
            device_id_type=pl.DeviceIdType.MESH,
        )

    def launch(step, carry):
        for which in range(width):
            outgoing(which, step).start()
        return carry

    lax.fori_loop(1, count, launch, 0)
    for which in range(width):
        landed[which][me] = piece(which, me)[...]

    def finish(step, carry):
        for which in range(width):
            outgoing(which, step).wait_send()
            incoming(which, step).wait_recv()
        return carry

    lax.fori_loop(1, count, finish, 0)
    for which in range(width):
        outputs[which][...] = landed[which][...]


def axis_share(payloads, modes, axis, count, stride, collective_id):
    shapes = [x.shape if mode else (count,) + x.shape for x, mode in zip(payloads, modes)]
    width = len(payloads)
    return pl.pallas_call(
        functools.partial(share_kernel, axis, count, stride, tuple(modes)),
        out_shape=[jax.ShapeDtypeStruct(s, x.dtype) for s, x in zip(shapes, payloads)],
        in_specs=[pl.BlockSpec(memory_space=pltpu.VMEM)] * width,
        out_specs=[pl.BlockSpec(memory_space=pltpu.VMEM)] * width,
        scratch_shapes=[pltpu.VMEM(s, x.dtype) for s, x in zip(shapes, payloads)]
        + [pltpu.SemaphoreType.DMA((count,))] * (2 * width),
        compiler_params=pltpu.CompilerParams(collective_id=collective_id, has_side_effects=True),
    )(*payloads)


def outbound_kernel(groups, shards, slab_ref, part_ref, rows_out, parts_out,
                    far_rows, far_parts, near_rows, near_parts,
                    far_send, far_recv, far_psend, far_precv,
                    near_send, near_recv, near_psend, near_precv, local_sem):
    index = lax.axis_index("seq")
    far_me = lax.rem(index // shards, groups)
    far_base = index - far_me * shards
    near_me = lax.rem(index, shards)
    near_base = index - near_me

    def far_member(slot):
        return peer_device("seq", far_base + slot * shards)

    def near_member(slot):
        return peer_device("seq", near_base + slot)

    barrier = pltpu.get_barrier_semaphore()

    def greet_far(step, carry):
        pl.semaphore_signal(barrier, inc=1, device_id=far_member(lax.rem(far_me + step, groups)),
                            device_id_type=pl.DeviceIdType.MESH)
        return carry

    def greet_near(step, carry):
        pl.semaphore_signal(barrier, inc=1, device_id=near_member(lax.rem(near_me + step, shards)),
                            device_id_type=pl.DeviceIdType.MESH)
        return carry

    lax.fori_loop(1, groups, greet_far, 0)
    lax.fori_loop(1, shards, greet_near, 0)
    pl.semaphore_wait(barrier, groups + shards - 2)

    def far_copy(step, slot, landed_slot):
        return (
            pltpu.make_async_remote_copy(
                src_ref=slab_ref.at[slot], dst_ref=far_rows.at[landed_slot],
                send_sem=far_send.at[step], recv_sem=far_recv.at[step],
                device_id=far_member(slot), device_id_type=pl.DeviceIdType.MESH),
            pltpu.make_async_remote_copy(
                src_ref=part_ref, dst_ref=far_parts.at[landed_slot],
                send_sem=far_psend.at[step], recv_sem=far_precv.at[step],
                device_id=far_member(slot), device_id_type=pl.DeviceIdType.MESH),
        )

    def far_start(step, carry):
        for copy in far_copy(step, lax.rem(far_me + step, groups), far_me):
            copy.start()
        return carry

    lax.fori_loop(1, groups, far_start, 0)
    own_slab = pltpu.make_async_copy(slab_ref.at[far_me], far_rows.at[far_me], local_sem.at[0])
    own_part = pltpu.make_async_copy(part_ref, far_parts.at[far_me], local_sem.at[1])
    own_slab.start()
    own_part.start()

    def near_copy(step, slab):
        target = lax.rem(near_me + step, shards)
        return pltpu.make_async_remote_copy(
            src_ref=far_rows.at[slab], dst_ref=near_rows.at[near_me, slab],
            send_sem=near_send.at[step, slab], recv_sem=near_recv.at[step, slab],
            device_id=near_member(target), device_id_type=pl.DeviceIdType.MESH)

    def forward(slab):
        for step in range(1, shards):
            near_copy(step, slab).start()

    own_slab.wait()
    forward(far_me)

    def far_finish(step, carry):
        source = lax.rem(far_me - step + groups, groups)
        rows_copy, parts_copy = far_copy(step, source, source)
        rows_copy.wait_send()
        rows_copy.wait_recv()
        forward(source)
        parts_copy.wait_send()
        parts_copy.wait_recv()
        return carry

    lax.fori_loop(1, groups, far_finish, 0)
    own_part.wait()
    own_rows = pltpu.make_async_copy(far_rows, near_rows.at[near_me], local_sem.at[2])
    own_parts = pltpu.make_async_copy(far_parts, near_parts.at[near_me], local_sem.at[3])
    own_rows.start()
    own_parts.start()

    def near_parts_copy(step, slot):
        return pltpu.make_async_remote_copy(
            src_ref=far_parts, dst_ref=near_parts.at[slot],
            send_sem=near_psend.at[step], recv_sem=near_precv.at[step],
            device_id=near_member(lax.rem(near_me + step, shards)),
            device_id_type=pl.DeviceIdType.MESH)

    for step in range(1, shards):
        near_parts_copy(step, near_me).start()

    def near_finish(step, carry):
        source = lax.rem(near_me - step + shards, shards)

        def per_slab(slab, inner):
            copy = pltpu.make_async_remote_copy(
                src_ref=far_rows.at[slab], dst_ref=near_rows.at[source, slab],
                send_sem=near_send.at[step, slab], recv_sem=near_recv.at[step, slab],
                device_id=near_member(source), device_id_type=pl.DeviceIdType.MESH)
            copy.wait_send()
            copy.wait_recv()
            return inner

        lax.fori_loop(0, groups, per_slab, 0)
        parts_copy = near_parts_copy(step, source)
        parts_copy.wait_send()
        parts_copy.wait_recv()
        return carry

    lax.fori_loop(1, shards, near_finish, 0)
    own_rows.wait()
    own_parts.wait()
    rows_out[...] = near_rows[...]
    parts_out[...] = near_parts[...]


def outbound(slabs, parts, groups, shards, collective_id):
    rows_shape = (shards,) + slabs.shape
    parts_shape = (shards, groups) + parts.shape
    return pl.pallas_call(
        functools.partial(outbound_kernel, groups, shards),
        out_shape=[jax.ShapeDtypeStruct(rows_shape, slabs.dtype),
                   jax.ShapeDtypeStruct(parts_shape, parts.dtype)],
        in_specs=[pl.BlockSpec(memory_space=pltpu.VMEM)] * 2,
        out_specs=[pl.BlockSpec(memory_space=pltpu.VMEM)] * 2,
        scratch_shapes=[
            pltpu.VMEM(slabs.shape, slabs.dtype),
            pltpu.VMEM((groups,) + parts.shape, parts.dtype),
            pltpu.VMEM(rows_shape, slabs.dtype),
            pltpu.VMEM(parts_shape, parts.dtype),
        ]
        + [pltpu.SemaphoreType.DMA((groups,))] * 4
        + [pltpu.SemaphoreType.DMA((shards, groups))] * 2
        + [pltpu.SemaphoreType.DMA((shards,))] * 2
        + [pltpu.SemaphoreType.DMA((4,))],
        compiler_params=pltpu.CompilerParams(collective_id=collective_id, has_side_effects=True),
    )(slabs, parts)


def merge_softmax(stacked, rows, width):
    slot_max = stacked[:, rows, :width]
    slot_sum = stacked[:, rows + 1, :width]
    joint_max = jnp.max(slot_max, axis=0)
    slot_scale = jnp.exp(slot_max - joint_max[None])
    joint_sum = jnp.sum(slot_sum * slot_scale, axis=0)
    lane_scale = jnp.repeat(slot_scale.reshape(slot_scale.shape[0], rows, -1), HD, axis=2)
    joint_acc = jnp.sum(stacked[:, :rows, :] * lane_scale, axis=0)
    return joint_max, joint_sum, joint_acc


def pack_softmax(joint_max, joint_sum, joint_acc):
    rows, lanes = joint_acc.shape
    stats = jnp.stack([joint_max, joint_sum])
    return jnp.concatenate([joint_acc, jnp.pad(stats, ((0, 2), (0, lanes - stats.shape[1])))], axis=0)


def rms_scale(hidden, norm_gain):
    values = hidden.astype(jnp.float32)
    meansq = jnp.mean(values * values, axis=-1, keepdims=True)
    return (values * lax.rsqrt(meansq + 1e-06) * norm_gain).astype(jnp.bfloat16)


def route_slots(route_rows, capacity):
    flat_routes = route_rows.reshape(-1)
    onehot = (flat_routes[:, None] == jnp.arange(EXPERTS, dtype=jnp.int32)[None, :]).astype(
        jnp.int32
    )
    earlier = jnp.cumsum(onehot, axis=0) - onehot
    slot_rank = jnp.sum(earlier * onehot, axis=1)
    return flat_routes * capacity + slot_rank


def expert_block(row_block, weights):
    gate_full, up_full, down_full = weights
    gate_pre = jnp.dot(row_block, gate_full, preferred_element_type=jnp.float32)
    up_pre = jnp.dot(row_block, up_full, preferred_element_type=jnp.float32)
    act = (jax.nn.gelu(gate_pre, approximate=True) * up_pre).astype(jnp.bfloat16)
    return jnp.dot(act, down_full, preferred_element_type=jnp.float32).astype(jnp.bfloat16)


def body(
    queries,
    keys_new,
    values_new,
    key_cache,
    value_cache,
    buckets,
    lengths,
    bias_table,
    out_proj,
    decode_in,
    prefill_in,
    routes,
    gates,
    dec_routes,
    dec_gates,
    norm_gain,
    w_gate,
    w_up,
    w_down,
):
    seq_count = lax.axis_size("seq")
    seq_index = lax.axis_index("seq")
    tp_index = lax.axis_index("tp")
    shards = seq_count // EXPERTS
    weights = (
        lax.all_gather(w_gate, "tp", axis=0, tiled=True),
        lax.all_gather(w_up, "tp", axis=0, tiled=True),
        lax.all_gather(w_down, "tp", axis=1, tiled=True),
    )
    normed_pre = rms_scale(prefill_in, norm_gain)
    request_count, heads_width = queries.shape
    heads_here = heads_width // HD
    ctx_local = key_cache.shape[1]
    score_scale = 1.0 / math.sqrt(HD)
    query_rows = queries.reshape(request_count, heads_here, HD)
    key_rows = key_cache.reshape(request_count, ctx_local, heads_here, HD)
    value_rows = value_cache.reshape(request_count, ctx_local, heads_here, HD).astype(jnp.float32)
    bias_here = lax.dynamic_slice_in_dim(bias_table, tp_index * heads_here, heads_here, 1)
    bucket_hot = (
        buckets[..., None] == jnp.arange(bias_table.shape[0], dtype=jnp.int32)[None, None, :]
    ).astype(jnp.float32)
    bias_rows = jnp.einsum("rcn,nh->rhc", bucket_hot, bias_here, precision=lax.Precision.HIGHEST)
    cache_scores = (
        jnp.einsum("rhd,rchd->rhc", query_rows, key_rows, preferred_element_type=jnp.float32)
        * score_scale
        + bias_rows
    )
    positions = seq_index * ctx_local + jnp.arange(ctx_local, dtype=jnp.int32)
    valid_mask = (positions[None, :] < lengths[:, None])[:, None, :]
    cache_scores = jnp.where(valid_mask, cache_scores, -1e30)
    local_max = jnp.max(cache_scores, axis=-1)
    local_weights = jnp.where(valid_mask, jnp.exp(cache_scores - local_max[..., None]), 0.0)
    local_sum = jnp.sum(local_weights, axis=-1)
    local_acc = jnp.einsum(
        "rhc,rchd->rhd", local_weights, value_rows, precision=lax.Precision.HIGHEST
    )
    tp_count = lax.axis_size("tp")
    flat_width = request_count * heads_here
    packed_parts = pack_softmax(
        local_max.reshape(-1), local_sum.reshape(-1), local_acc.reshape(request_count, heads_here * HD)
    )
    flat_index = route_slots(routes, CAP)
    feature_width = normed_pre.shape[1]
    slabs = (
        jnp.zeros((EXPERTS * CAP, feature_width), jnp.bfloat16)
        .at[flat_index]
        .set(jnp.repeat(normed_pre, TOP, axis=0))
        .reshape(EXPERTS, CAP, feature_width)
    )
    group_count = seq_count // shards
    block_rows, block_parts = outbound(slabs, packed_parts, group_count, shards, 1)
    stage = merge_softmax(
        block_parts.reshape((-1,) + packed_parts.shape), request_count, flat_width
    )
    part_max = stage[0].reshape(request_count, heads_here)
    part_sum = stage[1].reshape(request_count, heads_here)
    part_acc = stage[2].reshape(request_count, heads_here, HD)
    own_key = keys_new.reshape(request_count, heads_here, HD).astype(jnp.float32)
    own_value = values_new.reshape(request_count, heads_here, HD).astype(jnp.float32)
    own_score = (
        jnp.sum(query_rows.astype(jnp.float32) * own_key, axis=-1) * score_scale
        + bias_here[0][None, :]
    )
    row_peak = jnp.maximum(part_max, own_score)
    keep_scale = jnp.exp(part_max - row_peak)
    own_weight = jnp.exp(own_score - row_peak)
    weight_total = part_sum * keep_scale + own_weight
    weighted = part_acc * keep_scale[..., None] + own_weight[..., None] * own_value
    mixed_rows = (
        (weighted / weight_total[..., None])
        .astype(jnp.bfloat16)
        .reshape(request_count, heads_width)
    )
    head_terms = jnp.dot(mixed_rows, out_proj, preferred_element_type=jnp.float32)
    (head_all,) = axis_share([head_terms], [False], "tp", tp_count, 1, 3)
    attended = jnp.sum(head_all, axis=0)
    decode_hidden = (decode_in.astype(jnp.float32) + attended).astype(jnp.bfloat16)
    normed_dec = rms_scale(decode_hidden, norm_gain)
    block_count = block_rows.shape[0] * block_rows.shape[1] * block_rows.shape[2]
    all_rows = jnp.concatenate([block_rows.reshape(block_count, feature_width), normed_dec], axis=0)
    all_out = expert_block(all_rows, weights)
    block_out = all_out[:block_count].reshape(block_rows.shape)
    dec_part = all_out[block_count:]
    part_rows, dec_block = axis_share(
        [block_out, dec_part], [True, False], "seq", shards, 1, 4
    )
    summed = jnp.zeros(part_rows.shape[1:], jnp.float32)
    dec_expert = jnp.zeros(dec_block.shape[1:], jnp.float32)
    for part in range(shards):
        summed = summed + part_rows[part].astype(jnp.float32)
        dec_expert = dec_expert + dec_block[part].astype(jnp.float32)
    my_expert = seq_index // shards
    gate_here = jnp.sum(jnp.where(dec_routes == my_expert, dec_gates, 0.0), axis=1)
    returned, dec_all = axis_share(
        [summed, gate_here[:, None] * dec_expert], [True, False], "seq", group_count, shards, 5
    )
    dec_terms = jnp.sum(dec_all, axis=0)
    decode_out = (decode_hidden.astype(jnp.float32) + dec_terms).astype(jnp.bfloat16)
    picked = jnp.take(returned.reshape(EXPERTS * CAP, -1), flat_index, axis=0)
    picked = picked.reshape(-1, TOP, picked.shape[-1])
    prefill_out = (
        prefill_in.astype(jnp.float32) + jnp.sum(gates[..., None] * picked, axis=1)
    ).astype(jnp.bfloat16)
    return (decode_out, prefill_out)


def solution(mesh):
    placed = (
        P(None, "tp"),
        P(None, "tp"),
        P(None, "tp"),
        P(None, "seq", "tp"),
        P(None, "seq", "tp"),
        P(None, "seq"),
        P(),
        P(),
        P("tp", None),
        P(),
        P(("seq", "tp"), None),
        P(("seq", "tp"), None),
        P(("seq", "tp"), None),
        P(),
        P(),
        P(),
        P("tp", "seq"),
        P("tp", "seq"),
        P("seq", "tp"),
    )
    return jax.shard_map(
        body, mesh=mesh, in_specs=placed, out_specs=(P(), P(("seq", "tp"), None)), check_vma=False
    )
```

```python
import functools
import math

import jax
import jax.numpy as jnp
from jax import lax
from jax.experimental import pallas as pl
from jax.experimental.pallas import tpu as pltpu
from jax.sharding import PartitionSpec as P

HD = 64
EXPERTS = 16
TOP = 2
CAP = 10


def peer_device(axis, peer):
    if axis == "seq":
        return (peer, lax.axis_index("tp"))
    return (lax.axis_index("seq"), peer)


def share_kernel(axis, count, stride, modes, *refs):
    width = len(modes)
    sources = refs[:width]
    outputs = refs[width : 2 * width]
    landed = refs[2 * width : 3 * width]
    send_sems = refs[3 * width : 4 * width]
    recv_sems = refs[4 * width :]
    index = lax.axis_index(axis)
    me = lax.rem(index // stride, count)
    base = index - me * stride

    def member(slot):
        return peer_device(axis, base + slot * stride)

    def piece(which, slot):
        return sources[which].at[slot] if modes[which] else sources[which]

    barrier = pltpu.get_barrier_semaphore()

    def greet(step, carry):
        pl.semaphore_signal(
            barrier,
            inc=1,
            device_id=member(lax.rem(me + step, count)),
            device_id_type=pl.DeviceIdType.MESH,
        )
        return carry

    lax.fori_loop(1, count, greet, 0)
    pl.semaphore_wait(barrier, count - 1)

    def outgoing(which, step):
        target = lax.rem(me + step, count)
        return pltpu.make_async_remote_copy(
            src_ref=piece(which, target),
            dst_ref=landed[which].at[me],
            send_sem=send_sems[which].at[step],
            recv_sem=recv_sems[which].at[step],
            device_id=member(target),
            device_id_type=pl.DeviceIdType.MESH,
        )

    def incoming(which, step):
        source = lax.rem(me - step + count, count)
        return pltpu.make_async_remote_copy(
            src_ref=piece(which, source),
            dst_ref=landed[which].at[source],
            send_sem=send_sems[which].at[step],
            recv_sem=recv_sems[which].at[step],
            device_id=member(source),
            device_id_type=pl.DeviceIdType.MESH,
        )

    def launch(step, carry):
        for which in range(width):
            outgoing(which, step).start()
        return carry

    lax.fori_loop(1, count, launch, 0)
    for which in range(width):
        landed[which][me] = piece(which, me)[...]

    def finish(step, carry):
        for which in range(width):
            outgoing(which, step).wait_send()
            incoming(which, step).wait_recv()
        return carry

    lax.fori_loop(1, count, finish, 0)
    for which in range(width):
        outputs[which][...] = landed[which][...]


def axis_share(payloads, modes, axis, count, stride, collective_id):
    shapes = [x.shape if mode else (count,) + x.shape for x, mode in zip(payloads, modes)]
    width = len(payloads)
    return pl.pallas_call(
        functools.partial(share_kernel, axis, count, stride, tuple(modes)),
        out_shape=[jax.ShapeDtypeStruct(s, x.dtype) for s, x in zip(shapes, payloads)],
        in_specs=[pl.BlockSpec(memory_space=pltpu.VMEM)] * width,
        out_specs=[pl.BlockSpec(memory_space=pltpu.VMEM)] * width,
        scratch_shapes=[pltpu.VMEM(s, x.dtype) for s, x in zip(shapes, payloads)]
        + [pltpu.SemaphoreType.DMA((count,))] * (2 * width),
        compiler_params=pltpu.CompilerParams(collective_id=collective_id, has_side_effects=True),
    )(*payloads)


def outbound_kernel(groups, shards, slab_ref, part_ref, rows_out, parts_out,
                    far_parts, near_rows, near_parts,
                    far_send, far_recv, far_psend, far_precv,
                    near_send, near_recv, near_psend, near_precv, local_sem):
    index = lax.axis_index("seq")
    far_me = lax.rem(index // shards, groups)
    far_base = index - far_me * shards
    place = lax.rem(index, shards)
    near_base = index - place
    has_right = place < shards - 1
    has_left = place > 0

    def far_member(slot):
        return peer_device("seq", far_base + slot * shards)

    def near_member(slot):
        return peer_device("seq", near_base + slot)

    barrier = pltpu.get_barrier_semaphore()

    def greet_far(step, carry):
        pl.semaphore_signal(barrier, inc=1, device_id=far_member(lax.rem(far_me + step, groups)),
                            device_id_type=pl.DeviceIdType.MESH)
        return carry

    def greet_near(step, carry):
        pl.semaphore_signal(barrier, inc=1, device_id=near_member(lax.rem(place + step, shards)),
                            device_id_type=pl.DeviceIdType.MESH)
        return carry

    lax.fori_loop(1, groups, greet_far, 0)
    lax.fori_loop(1, shards, greet_near, 0)
    pl.semaphore_wait(barrier, groups + shards - 2)

    def far_copy(step, slot, landed_slot):
        return (
            pltpu.make_async_remote_copy(
                src_ref=slab_ref.at[slot], dst_ref=near_rows.at[place, landed_slot],
                send_sem=far_send.at[step], recv_sem=far_recv.at[step],
                device_id=far_member(slot), device_id_type=pl.DeviceIdType.MESH),
            pltpu.make_async_remote_copy(
                src_ref=part_ref, dst_ref=far_parts.at[landed_slot],
                send_sem=far_psend.at[step], recv_sem=far_precv.at[step],
                device_id=far_member(slot), device_id_type=pl.DeviceIdType.MESH),
        )

    def far_start(step, carry):
        for copy in far_copy(step, lax.rem(far_me + step, groups), far_me):
            copy.start()
        return carry

    lax.fori_loop(1, groups, far_start, 0)
    own_slab = pltpu.make_async_copy(slab_ref.at[far_me], near_rows.at[place, far_me], local_sem.at[0])
    own_part = pltpu.make_async_copy(part_ref, far_parts.at[far_me], local_sem.at[1])
    own_slab.start()
    own_part.start()

    def chain_copy(direction, origin, slab):
        return pltpu.make_async_remote_copy(
            src_ref=near_rows.at[origin, slab], dst_ref=near_rows.at[origin, slab],
            send_sem=near_send.at[direction, origin, slab], recv_sem=near_recv.at[origin, slab],
            device_id=near_member(place + 1 - 2 * direction), device_id_type=pl.DeviceIdType.MESH)

    def pass_on(origin, slab, to_right, to_left):
        @pl.when(to_right)
        def _():
            chain_copy(0, origin, slab).start()

        @pl.when(to_left)
        def _():
            chain_copy(1, origin, slab).start()

    own_slab.wait()
    pass_on(place, far_me, has_right, has_left)

    def far_finish(step, carry):
        source = lax.rem(far_me - step + groups, groups)
        rows_copy, parts_copy = far_copy(step, source, source)
        rows_copy.wait_send()
        rows_copy.wait_recv()
        pass_on(place, source, has_right, has_left)
        parts_copy.wait_send()
        parts_copy.wait_recv()
        return carry

    lax.fori_loop(1, groups, far_finish, 0)
    own_part.wait()
    own_parts = pltpu.make_async_copy(far_parts, near_parts.at[place], local_sem.at[2])
    own_parts.start()

    def near_parts_copy(step, slot):
        return pltpu.make_async_remote_copy(
            src_ref=far_parts, dst_ref=near_parts.at[slot],
            send_sem=near_psend.at[step], recv_sem=near_precv.at[step],
            device_id=near_member(lax.rem(place + step, shards)),
            device_id_type=pl.DeviceIdType.MESH)

    for step in range(1, shards):
        near_parts_copy(step, place).start()

    for distance in range(1, shards):
        def relay(slab, carry, distance=distance):
            from_left = place - distance
            from_right = place + distance

            @pl.when(from_left >= 0)
            def _():
                chain_copy(0, from_left, slab).wait_recv()
                pass_on(from_left, slab, has_right, False)

            @pl.when(from_right < shards)
            def _():
                chain_copy(1, from_right, slab).wait_recv()
                pass_on(from_right, slab, False, has_left)

            return carry

        lax.fori_loop(0, groups, relay, 0)

    for origin in range(shards):
        def drain(slab, carry, origin=origin):
            @pl.when((origin <= place) & has_right)
            def _():
                chain_copy(0, origin, slab).wait_send()

            @pl.when((origin >= place) & has_left)
            def _():
                chain_copy(1, origin, slab).wait_send()

            return carry

        lax.fori_loop(0, groups, drain, 0)

    def parts_finish(step, carry):
        parts_copy = near_parts_copy(step, lax.rem(place - step + shards, shards))
        parts_copy.wait_send()
        parts_copy.wait_recv()
        return carry

    lax.fori_loop(1, shards, parts_finish, 0)
    own_parts.wait()
    rows_out[...] = near_rows[...]
    parts_out[...] = near_parts[...]


def outbound(slabs, parts, groups, shards, collective_id):
    rows_shape = (shards,) + slabs.shape
    parts_shape = (shards, groups) + parts.shape
    return pl.pallas_call(
        functools.partial(outbound_kernel, groups, shards),
        out_shape=[jax.ShapeDtypeStruct(rows_shape, slabs.dtype),
                   jax.ShapeDtypeStruct(parts_shape, parts.dtype)],
        in_specs=[pl.BlockSpec(memory_space=pltpu.VMEM)] * 2,
        out_specs=[pl.BlockSpec(memory_space=pltpu.VMEM)] * 2,
        scratch_shapes=[
            pltpu.VMEM((groups,) + parts.shape, parts.dtype),
            pltpu.VMEM(rows_shape, slabs.dtype),
            pltpu.VMEM(parts_shape, parts.dtype),
        ]
        + [pltpu.SemaphoreType.DMA((groups,))] * 4
        + [pltpu.SemaphoreType.DMA((2, shards, groups)), pltpu.SemaphoreType.DMA((shards, groups))]
        + [pltpu.SemaphoreType.DMA((shards,))] * 2
        + [pltpu.SemaphoreType.DMA((4,))],
        compiler_params=pltpu.CompilerParams(collective_id=collective_id, has_side_effects=True),
    )(slabs, parts)


def merge_softmax(stacked, rows, width):
    slot_max = stacked[:, rows, :width]
    slot_sum = stacked[:, rows + 1, :width]
    joint_max = jnp.max(slot_max, axis=0)
    slot_scale = jnp.exp(slot_max - joint_max[None])
    joint_sum = jnp.sum(slot_sum * slot_scale, axis=0)
    lane_scale = jnp.repeat(slot_scale.reshape(slot_scale.shape[0], rows, -1), HD, axis=2)
    joint_acc = jnp.sum(stacked[:, :rows, :] * lane_scale, axis=0)
    return joint_max, joint_sum, joint_acc


def pack_softmax(joint_max, joint_sum, joint_acc):
    rows, lanes = joint_acc.shape
    stats = jnp.stack([joint_max, joint_sum])
    return jnp.concatenate([joint_acc, jnp.pad(stats, ((0, 2), (0, lanes - stats.shape[1])))], axis=0)


def rms_scale(hidden, norm_gain):
    values = hidden.astype(jnp.float32)
    meansq = jnp.mean(values * values, axis=-1, keepdims=True)
    return (values * lax.rsqrt(meansq + 1e-06) * norm_gain).astype(jnp.bfloat16)


def route_slots(route_rows, capacity):
    flat_routes = route_rows.reshape(-1)
    onehot = (flat_routes[:, None] == jnp.arange(EXPERTS, dtype=jnp.int32)[None, :]).astype(
        jnp.int32
    )
    earlier = jnp.cumsum(onehot, axis=0) - onehot
    slot_rank = jnp.sum(earlier * onehot, axis=1)
    return flat_routes * capacity + slot_rank


def expert_block(row_block, weights):
    gate_full, up_full, down_full = weights
    gate_pre = jnp.dot(row_block, gate_full, preferred_element_type=jnp.float32)
    up_pre = jnp.dot(row_block, up_full, preferred_element_type=jnp.float32)
    act = (jax.nn.gelu(gate_pre, approximate=True) * up_pre).astype(jnp.bfloat16)
    return jnp.dot(act, down_full, preferred_element_type=jnp.float32).astype(jnp.bfloat16)


def body(
    queries,
    keys_new,
    values_new,
    key_cache,
    value_cache,
    buckets,
    lengths,
    bias_table,
    out_proj,
    decode_in,
    prefill_in,
    routes,
    gates,
    dec_routes,
    dec_gates,
    norm_gain,
    w_gate,
    w_up,
    w_down,
):
    seq_count = lax.axis_size("seq")
    seq_index = lax.axis_index("seq")
    tp_index = lax.axis_index("tp")
    shards = seq_count // EXPERTS
    weights = (
        lax.all_gather(w_gate, "tp", axis=0, tiled=True),
        lax.all_gather(w_up, "tp", axis=0, tiled=True),
        lax.all_gather(w_down, "tp", axis=1, tiled=True),
    )
    normed_pre = rms_scale(prefill_in, norm_gain)
    request_count, heads_width = queries.shape
    heads_here = heads_width // HD
    ctx_local = key_cache.shape[1]
    score_scale = 1.0 / math.sqrt(HD)
    query_rows = queries.reshape(request_count, heads_here, HD)
    key_rows = key_cache.reshape(request_count, ctx_local, heads_here, HD)
    value_rows = value_cache.reshape(request_count, ctx_local, heads_here, HD).astype(jnp.float32)
    bias_here = lax.dynamic_slice_in_dim(bias_table, tp_index * heads_here, heads_here, 1)
    bucket_hot = (
        buckets[..., None] == jnp.arange(bias_table.shape[0], dtype=jnp.int32)[None, None, :]
    ).astype(jnp.float32)
    bias_rows = jnp.einsum("rcn,nh->rhc", bucket_hot, bias_here, precision=lax.Precision.HIGHEST)
    cache_scores = (
        jnp.einsum("rhd,rchd->rhc", query_rows, key_rows, preferred_element_type=jnp.float32)
        * score_scale
        + bias_rows
    )
    positions = seq_index * ctx_local + jnp.arange(ctx_local, dtype=jnp.int32)
    valid_mask = (positions[None, :] < lengths[:, None])[:, None, :]
    cache_scores = jnp.where(valid_mask, cache_scores, -1e30)
    local_max = jnp.max(cache_scores, axis=-1)
    local_weights = jnp.where(valid_mask, jnp.exp(cache_scores - local_max[..., None]), 0.0)
    local_sum = jnp.sum(local_weights, axis=-1)
    local_acc = jnp.einsum(
        "rhc,rchd->rhd", local_weights, value_rows, precision=lax.Precision.HIGHEST
    )
    tp_count = lax.axis_size("tp")
    flat_width = request_count * heads_here
    packed_parts = pack_softmax(
        local_max.reshape(-1), local_sum.reshape(-1), local_acc.reshape(request_count, heads_here * HD)
    )
    flat_index = route_slots(routes, CAP)
    feature_width = normed_pre.shape[1]
    slabs = (
        jnp.zeros((EXPERTS * CAP, feature_width), jnp.bfloat16)
        .at[flat_index]
        .set(jnp.repeat(normed_pre, TOP, axis=0))
        .reshape(EXPERTS, CAP, feature_width)
    )
    group_count = seq_count // shards
    block_rows, block_parts = outbound(slabs, packed_parts, group_count, shards, 1)
    stage = merge_softmax(
        block_parts.reshape((-1,) + packed_parts.shape), request_count, flat_width
    )
    part_max = stage[0].reshape(request_count, heads_here)
    part_sum = stage[1].reshape(request_count, heads_here)
    part_acc = stage[2].reshape(request_count, heads_here, HD)
    own_key = keys_new.reshape(request_count, heads_here, HD).astype(jnp.float32)
    own_value = values_new.reshape(request_count, heads_here, HD).astype(jnp.float32)
    own_score = (
        jnp.sum(query_rows.astype(jnp.float32) * own_key, axis=-1) * score_scale
        + bias_here[0][None, :]
    )
    row_peak = jnp.maximum(part_max, own_score)
    keep_scale = jnp.exp(part_max - row_peak)
    own_weight = jnp.exp(own_score - row_peak)
    weight_total = part_sum * keep_scale + own_weight
    weighted = part_acc * keep_scale[..., None] + own_weight[..., None] * own_value
    mixed_rows = (
        (weighted / weight_total[..., None])
        .astype(jnp.bfloat16)
        .reshape(request_count, heads_width)
    )
    head_terms = jnp.dot(mixed_rows, out_proj, preferred_element_type=jnp.float32)
    (head_all,) = axis_share([head_terms], [False], "tp", tp_count, 1, 3)
    attended = jnp.sum(head_all, axis=0)
    decode_hidden = (decode_in.astype(jnp.float32) + attended).astype(jnp.bfloat16)
    normed_dec = rms_scale(decode_hidden, norm_gain)
    block_count = block_rows.shape[0] * block_rows.shape[1] * block_rows.shape[2]
    all_rows = jnp.concatenate([block_rows.reshape(block_count, feature_width), normed_dec], axis=0)
    all_out = expert_block(all_rows, weights)
    block_out = all_out[:block_count].reshape(block_rows.shape)
    dec_part = all_out[block_count:]
    part_rows, dec_block = axis_share(
        [block_out, dec_part], [True, False], "seq", shards, 1, 4
    )
    summed = jnp.zeros(part_rows.shape[1:], jnp.float32)
    dec_expert = jnp.zeros(dec_block.shape[1:], jnp.float32)
    for part in range(shards):
        summed = summed + part_rows[part].astype(jnp.float32)
        dec_expert = dec_expert + dec_block[part].astype(jnp.float32)
    my_expert = seq_index // shards
    gate_here = jnp.sum(jnp.where(dec_routes == my_expert, dec_gates, 0.0), axis=1)
    returned, dec_all = axis_share(
        [summed, gate_here[:, None] * dec_expert], [True, False], "seq", group_count, shards, 5
    )
    dec_terms = jnp.sum(dec_all, axis=0)
    decode_out = (decode_hidden.astype(jnp.float32) + dec_terms).astype(jnp.bfloat16)
    picked = jnp.take(returned.reshape(EXPERTS * CAP, -1), flat_index, axis=0)
    picked = picked.reshape(-1, TOP, picked.shape[-1])
    prefill_out = (
        prefill_in.astype(jnp.float32) + jnp.sum(gates[..., None] * picked, axis=1)
    ).astype(jnp.bfloat16)
    return (decode_out, prefill_out)


def solution(mesh):
    placed = (
        P(None, "tp"),
        P(None, "tp"),
        P(None, "tp"),
        P(None, "seq", "tp"),
        P(None, "seq", "tp"),
        P(None, "seq"),
        P(),
        P(),
        P("tp", None),
        P(),
        P(("seq", "tp"), None),
        P(("seq", "tp"), None),
        P(("seq", "tp"), None),
        P(),
        P(),
        P(),
        P("tp", "seq"),
        P("tp", "seq"),
        P("seq", "tp"),
    )
    return jax.shard_map(
        body, mesh=mesh, in_specs=placed, out_specs=(P(), P(("seq", "tp"), None)), check_vma=False
    )
```

```python
import functools
import math

import jax
import jax.numpy as jnp
from jax import lax
from jax.experimental import pallas as pl
from jax.experimental.pallas import tpu as pltpu
from jax.sharding import PartitionSpec as P

HD = 64
EXPERTS = 16
TOP = 2
CAP = 10


def peer_device(axis, peer):
    if axis == "seq":
        return (peer, lax.axis_index("tp"))
    return (lax.axis_index("seq"), peer)


def share_kernel(axis, count, stride, modes, *refs):
    width = len(modes)
    sources = refs[:width]
    outputs = refs[width : 2 * width]
    landed = refs[2 * width : 3 * width]
    send_sems = refs[3 * width : 4 * width]
    recv_sems = refs[4 * width :]
    index = lax.axis_index(axis)
    me = lax.rem(index // stride, count)
    base = index - me * stride

    def member(slot):
        return peer_device(axis, base + slot * stride)

    def piece(which, slot):
        return sources[which].at[slot] if modes[which] else sources[which]

    barrier = pltpu.get_barrier_semaphore()

    def greet(step, carry):
        pl.semaphore_signal(
            barrier,
            inc=1,
            device_id=member(lax.rem(me + step, count)),
            device_id_type=pl.DeviceIdType.MESH,
        )
        return carry

    lax.fori_loop(1, count, greet, 0)
    pl.semaphore_wait(barrier, count - 1)

    def outgoing(which, step):
        target = lax.rem(me + step, count)
        return pltpu.make_async_remote_copy(
            src_ref=piece(which, target),
            dst_ref=landed[which].at[me],
            send_sem=send_sems[which].at[step],
            recv_sem=recv_sems[which].at[step],
            device_id=member(target),
            device_id_type=pl.DeviceIdType.MESH,
        )

    def incoming(which, step):
        source = lax.rem(me - step + count, count)
        return pltpu.make_async_remote_copy(
            src_ref=piece(which, source),
            dst_ref=landed[which].at[source],
            send_sem=send_sems[which].at[step],
            recv_sem=recv_sems[which].at[step],
            device_id=member(source),
            device_id_type=pl.DeviceIdType.MESH,
        )

    def launch(step, carry):
        for which in range(width):
            outgoing(which, step).start()
        return carry

    lax.fori_loop(1, count, launch, 0)
    for which in range(width):
        landed[which][me] = piece(which, me)[...]

    def finish(step, carry):
        for which in range(width):
            outgoing(which, step).wait_send()
            incoming(which, step).wait_recv()
        return carry

    lax.fori_loop(1, count, finish, 0)
    for which in range(width):
        outputs[which][...] = landed[which][...]


def axis_share(payloads, modes, axis, count, stride, collective_id):
    shapes = [x.shape if mode else (count,) + x.shape for x, mode in zip(payloads, modes)]
    width = len(payloads)
    return pl.pallas_call(
        functools.partial(share_kernel, axis, count, stride, tuple(modes)),
        out_shape=[jax.ShapeDtypeStruct(s, x.dtype) for s, x in zip(shapes, payloads)],
        in_specs=[pl.BlockSpec(memory_space=pltpu.VMEM)] * width,
        out_specs=[pl.BlockSpec(memory_space=pltpu.VMEM)] * width,
        scratch_shapes=[pltpu.VMEM(s, x.dtype) for s, x in zip(shapes, payloads)]
        + [pltpu.SemaphoreType.DMA((count,))] * (2 * width),
        compiler_params=pltpu.CompilerParams(collective_id=collective_id, has_side_effects=True),
    )(*payloads)


def outbound_kernel(groups, shards, lanes, slab_ref, part_ref, gate_ref, up_ref, down_ref,
                    rows_out, parts_out, gate_out, up_out, down_out,
                    far_parts, near_rows, near_parts, gate_all, up_all, down_all,
                    far_send, far_recv, far_psend, far_precv,
                    near_send, near_recv, near_psend, near_precv, local_sem,
                    lane_send, lane_recv):
    index = lax.axis_index("seq")
    far_me = lax.rem(index // shards, groups)
    far_base = index - far_me * shards
    place = lax.rem(index, shards)
    near_base = index - place
    has_right = place < shards - 1
    has_left = place > 0

    def far_member(slot):
        return peer_device("seq", far_base + slot * shards)

    def near_member(slot):
        return peer_device("seq", near_base + slot)

    barrier = pltpu.get_barrier_semaphore()

    def greet_far(step, carry):
        pl.semaphore_signal(barrier, inc=1, device_id=far_member(lax.rem(far_me + step, groups)),
                            device_id_type=pl.DeviceIdType.MESH)
        return carry

    def greet_near(step, carry):
        pl.semaphore_signal(barrier, inc=1, device_id=near_member(lax.rem(place + step, shards)),
                            device_id_type=pl.DeviceIdType.MESH)
        return carry

    lane_me = lax.axis_index("tp")

    def lane_member(slot):
        return peer_device("tp", slot)

    def greet_lane(step, carry):
        pl.semaphore_signal(barrier, inc=1, device_id=lane_member(lax.rem(lane_me + step, lanes)),
                            device_id_type=pl.DeviceIdType.MESH)
        return carry

    lax.fori_loop(1, groups, greet_far, 0)
    lax.fori_loop(1, shards, greet_near, 0)
    lax.fori_loop(1, lanes, greet_lane, 0)
    pl.semaphore_wait(barrier, groups + shards + lanes - 3)
    weight_refs = ((gate_ref, gate_all), (up_ref, up_all), (down_ref, down_all))

    def lane_copy(which, step, slot, landed_slot):
        source_ref, landed_ref = weight_refs[which]
        return pltpu.make_async_remote_copy(
            src_ref=source_ref, dst_ref=landed_ref.at[landed_slot],
            send_sem=lane_send.at[which, step], recv_sem=lane_recv.at[which, step],
            device_id=lane_member(slot), device_id_type=pl.DeviceIdType.MESH)

    def lane_start(step, carry):
        for which in range(3):
            lane_copy(which, step, lax.rem(lane_me + step, lanes), lane_me).start()
        return carry

    lax.fori_loop(1, lanes, lane_start, 0)
    own_weights = [
        pltpu.make_async_copy(source_ref, landed_ref.at[lane_me], local_sem.at[3 + which])
        for which, (source_ref, landed_ref) in enumerate(weight_refs)
    ]
    for copy in own_weights:
        copy.start()

    def far_copy(step, slot, landed_slot):
        return (
            pltpu.make_async_remote_copy(
                src_ref=slab_ref.at[slot], dst_ref=near_rows.at[place, landed_slot],
                send_sem=far_send.at[step], recv_sem=far_recv.at[step],
                device_id=far_member(slot), device_id_type=pl.DeviceIdType.MESH),
            pltpu.make_async_remote_copy(
                src_ref=part_ref, dst_ref=far_parts.at[landed_slot],
                send_sem=far_psend.at[step], recv_sem=far_precv.at[step],
                device_id=far_member(slot), device_id_type=pl.DeviceIdType.MESH),
        )

    def far_start(step, carry):
        for copy in far_copy(step, lax.rem(far_me + step, groups), far_me):
            copy.start()
        return carry

    lax.fori_loop(1, groups, far_start, 0)
    own_slab = pltpu.make_async_copy(slab_ref.at[far_me], near_rows.at[place, far_me], local_sem.at[0])
    own_part = pltpu.make_async_copy(part_ref, far_parts.at[far_me], local_sem.at[1])
    own_slab.start()
    own_part.start()

    def chain_copy(direction, origin, slab):
        return pltpu.make_async_remote_copy(
            src_ref=near_rows.at[origin, slab], dst_ref=near_rows.at[origin, slab],
            send_sem=near_send.at[direction, origin, slab], recv_sem=near_recv.at[origin, slab],
            device_id=near_member(place + 1 - 2 * direction), device_id_type=pl.DeviceIdType.MESH)

    def pass_on(origin, slab, to_right, to_left):
        @pl.when(to_right)
        def _():
            chain_copy(0, origin, slab).start()

        @pl.when(to_left)
        def _():
            chain_copy(1, origin, slab).start()

    own_slab.wait()
    pass_on(place, far_me, has_right, has_left)

    def far_finish(step, carry):
        source = lax.rem(far_me - step + groups, groups)
        rows_copy, parts_copy = far_copy(step, source, source)
        rows_copy.wait_send()
        rows_copy.wait_recv()
        pass_on(place, source, has_right, has_left)
        parts_copy.wait_send()
        parts_copy.wait_recv()
        return carry

    lax.fori_loop(1, groups, far_finish, 0)
    own_part.wait()
    own_parts = pltpu.make_async_copy(far_parts, near_parts.at[place], local_sem.at[2])
    own_parts.start()

    def near_parts_copy(step, slot):
        return pltpu.make_async_remote_copy(
            src_ref=far_parts, dst_ref=near_parts.at[slot],
            send_sem=near_psend.at[step], recv_sem=near_precv.at[step],
            device_id=near_member(lax.rem(place + step, shards)),
            device_id_type=pl.DeviceIdType.MESH)

    for step in range(1, shards):
        near_parts_copy(step, place).start()

    for distance in range(1, shards):
        def relay(slab, carry, distance=distance):
            from_left = place - distance
            from_right = place + distance

            @pl.when(from_left >= 0)
            def _():
                chain_copy(0, from_left, slab).wait_recv()
                pass_on(from_left, slab, has_right, False)

            @pl.when(from_right < shards)
            def _():
                chain_copy(1, from_right, slab).wait_recv()
                pass_on(from_right, slab, False, has_left)

            return carry

        lax.fori_loop(0, groups, relay, 0)

    for origin in range(shards):
        def drain(slab, carry, origin=origin):
            @pl.when((origin <= place) & has_right)
            def _():
                chain_copy(0, origin, slab).wait_send()

            @pl.when((origin >= place) & has_left)
            def _():
                chain_copy(1, origin, slab).wait_send()

            return carry

        lax.fori_loop(0, groups, drain, 0)

    def parts_finish(step, carry):
        parts_copy = near_parts_copy(step, lax.rem(place - step + shards, shards))
        parts_copy.wait_send()
        parts_copy.wait_recv()
        return carry

    lax.fori_loop(1, shards, parts_finish, 0)
    own_parts.wait()

    def lane_finish(step, carry):
        source = lax.rem(lane_me - step + lanes, lanes)
        for which in range(3):
            copy = lane_copy(which, step, source, source)
            copy.wait_send()
            copy.wait_recv()
        return carry

    lax.fori_loop(1, lanes, lane_finish, 0)
    for copy in own_weights:
        copy.wait()
    rows_out[...] = near_rows[...]
    parts_out[...] = near_parts[...]
    gate_out[...] = gate_all[...]
    up_out[...] = up_all[...]
    down_out[...] = down_all[...]


def outbound(slabs, parts, weights, groups, shards, lanes, collective_id):
    rows_shape = (shards,) + slabs.shape
    parts_shape = (shards, groups) + parts.shape
    weight_shapes = [jax.ShapeDtypeStruct((lanes,) + w.shape, w.dtype) for w in weights]
    return pl.pallas_call(
        functools.partial(outbound_kernel, groups, shards, lanes),
        out_shape=[jax.ShapeDtypeStruct(rows_shape, slabs.dtype),
                   jax.ShapeDtypeStruct(parts_shape, parts.dtype)] + weight_shapes,
        in_specs=[pl.BlockSpec(memory_space=pltpu.VMEM)] * 5,
        out_specs=[pl.BlockSpec(memory_space=pltpu.VMEM)] * 5,
        scratch_shapes=[
            pltpu.VMEM((groups,) + parts.shape, parts.dtype),
            pltpu.VMEM(rows_shape, slabs.dtype),
            pltpu.VMEM(parts_shape, parts.dtype),
        ]
        + [pltpu.VMEM(w.shape, w.dtype) for w in weight_shapes]
        + [pltpu.SemaphoreType.DMA((groups,))] * 4
        + [pltpu.SemaphoreType.DMA((2, shards, groups)), pltpu.SemaphoreType.DMA((shards, groups))]
        + [pltpu.SemaphoreType.DMA((shards,))] * 2
        + [pltpu.SemaphoreType.DMA((8,))]
        + [pltpu.SemaphoreType.DMA((3, lanes))] * 2,
        compiler_params=pltpu.CompilerParams(collective_id=collective_id, has_side_effects=True),
    )(slabs, parts, *weights)


def merge_softmax(stacked, rows, width):
    slot_max = stacked[:, rows, :width]
    slot_sum = stacked[:, rows + 1, :width]
    joint_max = jnp.max(slot_max, axis=0)
    slot_scale = jnp.exp(slot_max - joint_max[None])
    joint_sum = jnp.sum(slot_sum * slot_scale, axis=0)
    lane_scale = jnp.repeat(slot_scale.reshape(slot_scale.shape[0], rows, -1), HD, axis=2)
    joint_acc = jnp.sum(stacked[:, :rows, :] * lane_scale, axis=0)
    return joint_max, joint_sum, joint_acc


def pack_softmax(joint_max, joint_sum, joint_acc):
    rows, lanes = joint_acc.shape
    stats = jnp.stack([joint_max, joint_sum])
    return jnp.concatenate([joint_acc, jnp.pad(stats, ((0, 2), (0, lanes - stats.shape[1])))], axis=0)


def rms_scale(hidden, norm_gain):
    values = hidden.astype(jnp.float32)
    meansq = jnp.mean(values * values, axis=-1, keepdims=True)
    return (values * lax.rsqrt(meansq + 1e-06) * norm_gain).astype(jnp.bfloat16)


def route_slots(route_rows, capacity):
    flat_routes = route_rows.reshape(-1)
    onehot = (flat_routes[:, None] == jnp.arange(EXPERTS, dtype=jnp.int32)[None, :]).astype(
        jnp.int32
    )
    earlier = jnp.cumsum(onehot, axis=0) - onehot
    slot_rank = jnp.sum(earlier * onehot, axis=1)
    return flat_routes * capacity + slot_rank


def expert_block(row_block, weights):
    gate_full, up_full, down_full = weights
    gate_pre = jnp.dot(row_block, gate_full, preferred_element_type=jnp.float32)
    up_pre = jnp.dot(row_block, up_full, preferred_element_type=jnp.float32)
    act = (jax.nn.gelu(gate_pre, approximate=True) * up_pre).astype(jnp.bfloat16)
    return jnp.dot(act, down_full, preferred_element_type=jnp.float32).astype(jnp.bfloat16)


def body(
    queries,
    keys_new,
    values_new,
    key_cache,
    value_cache,
    buckets,
    lengths,
    bias_table,
    out_proj,
    decode_in,
    prefill_in,
    routes,
    gates,
    dec_routes,
    dec_gates,
    norm_gain,
    w_gate,
    w_up,
    w_down,
):
    seq_count = lax.axis_size("seq")
    seq_index = lax.axis_index("seq")
    tp_index = lax.axis_index("tp")
    shards = seq_count // EXPERTS
    normed_pre = rms_scale(prefill_in, norm_gain)
    request_count, heads_width = queries.shape
    heads_here = heads_width // HD
    ctx_local = key_cache.shape[1]
    score_scale = 1.0 / math.sqrt(HD)
    query_rows = queries.reshape(request_count, heads_here, HD)
    key_rows = key_cache.reshape(request_count, ctx_local, heads_here, HD)
    value_rows = value_cache.reshape(request_count, ctx_local, heads_here, HD).astype(jnp.float32)
    bias_here = lax.dynamic_slice_in_dim(bias_table, tp_index * heads_here, heads_here, 1)
    bucket_hot = (
        buckets[..., None] == jnp.arange(bias_table.shape[0], dtype=jnp.int32)[None, None, :]
    ).astype(jnp.float32)
    bias_rows = jnp.einsum("rcn,nh->rhc", bucket_hot, bias_here, precision=lax.Precision.HIGHEST)
    cache_scores = (
        jnp.einsum("rhd,rchd->rhc", query_rows, key_rows, preferred_element_type=jnp.float32)
        * score_scale
        + bias_rows
    )
    positions = seq_index * ctx_local + jnp.arange(ctx_local, dtype=jnp.int32)
    valid_mask = (positions[None, :] < lengths[:, None])[:, None, :]
    cache_scores = jnp.where(valid_mask, cache_scores, -1e30)
    local_max = jnp.max(cache_scores, axis=-1)
    local_weights = jnp.where(valid_mask, jnp.exp(cache_scores - local_max[..., None]), 0.0)
    local_sum = jnp.sum(local_weights, axis=-1)
    local_acc = jnp.einsum(
        "rhc,rchd->rhd", local_weights, value_rows, precision=lax.Precision.HIGHEST
    )
    tp_count = lax.axis_size("tp")
    flat_width = request_count * heads_here
    packed_parts = pack_softmax(
        local_max.reshape(-1), local_sum.reshape(-1), local_acc.reshape(request_count, heads_here * HD)
    )
    flat_index = route_slots(routes, CAP)
    feature_width = normed_pre.shape[1]
    slabs = (
        jnp.zeros((EXPERTS * CAP, feature_width), jnp.bfloat16)
        .at[flat_index]
        .set(jnp.repeat(normed_pre, TOP, axis=0))
        .reshape(EXPERTS, CAP, feature_width)
    )
    group_count = seq_count // shards
    block_rows, block_parts, gate_all, up_all, down_all = outbound(
        slabs, packed_parts, (w_gate, w_up, w_down), group_count, shards, tp_count, 1
    )
    weights = (
        gate_all.reshape(-1, gate_all.shape[-1]),
        up_all.reshape(-1, up_all.shape[-1]),
        jnp.transpose(down_all, (1, 0, 2)).reshape(down_all.shape[1], -1),
    )
    stage = merge_softmax(
        block_parts.reshape((-1,) + packed_parts.shape), request_count, flat_width
    )
    part_max = stage[0].reshape(request_count, heads_here)
    part_sum = stage[1].reshape(request_count, heads_here)
    part_acc = stage[2].reshape(request_count, heads_here, HD)
    own_key = keys_new.reshape(request_count, heads_here, HD).astype(jnp.float32)
    own_value = values_new.reshape(request_count, heads_here, HD).astype(jnp.float32)
    own_score = (
        jnp.sum(query_rows.astype(jnp.float32) * own_key, axis=-1) * score_scale
        + bias_here[0][None, :]
    )
    row_peak = jnp.maximum(part_max, own_score)
    keep_scale = jnp.exp(part_max - row_peak)
    own_weight = jnp.exp(own_score - row_peak)
    weight_total = part_sum * keep_scale + own_weight
    weighted = part_acc * keep_scale[..., None] + own_weight[..., None] * own_value
    mixed_rows = (
        (weighted / weight_total[..., None])
        .astype(jnp.bfloat16)
        .reshape(request_count, heads_width)
    )
    head_terms = jnp.dot(mixed_rows, out_proj, preferred_element_type=jnp.float32)
    (head_all,) = axis_share([head_terms], [False], "tp", tp_count, 1, 3)
    attended = jnp.sum(head_all, axis=0)
    decode_hidden = (decode_in.astype(jnp.float32) + attended).astype(jnp.bfloat16)
    normed_dec = rms_scale(decode_hidden, norm_gain)
    block_count = block_rows.shape[0] * block_rows.shape[1] * block_rows.shape[2]
    all_rows = jnp.concatenate([block_rows.reshape(block_count, feature_width), normed_dec], axis=0)
    all_out = expert_block(all_rows, weights)
    block_out = all_out[:block_count].reshape(block_rows.shape)
    dec_part = all_out[block_count:]
    part_rows, dec_block = axis_share(
        [block_out, dec_part], [True, False], "seq", shards, 1, 4
    )
    summed = jnp.zeros(part_rows.shape[1:], jnp.float32)
    dec_expert = jnp.zeros(dec_block.shape[1:], jnp.float32)
    for part in range(shards):
        summed = summed + part_rows[part].astype(jnp.float32)
        dec_expert = dec_expert + dec_block[part].astype(jnp.float32)
    my_expert = seq_index // shards
    gate_here = jnp.sum(jnp.where(dec_routes == my_expert, dec_gates, 0.0), axis=1)
    returned, dec_all = axis_share(
        [summed, gate_here[:, None] * dec_expert], [True, False], "seq", group_count, shards, 5
    )
    dec_terms = jnp.sum(dec_all, axis=0)
    decode_out = (decode_hidden.astype(jnp.float32) + dec_terms).astype(jnp.bfloat16)
    picked = jnp.take(returned.reshape(EXPERTS * CAP, -1), flat_index, axis=0)
    picked = picked.reshape(-1, TOP, picked.shape[-1])
    prefill_out = (
        prefill_in.astype(jnp.float32) + jnp.sum(gates[..., None] * picked, axis=1)
    ).astype(jnp.bfloat16)
    return (decode_out, prefill_out)


def solution(mesh):
    placed = (
        P(None, "tp"),
        P(None, "tp"),
        P(None, "tp"),
        P(None, "seq", "tp"),
        P(None, "seq", "tp"),
        P(None, "seq"),
        P(),
        P(),
        P("tp", None),
        P(),
        P(("seq", "tp"), None),
        P(("seq", "tp"), None),
        P(("seq", "tp"), None),
        P(),
        P(),
        P(),
        P("tp", "seq"),
        P("tp", "seq"),
        P("seq", "tp"),
    )
    return jax.shard_map(
        body, mesh=mesh, in_specs=placed, out_specs=(P(), P(("seq", "tp"), None)), check_vma=False
    )
```

```python
import functools
import math

import jax
import jax.numpy as jnp
from jax import lax
from jax.experimental import pallas as pl
from jax.experimental.pallas import tpu as pltpu
from jax.sharding import PartitionSpec as P

HD = 64
EXPERTS = 16
TOP = 2
CAP = 10


def peer_device(axis, peer):
    if axis == "seq":
        return (peer, lax.axis_index("tp"))
    return (lax.axis_index("seq"), peer)


def share_kernel(axis, count, stride, modes, *refs):
    width = len(modes)
    sources = refs[:width]
    outputs = refs[width : 2 * width]
    landed = refs[2 * width : 3 * width]
    send_sems = refs[3 * width : 4 * width]
    recv_sems = refs[4 * width :]
    index = lax.axis_index(axis)
    me = lax.rem(index // stride, count)
    base = index - me * stride

    def member(slot):
        return peer_device(axis, base + slot * stride)

    def piece(which, slot):
        return sources[which].at[slot] if modes[which] else sources[which]

    barrier = pltpu.get_barrier_semaphore()

    def greet(step, carry):
        pl.semaphore_signal(
            barrier,
            inc=1,
            device_id=member(lax.rem(me + step, count)),
            device_id_type=pl.DeviceIdType.MESH,
        )
        return carry

    lax.fori_loop(1, count, greet, 0)
    pl.semaphore_wait(barrier, count - 1)

    def outgoing(which, step):
        target = lax.rem(me + step, count)
        return pltpu.make_async_remote_copy(
            src_ref=piece(which, target),
            dst_ref=landed[which].at[me],
            send_sem=send_sems[which].at[step],
            recv_sem=recv_sems[which].at[step],
            device_id=member(target),
            device_id_type=pl.DeviceIdType.MESH,
        )

    def incoming(which, step):
        source = lax.rem(me - step + count, count)
        return pltpu.make_async_remote_copy(
            src_ref=piece(which, source),
            dst_ref=landed[which].at[source],
            send_sem=send_sems[which].at[step],
            recv_sem=recv_sems[which].at[step],
            device_id=member(source),
            device_id_type=pl.DeviceIdType.MESH,
        )

    def launch(step, carry):
        for which in range(width):
            outgoing(which, step).start()
        return carry

    lax.fori_loop(1, count, launch, 0)
    for which in range(width):
        landed[which][me] = piece(which, me)[...]

    def finish(step, carry):
        for which in range(width):
            outgoing(which, step).wait_send()
            incoming(which, step).wait_recv()
        return carry

    lax.fori_loop(1, count, finish, 0)
    for which in range(width):
        outputs[which][...] = landed[which][...]


def axis_share(payloads, modes, axis, count, stride, collective_id):
    shapes = [x.shape if mode else (count,) + x.shape for x, mode in zip(payloads, modes)]
    width = len(payloads)
    return pl.pallas_call(
        functools.partial(share_kernel, axis, count, stride, tuple(modes)),
        out_shape=[jax.ShapeDtypeStruct(s, x.dtype) for s, x in zip(shapes, payloads)],
        in_specs=[pl.BlockSpec(memory_space=pltpu.VMEM)] * width,
        out_specs=[pl.BlockSpec(memory_space=pltpu.VMEM)] * width,
        scratch_shapes=[pltpu.VMEM(s, x.dtype) for s, x in zip(shapes, payloads)]
        + [pltpu.SemaphoreType.DMA((count,))] * (2 * width),
        compiler_params=pltpu.CompilerParams(collective_id=collective_id, has_side_effects=True),
    )(*payloads)


def outbound_kernel(groups, shards, lanes, slab_ref, part_ref, gate_ref, up_ref, down_ref,
                    rows_out, parts_out, gate_out, up_out, down_out,
                    far_parts, near_rows, near_parts, gate_all, up_all, down_all,
                    far_send, far_recv, far_psend, far_precv,
                    near_send, near_recv, near_psend, near_precv, local_sem,
                    lane_send, lane_recv):
    index = lax.axis_index("seq")
    far_me = lax.rem(index // shards, groups)
    far_base = index - far_me * shards
    place = lax.rem(index, shards)
    near_base = index - place
    has_right = place < shards - 1
    has_left = place > 0

    def far_member(slot):
        return peer_device("seq", far_base + slot * shards)

    def near_member(slot):
        return peer_device("seq", near_base + slot)

    barrier = pltpu.get_barrier_semaphore()

    def greet_far(step, carry):
        pl.semaphore_signal(barrier, inc=1, device_id=far_member(lax.rem(far_me + step, groups)),
                            device_id_type=pl.DeviceIdType.MESH)
        return carry

    def greet_near(step, carry):
        pl.semaphore_signal(barrier, inc=1, device_id=near_member(lax.rem(place + step, shards)),
                            device_id_type=pl.DeviceIdType.MESH)
        return carry

    lane_me = lax.axis_index("tp")

    def lane_member(slot):
        return peer_device("tp", slot)

    def greet_lane(step, carry):
        pl.semaphore_signal(barrier, inc=1, device_id=lane_member(lax.rem(lane_me + step, lanes)),
                            device_id_type=pl.DeviceIdType.MESH)
        return carry

    lax.fori_loop(1, groups, greet_far, 0)
    lax.fori_loop(1, shards, greet_near, 0)
    lax.fori_loop(1, lanes, greet_lane, 0)
    pl.semaphore_wait(barrier, groups + shards + lanes - 3)
    weight_refs = ((gate_ref, gate_all), (up_ref, up_all), (down_ref, down_all))

    def lane_copy(which, step, slot, landed_slot):
        source_ref, landed_ref = weight_refs[which]
        return pltpu.make_async_remote_copy(
            src_ref=source_ref, dst_ref=landed_ref.at[landed_slot],
            send_sem=lane_send.at[which, step], recv_sem=lane_recv.at[which, step],
            device_id=lane_member(slot), device_id_type=pl.DeviceIdType.MESH)

    def lane_start(step, carry):
        for which in range(3):
            lane_copy(which, step, lax.rem(lane_me + step, lanes), lane_me).start()
        return carry

    lax.fori_loop(1, lanes, lane_start, 0)
    own_weights = [
        pltpu.make_async_copy(source_ref, landed_ref.at[lane_me], local_sem.at[3 + which])
        for which, (source_ref, landed_ref) in enumerate(weight_refs)
    ]
    for copy in own_weights:
        copy.start()

    def far_copy(step, slot, landed_slot):
        return (
            pltpu.make_async_remote_copy(
                src_ref=slab_ref.at[slot], dst_ref=near_rows.at[place, landed_slot],
                send_sem=far_send.at[step], recv_sem=far_recv.at[step],
                device_id=far_member(slot), device_id_type=pl.DeviceIdType.MESH),
            pltpu.make_async_remote_copy(
                src_ref=part_ref, dst_ref=far_parts.at[landed_slot],
                send_sem=far_psend.at[step], recv_sem=far_precv.at[step],
                device_id=far_member(slot), device_id_type=pl.DeviceIdType.MESH),
        )

    def far_start(step, carry):
        for copy in far_copy(step, lax.rem(far_me + step, groups), far_me):
            copy.start()
        return carry

    lax.fori_loop(1, groups, far_start, 0)
    own_slab = pltpu.make_async_copy(slab_ref.at[far_me], near_rows.at[place, far_me], local_sem.at[0])
    own_part = pltpu.make_async_copy(part_ref, far_parts.at[far_me], local_sem.at[1])
    own_slab.start()
    own_part.start()

    def chain_copy(direction, origin, slab):
        return pltpu.make_async_remote_copy(
            src_ref=near_rows.at[origin, slab], dst_ref=near_rows.at[origin, slab],
            send_sem=near_send.at[direction, origin, slab], recv_sem=near_recv.at[origin, slab],
            device_id=near_member(place + 1 - 2 * direction), device_id_type=pl.DeviceIdType.MESH)

    def pass_on(origin, slab, to_right, to_left):
        @pl.when(to_right)
        def _():
            chain_copy(0, origin, slab).start()

        @pl.when(to_left)
        def _():
            chain_copy(1, origin, slab).start()

    own_slab.wait()
    pass_on(place, far_me, has_right, has_left)

    def far_finish(step, carry):
        source = lax.rem(far_me - step + groups, groups)
        rows_copy, parts_copy = far_copy(step, source, source)
        rows_copy.wait_send()
        rows_copy.wait_recv()
        pass_on(place, source, has_right, has_left)
        parts_copy.wait_send()
        parts_copy.wait_recv()
        return carry

    lax.fori_loop(1, groups, far_finish, 0)
    own_part.wait()
    own_parts = pltpu.make_async_copy(far_parts, near_parts.at[place], local_sem.at[2])
    own_parts.start()

    def near_parts_copy(step, slot):
        return pltpu.make_async_remote_copy(
            src_ref=far_parts, dst_ref=near_parts.at[slot],
            send_sem=near_psend.at[step], recv_sem=near_precv.at[step],
            device_id=near_member(lax.rem(place + step, shards)),
            device_id_type=pl.DeviceIdType.MESH)

    for step in range(1, shards):
        near_parts_copy(step, place).start()

    for distance in range(1, shards):
        def relay(slab, carry, distance=distance):
            from_left = place - distance
            from_right = place + distance

            @pl.when(from_left >= 0)
            def _():
                chain_copy(0, from_left, slab).wait_recv()
                pass_on(from_left, slab, has_right, False)

            @pl.when(from_right < shards)
            def _():
                chain_copy(1, from_right, slab).wait_recv()
                pass_on(from_right, slab, False, has_left)

            return carry

        lax.fori_loop(0, groups, relay, 0)

    for origin in range(shards):
        def drain(slab, carry, origin=origin):
            @pl.when((origin <= place) & has_right)
            def _():
                chain_copy(0, origin, slab).wait_send()

            @pl.when((origin >= place) & has_left)
            def _():
                chain_copy(1, origin, slab).wait_send()

            return carry

        lax.fori_loop(0, groups, drain, 0)

    def parts_finish(step, carry):
        parts_copy = near_parts_copy(step, lax.rem(place - step + shards, shards))
        parts_copy.wait_send()
        parts_copy.wait_recv()
        return carry

    lax.fori_loop(1, shards, parts_finish, 0)
    own_parts.wait()

    def lane_finish(step, carry):
        source = lax.rem(lane_me - step + lanes, lanes)
        for which in range(3):
            copy = lane_copy(which, step, source, source)
            copy.wait_send()
            copy.wait_recv()
        return carry

    lax.fori_loop(1, lanes, lane_finish, 0)
    for copy in own_weights:
        copy.wait()
    rows_out[...] = near_rows[...]
    parts_out[...] = near_parts[...]
    gate_out[...] = gate_all[...]
    up_out[...] = up_all[...]
    down_out[...] = down_all[...]


def outbound(slabs, parts, weights, groups, shards, lanes, collective_id):
    rows_shape = (shards,) + slabs.shape
    parts_shape = (shards, groups) + parts.shape
    weight_shapes = [jax.ShapeDtypeStruct((lanes,) + w.shape, w.dtype) for w in weights]
    return pl.pallas_call(
        functools.partial(outbound_kernel, groups, shards, lanes),
        out_shape=[jax.ShapeDtypeStruct(rows_shape, slabs.dtype),
                   jax.ShapeDtypeStruct(parts_shape, parts.dtype)] + weight_shapes,
        in_specs=[pl.BlockSpec(memory_space=pltpu.VMEM)] * 5,
        out_specs=[pl.BlockSpec(memory_space=pltpu.VMEM)] * 5,
        scratch_shapes=[
            pltpu.VMEM((groups,) + parts.shape, parts.dtype),
            pltpu.VMEM(rows_shape, slabs.dtype),
            pltpu.VMEM(parts_shape, parts.dtype),
        ]
        + [pltpu.VMEM(w.shape, w.dtype) for w in weight_shapes]
        + [pltpu.SemaphoreType.DMA((groups,))] * 4
        + [pltpu.SemaphoreType.DMA((2, shards, groups)), pltpu.SemaphoreType.DMA((shards, groups))]
        + [pltpu.SemaphoreType.DMA((shards,))] * 2
        + [pltpu.SemaphoreType.DMA((8,))]
        + [pltpu.SemaphoreType.DMA((3, lanes))] * 2,
        compiler_params=pltpu.CompilerParams(collective_id=collective_id, has_side_effects=True),
    )(slabs, parts, *weights)


def merge_softmax(stacked, rows, width):
    slot_max = stacked[:, rows, :width]
    slot_sum = stacked[:, rows + 1, :width]
    joint_max = jnp.max(slot_max, axis=0)
    slot_scale = jnp.exp(slot_max - joint_max[None])
    joint_sum = jnp.sum(slot_sum * slot_scale, axis=0)
    lane_scale = jnp.repeat(slot_scale.reshape(slot_scale.shape[0], rows, -1), HD, axis=2)
    joint_acc = jnp.sum(stacked[:, :rows, :] * lane_scale, axis=0)
    return joint_max, joint_sum, joint_acc


def pack_softmax(joint_max, joint_sum, joint_acc):
    rows, lanes = joint_acc.shape
    stats = jnp.stack([joint_max, joint_sum])
    return jnp.concatenate([joint_acc, jnp.pad(stats, ((0, 2), (0, lanes - stats.shape[1])))], axis=0)


def rms_scale(hidden, norm_gain):
    values = hidden.astype(jnp.float32)
    meansq = jnp.mean(values * values, axis=-1, keepdims=True)
    return (values * lax.rsqrt(meansq + 1e-06) * norm_gain).astype(jnp.bfloat16)


def route_slots(route_rows, capacity):
    flat_routes = route_rows.reshape(-1)
    onehot = (flat_routes[:, None] == jnp.arange(EXPERTS, dtype=jnp.int32)[None, :]).astype(
        jnp.int32
    )
    earlier = jnp.cumsum(onehot, axis=0) - onehot
    slot_rank = jnp.sum(earlier * onehot, axis=1)
    return flat_routes * capacity + slot_rank


def expert_block(row_block, weights):
    gate_full, up_full, down_full = weights
    gate_pre = jnp.dot(row_block, gate_full, preferred_element_type=jnp.float32)
    up_pre = jnp.dot(row_block, up_full, preferred_element_type=jnp.float32)
    act = (jax.nn.gelu(gate_pre, approximate=True) * up_pre).astype(jnp.bfloat16)
    return jnp.dot(act, down_full, preferred_element_type=jnp.float32).astype(jnp.bfloat16)


def body(
    queries,
    keys_new,
    values_new,
    key_cache,
    value_cache,
    buckets,
    lengths,
    bias_table,
    out_proj,
    decode_in,
    prefill_in,
    routes,
    gates,
    dec_routes,
    dec_gates,
    norm_gain,
    w_gate,
    w_up,
    w_down,
):
    seq_count = lax.axis_size("seq")
    seq_index = lax.axis_index("seq")
    tp_index = lax.axis_index("tp")
    shards = seq_count // EXPERTS
    normed_pre = rms_scale(prefill_in, norm_gain)
    request_count, heads_width = queries.shape
    heads_here = heads_width // HD
    ctx_local = key_cache.shape[1]
    score_scale = 1.0 / math.sqrt(HD)
    query_rows = queries.reshape(request_count, heads_here, HD)
    key_rows = key_cache.reshape(request_count, ctx_local, heads_here, HD)
    value_rows = value_cache.reshape(request_count, ctx_local, heads_here, HD).astype(jnp.float32)
    bias_here = lax.dynamic_slice_in_dim(bias_table, tp_index * heads_here, heads_here, 1)
    bucket_hot = (
        buckets[..., None] == jnp.arange(bias_table.shape[0], dtype=jnp.int32)[None, None, :]
    ).astype(jnp.float32)
    bias_rows = jnp.einsum("rcn,nh->rhc", bucket_hot, bias_here, precision=lax.Precision.HIGHEST)
    cache_scores = (
        jnp.einsum("rhd,rchd->rhc", query_rows, key_rows, preferred_element_type=jnp.float32)
        * score_scale
        + bias_rows
    )
    positions = seq_index * ctx_local + jnp.arange(ctx_local, dtype=jnp.int32)
    valid_mask = (positions[None, :] < lengths[:, None])[:, None, :]
    cache_scores = jnp.where(valid_mask, cache_scores, -1e30)
    local_max = jnp.max(cache_scores, axis=-1)
    local_weights = jnp.where(valid_mask, jnp.exp(cache_scores - local_max[..., None]), 0.0)
    local_sum = jnp.sum(local_weights, axis=-1)
    local_acc = jnp.einsum(
        "rhc,rchd->rhd", local_weights, value_rows, precision=lax.Precision.HIGHEST
    )
    tp_count = lax.axis_size("tp")
    flat_width = request_count * heads_here
    packed_parts = pack_softmax(
        local_max.reshape(-1), local_sum.reshape(-1), local_acc.reshape(request_count, heads_here * HD)
    )
    flat_index = route_slots(routes, CAP)
    feature_width = normed_pre.shape[1]
    slot_expert = flat_index // CAP
    slot_rank = flat_index % CAP
    slabs = (
        jnp.zeros((EXPERTS, CAP, feature_width), jnp.bfloat16)
        .at[slot_expert, slot_rank]
        .set(jnp.repeat(normed_pre, TOP, axis=0))
    )
    group_count = seq_count // shards
    block_rows, block_parts, gate_all, up_all, down_all = outbound(
        slabs, packed_parts, (w_gate, w_up, w_down), group_count, shards, tp_count, 1
    )
    weights = (
        gate_all.reshape(-1, gate_all.shape[-1]),
        up_all.reshape(-1, up_all.shape[-1]),
        jnp.transpose(down_all, (1, 0, 2)).reshape(down_all.shape[1], -1),
    )
    stage = merge_softmax(
        block_parts.reshape((-1,) + packed_parts.shape), request_count, flat_width
    )
    part_max = stage[0].reshape(request_count, heads_here)
    part_sum = stage[1].reshape(request_count, heads_here)
    part_acc = stage[2].reshape(request_count, heads_here, HD)
    own_key = keys_new.reshape(request_count, heads_here, HD).astype(jnp.float32)
    own_value = values_new.reshape(request_count, heads_here, HD).astype(jnp.float32)
    own_score = (
        jnp.sum(query_rows.astype(jnp.float32) * own_key, axis=-1) * score_scale
        + bias_here[0][None, :]
    )
    row_peak = jnp.maximum(part_max, own_score)
    keep_scale = jnp.exp(part_max - row_peak)
    own_weight = jnp.exp(own_score - row_peak)
    weight_total = part_sum * keep_scale + own_weight
    weighted = part_acc * keep_scale[..., None] + own_weight[..., None] * own_value
    mixed_rows = (
        (weighted / weight_total[..., None])
        .astype(jnp.bfloat16)
        .reshape(request_count, heads_width)
    )
    head_terms = jnp.dot(mixed_rows, out_proj, preferred_element_type=jnp.float32)
    (head_all,) = axis_share([head_terms], [False], "tp", tp_count, 1, 3)
    attended = jnp.sum(head_all, axis=0)
    decode_hidden = (decode_in.astype(jnp.float32) + attended).astype(jnp.bfloat16)
    normed_dec = rms_scale(decode_hidden, norm_gain)
    block_count = block_rows.shape[0] * block_rows.shape[1] * block_rows.shape[2]
    all_rows = jnp.concatenate([block_rows.reshape(block_count, feature_width), normed_dec], axis=0)
    all_out = expert_block(all_rows, weights)
    block_out = all_out[:block_count].reshape(block_rows.shape)
    dec_part = all_out[block_count:]
    part_rows, dec_block = axis_share(
        [block_out, dec_part], [True, False], "seq", shards, 1, 4
    )
    summed = jnp.zeros(part_rows.shape[1:], jnp.float32)
    dec_expert = jnp.zeros(dec_block.shape[1:], jnp.float32)
    for part in range(shards):
        summed = summed + part_rows[part].astype(jnp.float32)
        dec_expert = dec_expert + dec_block[part].astype(jnp.float32)
    my_expert = seq_index // shards
    gate_here = jnp.sum(jnp.where(dec_routes == my_expert, dec_gates, 0.0), axis=1)
    returned, dec_all = axis_share(
        [summed, gate_here[:, None] * dec_expert], [True, False], "seq", group_count, shards, 5
    )
    dec_terms = jnp.sum(dec_all, axis=0)
    decode_out = (decode_hidden.astype(jnp.float32) + dec_terms).astype(jnp.bfloat16)
    picked = returned[slot_expert, slot_rank].reshape(-1, TOP, returned.shape[-1])
    prefill_out = (
        prefill_in.astype(jnp.float32) + jnp.sum(gates[..., None] * picked, axis=1)
    ).astype(jnp.bfloat16)
    return (decode_out, prefill_out)


def solution(mesh):
    placed = (
        P(None, "tp"),
        P(None, "tp"),
        P(None, "tp"),
        P(None, "seq", "tp"),
        P(None, "seq", "tp"),
        P(None, "seq"),
        P(),
        P(),
        P("tp", None),
        P(),
        P(("seq", "tp"), None),
        P(("seq", "tp"), None),
        P(("seq", "tp"), None),
        P(),
        P(),
        P(),
        P("tp", "seq"),
        P("tp", "seq"),
        P("seq", "tp"),
    )
    return jax.shard_map(
        body, mesh=mesh, in_specs=placed, out_specs=(P(), P(("seq", "tp"), None)), check_vma=False
    )
```

```python
import functools
import math

import jax
import jax.numpy as jnp
from jax import lax
from jax.experimental import pallas as pl
from jax.experimental.pallas import tpu as pltpu
from jax.sharding import PartitionSpec as P

HD = 64
EXPERTS = 16
TOP = 2
CAP = 10


def peer_device(axis, peer):
    if axis == "seq":
        return (peer, lax.axis_index("tp"))
    return (lax.axis_index("seq"), peer)


def share_kernel(axis, count, stride, modes, *refs):
    width = len(modes)
    sources = refs[:width]
    landed = refs[width : 2 * width]
    send_sems = refs[2 * width : 3 * width]
    recv_sems = refs[3 * width :]
    index = lax.axis_index(axis)
    me = lax.rem(index // stride, count)
    base = index - me * stride

    def member(slot):
        return peer_device(axis, base + slot * stride)

    def piece(which, slot):
        return sources[which].at[slot] if modes[which] else sources[which]

    barrier = pltpu.get_barrier_semaphore()

    def greet(step, carry):
        pl.semaphore_signal(
            barrier,
            inc=1,
            device_id=member(lax.rem(me + step, count)),
            device_id_type=pl.DeviceIdType.MESH,
        )
        return carry

    lax.fori_loop(1, count, greet, 0)
    pl.semaphore_wait(barrier, count - 1)

    def outgoing(which, step):
        target = lax.rem(me + step, count)
        return pltpu.make_async_remote_copy(
            src_ref=piece(which, target),
            dst_ref=landed[which].at[me],
            send_sem=send_sems[which].at[step],
            recv_sem=recv_sems[which].at[step],
            device_id=member(target),
            device_id_type=pl.DeviceIdType.MESH,
        )

    def incoming(which, step):
        source = lax.rem(me - step + count, count)
        return pltpu.make_async_remote_copy(
            src_ref=piece(which, source),
            dst_ref=landed[which].at[source],
            send_sem=send_sems[which].at[step],
            recv_sem=recv_sems[which].at[step],
            device_id=member(source),
            device_id_type=pl.DeviceIdType.MESH,
        )

    def launch(step, carry):
        for which in range(width):
            outgoing(which, step).start()
        return carry

    lax.fori_loop(1, count, launch, 0)
    for which in range(width):
        landed[which][me] = piece(which, me)[...]

    def finish(step, carry):
        for which in range(width):
            outgoing(which, step).wait_send()
            incoming(which, step).wait_recv()
        return carry

    lax.fori_loop(1, count, finish, 0)


def axis_share(payloads, modes, axis, count, stride, collective_id):
    shapes = [x.shape if mode else (count,) + x.shape for x, mode in zip(payloads, modes)]
    width = len(payloads)
    return pl.pallas_call(
        functools.partial(share_kernel, axis, count, stride, tuple(modes)),
        out_shape=[jax.ShapeDtypeStruct(s, x.dtype) for s, x in zip(shapes, payloads)],
        in_specs=[pl.BlockSpec(memory_space=pltpu.VMEM)] * width,
        out_specs=[pl.BlockSpec(memory_space=pltpu.VMEM)] * width,
        scratch_shapes=[pltpu.SemaphoreType.DMA((count,))] * (2 * width),
        compiler_params=pltpu.CompilerParams(collective_id=collective_id, has_side_effects=True),
    )(*payloads)


def outbound_kernel(groups, shards, lanes, slab_ref, part_ref, gate_ref, up_ref, down_ref,
                    near_rows, near_parts, gate_all, up_all, down_all, far_parts,
                    far_send, far_recv, far_psend, far_precv,
                    near_send, near_recv, near_psend, near_precv, local_sem,
                    lane_send, lane_recv):
    index = lax.axis_index("seq")
    far_me = lax.rem(index // shards, groups)
    far_base = index - far_me * shards
    place = lax.rem(index, shards)
    near_base = index - place
    has_right = place < shards - 1
    has_left = place > 0

    def far_member(slot):
        return peer_device("seq", far_base + slot * shards)

    def near_member(slot):
        return peer_device("seq", near_base + slot)

    barrier = pltpu.get_barrier_semaphore()

    def greet_far(step, carry):
        pl.semaphore_signal(barrier, inc=1, device_id=far_member(lax.rem(far_me + step, groups)),
                            device_id_type=pl.DeviceIdType.MESH)
        return carry

    def greet_near(step, carry):
        pl.semaphore_signal(barrier, inc=1, device_id=near_member(lax.rem(place + step, shards)),
                            device_id_type=pl.DeviceIdType.MESH)
        return carry

    lane_me = lax.axis_index("tp")

    def lane_member(slot):
        return peer_device("tp", slot)

    def greet_lane(step, carry):
        pl.semaphore_signal(barrier, inc=1, device_id=lane_member(lax.rem(lane_me + step, lanes)),
                            device_id_type=pl.DeviceIdType.MESH)
        return carry

    lax.fori_loop(1, groups, greet_far, 0)
    lax.fori_loop(1, shards, greet_near, 0)
    lax.fori_loop(1, lanes, greet_lane, 0)
    pl.semaphore_wait(barrier, groups + shards + lanes - 3)
    weight_refs = ((gate_ref, gate_all), (up_ref, up_all), (down_ref, down_all))

    def lane_copy(which, step, slot, landed_slot):
        source_ref, landed_ref = weight_refs[which]
        return pltpu.make_async_remote_copy(
            src_ref=source_ref, dst_ref=landed_ref.at[landed_slot],
            send_sem=lane_send.at[which, step], recv_sem=lane_recv.at[which, step],
            device_id=lane_member(slot), device_id_type=pl.DeviceIdType.MESH)

    def lane_start(step, carry):
        for which in range(3):
            lane_copy(which, step, lax.rem(lane_me + step, lanes), lane_me).start()
        return carry

    lax.fori_loop(1, lanes, lane_start, 0)
    own_weights = [
        pltpu.make_async_copy(source_ref, landed_ref.at[lane_me], local_sem.at[3 + which])
        for which, (source_ref, landed_ref) in enumerate(weight_refs)
    ]
    for copy in own_weights:
        copy.start()

    def far_copy(step, slot, landed_slot):
        return (
            pltpu.make_async_remote_copy(
                src_ref=slab_ref.at[slot], dst_ref=near_rows.at[place, landed_slot],
                send_sem=far_send.at[step], recv_sem=far_recv.at[step],
                device_id=far_member(slot), device_id_type=pl.DeviceIdType.MESH),
            pltpu.make_async_remote_copy(
                src_ref=part_ref, dst_ref=far_parts.at[landed_slot],
                send_sem=far_psend.at[step], recv_sem=far_precv.at[step],
                device_id=far_member(slot), device_id_type=pl.DeviceIdType.MESH),
        )

    def far_start(step, carry):
        for copy in far_copy(step, lax.rem(far_me + step, groups), far_me):
            copy.start()
        return carry

    lax.fori_loop(1, groups, far_start, 0)
    own_slab = pltpu.make_async_copy(slab_ref.at[far_me], near_rows.at[place, far_me], local_sem.at[0])
    own_part = pltpu.make_async_copy(part_ref, far_parts.at[far_me], local_sem.at[1])
    own_slab.start()
    own_part.start()

    def chain_copy(direction, origin, slab):
        return pltpu.make_async_remote_copy(
            src_ref=near_rows.at[origin, slab], dst_ref=near_rows.at[origin, slab],
            send_sem=near_send.at[direction, origin, slab], recv_sem=near_recv.at[origin, slab],
            device_id=near_member(place + 1 - 2 * direction), device_id_type=pl.DeviceIdType.MESH)

    def pass_on(origin, slab, to_right, to_left):
        @pl.when(to_right)
        def _():
            chain_copy(0, origin, slab).start()

        @pl.when(to_left)
        def _():
            chain_copy(1, origin, slab).start()

    own_slab.wait()
    pass_on(place, far_me, has_right, has_left)

    def far_finish(step, carry):
        source = lax.rem(far_me - step + groups, groups)
        rows_copy, parts_copy = far_copy(step, source, source)
        rows_copy.wait_send()
        rows_copy.wait_recv()
        pass_on(place, source, has_right, has_left)
        parts_copy.wait_send()
        parts_copy.wait_recv()
        return carry

    lax.fori_loop(1, groups, far_finish, 0)
    own_part.wait()
    own_parts = pltpu.make_async_copy(far_parts, near_parts.at[place], local_sem.at[2])
    own_parts.start()

    def near_parts_copy(step, slot):
        return pltpu.make_async_remote_copy(
            src_ref=far_parts, dst_ref=near_parts.at[slot],
            send_sem=near_psend.at[step], recv_sem=near_precv.at[step],
            device_id=near_member(lax.rem(place + step, shards)),
            device_id_type=pl.DeviceIdType.MESH)

    for step in range(1, shards):
        near_parts_copy(step, place).start()

    for distance in range(1, shards):
        def relay(slab, carry, distance=distance):
            from_left = place - distance
            from_right = place + distance

            @pl.when(from_left >= 0)
            def _():
                chain_copy(0, from_left, slab).wait_recv()
                pass_on(from_left, slab, has_right, False)

            @pl.when(from_right < shards)
            def _():
                chain_copy(1, from_right, slab).wait_recv()
                pass_on(from_right, slab, False, has_left)

            return carry

        lax.fori_loop(0, groups, relay, 0)

    for origin in range(shards):
        def drain(slab, carry, origin=origin):
            @pl.when((origin <= place) & has_right)
            def _():
                chain_copy(0, origin, slab).wait_send()

            @pl.when((origin >= place) & has_left)
            def _():
                chain_copy(1, origin, slab).wait_send()

            return carry

        lax.fori_loop(0, groups, drain, 0)

    def parts_finish(step, carry):
        parts_copy = near_parts_copy(step, lax.rem(place - step + shards, shards))
        parts_copy.wait_send()
        parts_copy.wait_recv()
        return carry

    lax.fori_loop(1, shards, parts_finish, 0)
    own_parts.wait()

    def lane_finish(step, carry):
        source = lax.rem(lane_me - step + lanes, lanes)
        for which in range(3):
            copy = lane_copy(which, step, source, source)
            copy.wait_send()
            copy.wait_recv()
        return carry

    lax.fori_loop(1, lanes, lane_finish, 0)
    for copy in own_weights:
        copy.wait()


def outbound(slabs, parts, weights, groups, shards, lanes, collective_id):
    rows_shape = (shards,) + slabs.shape
    parts_shape = (shards, groups) + parts.shape
    weight_shapes = [jax.ShapeDtypeStruct((lanes,) + w.shape, w.dtype) for w in weights]
    return pl.pallas_call(
        functools.partial(outbound_kernel, groups, shards, lanes),
        out_shape=[jax.ShapeDtypeStruct(rows_shape, slabs.dtype),
                   jax.ShapeDtypeStruct(parts_shape, parts.dtype)] + weight_shapes,
        in_specs=[pl.BlockSpec(memory_space=pltpu.VMEM)] * 5,
        out_specs=[pl.BlockSpec(memory_space=pltpu.VMEM)] * 5,
        scratch_shapes=[pltpu.VMEM((groups,) + parts.shape, parts.dtype)]
        + [pltpu.SemaphoreType.DMA((groups,))] * 4
        + [pltpu.SemaphoreType.DMA((2, shards, groups)), pltpu.SemaphoreType.DMA((shards, groups))]
        + [pltpu.SemaphoreType.DMA((shards,))] * 2
        + [pltpu.SemaphoreType.DMA((8,))]
        + [pltpu.SemaphoreType.DMA((3, lanes))] * 2,
        compiler_params=pltpu.CompilerParams(collective_id=collective_id, has_side_effects=True),
    )(slabs, parts, *weights)


def merge_softmax(stacked, rows, width):
    slot_max = stacked[:, rows, :width]
    slot_sum = stacked[:, rows + 1, :width]
    joint_max = jnp.max(slot_max, axis=0)
    slot_scale = jnp.exp(slot_max - joint_max[None])
    joint_sum = jnp.sum(slot_sum * slot_scale, axis=0)
    lane_scale = jnp.repeat(slot_scale.reshape(slot_scale.shape[0], rows, -1), HD, axis=2)
    joint_acc = jnp.sum(stacked[:, :rows, :] * lane_scale, axis=0)
    return joint_max, joint_sum, joint_acc


def pack_softmax(joint_max, joint_sum, joint_acc):
    rows, lanes = joint_acc.shape
    stats = jnp.stack([joint_max, joint_sum])
    return jnp.concatenate([joint_acc, jnp.pad(stats, ((0, 2), (0, lanes - stats.shape[1])))], axis=0)


def rms_scale(hidden, norm_gain):
    values = hidden.astype(jnp.float32)
    meansq = jnp.mean(values * values, axis=-1, keepdims=True)
    return (values * lax.rsqrt(meansq + 1e-06) * norm_gain).astype(jnp.bfloat16)


def route_slots(route_rows, capacity):
    flat_routes = route_rows.reshape(-1)
    onehot = (flat_routes[:, None] == jnp.arange(EXPERTS, dtype=jnp.int32)[None, :]).astype(
        jnp.int32
    )
    earlier = jnp.cumsum(onehot, axis=0) - onehot
    slot_rank = jnp.sum(earlier * onehot, axis=1)
    return flat_routes * capacity + slot_rank


def expert_block(row_block, weights):
    gate_full, up_full, down_full = weights
    gate_pre = jnp.dot(row_block, gate_full, preferred_element_type=jnp.float32)
    up_pre = jnp.dot(row_block, up_full, preferred_element_type=jnp.float32)
    act = (jax.nn.gelu(gate_pre, approximate=True) * up_pre).astype(jnp.bfloat16)
    return jnp.dot(act, down_full, preferred_element_type=jnp.float32).astype(jnp.bfloat16)


def body(
    queries,
    keys_new,
    values_new,
    key_cache,
    value_cache,
    buckets,
    lengths,
    bias_table,
    out_proj,
    decode_in,
    prefill_in,
    routes,
    gates,
    dec_routes,
    dec_gates,
    norm_gain,
    w_gate,
    w_up,
    w_down,
):
    seq_count = lax.axis_size("seq")
    seq_index = lax.axis_index("seq")
    tp_index = lax.axis_index("tp")
    shards = seq_count // EXPERTS
    normed_pre = rms_scale(prefill_in, norm_gain)
    request_count, heads_width = queries.shape
    heads_here = heads_width // HD
    ctx_local = key_cache.shape[1]
    score_scale = 1.0 / math.sqrt(HD)
    query_rows = queries.reshape(request_count, heads_here, HD)
    key_rows = key_cache.reshape(request_count, ctx_local, heads_here, HD)
    value_rows = value_cache.reshape(request_count, ctx_local, heads_here, HD).astype(jnp.float32)
    bias_here = lax.dynamic_slice_in_dim(bias_table, tp_index * heads_here, heads_here, 1)
    bucket_hot = (
        buckets[..., None] == jnp.arange(bias_table.shape[0], dtype=jnp.int32)[None, None, :]
    ).astype(jnp.float32)
    bias_rows = jnp.einsum("rcn,nh->rhc", bucket_hot, bias_here, precision=lax.Precision.HIGHEST)
    cache_scores = (
        jnp.einsum("rhd,rchd->rhc", query_rows, key_rows, preferred_element_type=jnp.float32)
        * score_scale
        + bias_rows
    )
    positions = seq_index * ctx_local + jnp.arange(ctx_local, dtype=jnp.int32)
    valid_mask = (positions[None, :] < lengths[:, None])[:, None, :]
    cache_scores = jnp.where(valid_mask, cache_scores, -1e30)
    local_max = jnp.max(cache_scores, axis=-1)
    local_weights = jnp.where(valid_mask, jnp.exp(cache_scores - local_max[..., None]), 0.0)
    local_sum = jnp.sum(local_weights, axis=-1)
    local_acc = jnp.einsum(
        "rhc,rchd->rhd", local_weights, value_rows, precision=lax.Precision.HIGHEST
    )
    tp_count = lax.axis_size("tp")
    flat_width = request_count * heads_here
    packed_parts = pack_softmax(
        local_max.reshape(-1), local_sum.reshape(-1), local_acc.reshape(request_count, heads_here * HD)
    )
    flat_index = route_slots(routes, CAP)
    feature_width = normed_pre.shape[1]
    slabs = (
        jnp.zeros((EXPERTS * CAP, feature_width), jnp.bfloat16)
        .at[flat_index]
        .set(jnp.repeat(normed_pre, TOP, axis=0))
        .reshape(EXPERTS, CAP, feature_width)
    )
    group_count = seq_count // shards
    block_rows, block_parts, gate_all, up_all, down_all = outbound(
        slabs, packed_parts, (w_gate, w_up, w_down), group_count, shards, tp_count, 1
    )
    weights = (
        gate_all.reshape(-1, gate_all.shape[-1]),
        up_all.reshape(-1, up_all.shape[-1]),
        jnp.transpose(down_all, (1, 0, 2)).reshape(down_all.shape[1], -1),
    )
    stage = merge_softmax(
        block_parts.reshape((-1,) + packed_parts.shape), request_count, flat_width
    )
    part_max = stage[0].reshape(request_count, heads_here)
    part_sum = stage[1].reshape(request_count, heads_here)
    part_acc = stage[2].reshape(request_count, heads_here, HD)
    own_key = keys_new.reshape(request_count, heads_here, HD).astype(jnp.float32)
    own_value = values_new.reshape(request_count, heads_here, HD).astype(jnp.float32)
    own_score = (
        jnp.sum(query_rows.astype(jnp.float32) * own_key, axis=-1) * score_scale
        + bias_here[0][None, :]
    )
    row_peak = jnp.maximum(part_max, own_score)
    keep_scale = jnp.exp(part_max - row_peak)
    own_weight = jnp.exp(own_score - row_peak)
    weight_total = part_sum * keep_scale + own_weight
    weighted = part_acc * keep_scale[..., None] + own_weight[..., None] * own_value
    mixed_rows = (
        (weighted / weight_total[..., None])
        .astype(jnp.bfloat16)
        .reshape(request_count, heads_width)
    )
    head_terms = jnp.dot(mixed_rows, out_proj, preferred_element_type=jnp.float32)
    (head_all,) = axis_share([head_terms], [False], "tp", tp_count, 1, 3)
    attended = jnp.sum(head_all, axis=0)
    decode_hidden = (decode_in.astype(jnp.float32) + attended).astype(jnp.bfloat16)
    normed_dec = rms_scale(decode_hidden, norm_gain)
    block_count = block_rows.shape[0] * block_rows.shape[1] * block_rows.shape[2]
    all_rows = jnp.concatenate([block_rows.reshape(block_count, feature_width), normed_dec], axis=0)
    all_out = expert_block(all_rows, weights)
    block_out = all_out[:block_count].reshape(block_rows.shape)
    dec_part = all_out[block_count:]
    part_rows, dec_block = axis_share(
        [block_out, dec_part], [True, False], "seq", shards, 1, 4
    )
    summed = jnp.zeros(part_rows.shape[1:], jnp.float32)
    dec_expert = jnp.zeros(dec_block.shape[1:], jnp.float32)
    for part in range(shards):
        summed = summed + part_rows[part].astype(jnp.float32)
        dec_expert = dec_expert + dec_block[part].astype(jnp.float32)
    my_expert = seq_index // shards
    gate_here = jnp.sum(jnp.where(dec_routes == my_expert, dec_gates, 0.0), axis=1)
    returned, dec_all = axis_share(
        [summed, gate_here[:, None] * dec_expert], [True, False], "seq", group_count, shards, 5
    )
    dec_terms = jnp.sum(dec_all, axis=0)
    decode_out = (decode_hidden.astype(jnp.float32) + dec_terms).astype(jnp.bfloat16)
    picked = jnp.take(returned.reshape(EXPERTS * CAP, -1), flat_index, axis=0)
    picked = picked.reshape(-1, TOP, picked.shape[-1])
    prefill_out = (
        prefill_in.astype(jnp.float32) + jnp.sum(gates[..., None] * picked, axis=1)
    ).astype(jnp.bfloat16)
    return (decode_out, prefill_out)


def solution(mesh):
    placed = (
        P(None, "tp"),
        P(None, "tp"),
        P(None, "tp"),
        P(None, "seq", "tp"),
        P(None, "seq", "tp"),
        P(None, "seq"),
        P(),
        P(),
        P("tp", None),
        P(),
        P(("seq", "tp"), None),
        P(("seq", "tp"), None),
        P(("seq", "tp"), None),
        P(),
        P(),
        P(),
        P("tp", "seq"),
        P("tp", "seq"),
        P("seq", "tp"),
    )
    return jax.shard_map(
        body, mesh=mesh, in_specs=placed, out_specs=(P(), P(("seq", "tp"), None)), check_vma=False
    )
```

```python
import functools
import math

import jax
import jax.numpy as jnp
from jax import lax
from jax.experimental import pallas as pl
from jax.experimental.pallas import tpu as pltpu
from jax.sharding import PartitionSpec as P

HD = 64
EXPERTS = 16
TOP = 2
CAP = 10


def far_seq(index, slot, shards):
    blocks = 16 // shards
    place = index % shards
    rel = (slot % blocks - (index // shards) % blocks + blocks) % blocks
    opposite = (rel // (blocks // 2)) * (1 - rel % 2)
    return slot * shards + (place + opposite * (shards // 2)) % shards


def peer_device(axis, peer):
    if axis == "seq":
        return (peer, lax.axis_index("tp"))
    return (lax.axis_index("seq"), peer)


def share_kernel(axis, count, stride, twisted, modes, *refs):
    width = len(modes)
    sources = refs[:width]
    landed = refs[width : 2 * width]
    send_sems = refs[2 * width : 3 * width]
    recv_sems = refs[3 * width :]
    index = lax.axis_index(axis)
    me = lax.rem(index // stride, count)
    base = index - me * stride

    def member(slot):
        if twisted:
            return peer_device(axis, far_seq(index, slot, stride))
        return peer_device(axis, base + slot * stride)

    def piece(which, slot):
        return sources[which].at[slot] if modes[which] else sources[which]

    barrier = pltpu.get_barrier_semaphore()

    def greet(step, carry):
        pl.semaphore_signal(
            barrier,
            inc=1,
            device_id=member(lax.rem(me + step, count)),
            device_id_type=pl.DeviceIdType.MESH,
        )
        return carry

    lax.fori_loop(1, count, greet, 0)
    pl.semaphore_wait(barrier, count - 1)

    def outgoing(which, step):
        target = lax.rem(me + step, count)
        return pltpu.make_async_remote_copy(
            src_ref=piece(which, target),
            dst_ref=landed[which].at[me],
            send_sem=send_sems[which].at[step],
            recv_sem=recv_sems[which].at[step],
            device_id=member(target),
            device_id_type=pl.DeviceIdType.MESH,
        )

    def incoming(which, step):
        source = lax.rem(me - step + count, count)
        return pltpu.make_async_remote_copy(
            src_ref=piece(which, source),
            dst_ref=landed[which].at[source],
            send_sem=send_sems[which].at[step],
            recv_sem=recv_sems[which].at[step],
            device_id=member(source),
            device_id_type=pl.DeviceIdType.MESH,
        )

    def launch(step, carry):
        for which in range(width):
            outgoing(which, step).start()
        return carry

    lax.fori_loop(1, count, launch, 0)
    for which in range(width):
        landed[which][me] = piece(which, me)[...]

    def finish(step, carry):
        for which in range(width):
            outgoing(which, step).wait_send()
            incoming(which, step).wait_recv()
        return carry

    lax.fori_loop(1, count, finish, 0)


def axis_share(payloads, modes, axis, count, stride, collective_id, twisted=False):
    shapes = [x.shape if mode else (count,) + x.shape for x, mode in zip(payloads, modes)]
    width = len(payloads)
    return pl.pallas_call(
        functools.partial(share_kernel, axis, count, stride, twisted, tuple(modes)),
        out_shape=[jax.ShapeDtypeStruct(s, x.dtype) for s, x in zip(shapes, payloads)],
        in_specs=[pl.BlockSpec(memory_space=pltpu.VMEM)] * width,
        out_specs=[pl.BlockSpec(memory_space=pltpu.VMEM)] * width,
        scratch_shapes=[pltpu.SemaphoreType.DMA((count,))] * (2 * width),
        compiler_params=pltpu.CompilerParams(collective_id=collective_id, has_side_effects=True),
    )(*payloads)


def outbound_kernel(groups, shards, lanes, slab_ref, part_ref, gate_ref, up_ref, down_ref,
                    near_rows, near_parts, gate_all, up_all, down_all, far_parts,
                    far_send, far_recv, far_psend, far_precv,
                    near_send, near_recv, near_psend, near_precv, local_sem,
                    lane_send, lane_recv):
    index = lax.axis_index("seq")
    far_me = lax.rem(index // shards, groups)
    far_base = index - far_me * shards
    place = lax.rem(index, shards)
    near_base = index - place
    has_right = place < shards - 1
    has_left = place > 0

    def far_member(slot):
        return peer_device("seq", far_seq(index, slot, shards))

    def near_member(slot):
        return peer_device("seq", near_base + slot)

    barrier = pltpu.get_barrier_semaphore()

    def greet_far(step, carry):
        pl.semaphore_signal(barrier, inc=1, device_id=far_member(lax.rem(far_me + step, groups)),
                            device_id_type=pl.DeviceIdType.MESH)
        return carry

    def greet_near(step, carry):
        pl.semaphore_signal(barrier, inc=1, device_id=near_member(lax.rem(place + step, shards)),
                            device_id_type=pl.DeviceIdType.MESH)
        return carry

    lane_me = lax.axis_index("tp")

    def lane_member(slot):
        return peer_device("tp", slot)

    def greet_lane(step, carry):
        pl.semaphore_signal(barrier, inc=1, device_id=lane_member(lax.rem(lane_me + step, lanes)),
                            device_id_type=pl.DeviceIdType.MESH)
        return carry

    lax.fori_loop(1, groups, greet_far, 0)
    lax.fori_loop(1, shards, greet_near, 0)
    lax.fori_loop(1, lanes, greet_lane, 0)
    pl.semaphore_wait(barrier, groups + shards + lanes - 3)
    weight_refs = ((gate_ref, gate_all), (up_ref, up_all), (down_ref, down_all))

    def lane_copy(which, step, slot, landed_slot):
        source_ref, landed_ref = weight_refs[which]
        return pltpu.make_async_remote_copy(
            src_ref=source_ref, dst_ref=landed_ref.at[landed_slot],
            send_sem=lane_send.at[which, step], recv_sem=lane_recv.at[which, step],
            device_id=lane_member(slot), device_id_type=pl.DeviceIdType.MESH)

    def lane_start(step, carry):
        for which in range(3):
            lane_copy(which, step, lax.rem(lane_me + step, lanes), lane_me).start()
        return carry

    lax.fori_loop(1, lanes, lane_start, 0)
    own_weights = [
        pltpu.make_async_copy(source_ref, landed_ref.at[lane_me], local_sem.at[3 + which])
        for which, (source_ref, landed_ref) in enumerate(weight_refs)
    ]
    for copy in own_weights:
        copy.start()

    def far_copy(step, slot, landed_slot):
        return (
            pltpu.make_async_remote_copy(
                src_ref=slab_ref.at[slot],
                dst_ref=near_rows.at[far_seq(index, slot, shards) % shards, landed_slot],
                send_sem=far_send.at[step], recv_sem=far_recv.at[step],
                device_id=far_member(slot), device_id_type=pl.DeviceIdType.MESH),
            pltpu.make_async_remote_copy(
                src_ref=part_ref, dst_ref=far_parts.at[landed_slot],
                send_sem=far_psend.at[step], recv_sem=far_precv.at[step],
                device_id=far_member(slot), device_id_type=pl.DeviceIdType.MESH),
        )

    def far_start(step, carry):
        for copy in far_copy(step, lax.rem(far_me + step, groups), far_me):
            copy.start()
        return carry

    lax.fori_loop(1, groups, far_start, 0)
    own_slab = pltpu.make_async_copy(slab_ref.at[far_me], near_rows.at[place, far_me], local_sem.at[0])
    own_part = pltpu.make_async_copy(part_ref, far_parts.at[far_me], local_sem.at[1])
    own_slab.start()
    own_part.start()

    def chain_copy(direction, origin, slab):
        return pltpu.make_async_remote_copy(
            src_ref=near_rows.at[origin, slab], dst_ref=near_rows.at[origin, slab],
            send_sem=near_send.at[direction, origin, slab], recv_sem=near_recv.at[origin, slab],
            device_id=near_member(place + 1 - 2 * direction), device_id_type=pl.DeviceIdType.MESH)

    def pass_on(origin, slab, to_right, to_left):
        @pl.when(to_right)
        def _():
            chain_copy(0, origin, slab).start()

        @pl.when(to_left)
        def _():
            chain_copy(1, origin, slab).start()

    own_slab.wait()
    pass_on(place, far_me, has_right, has_left)

    def far_finish(step, carry):
        source = lax.rem(far_me - step + groups, groups)
        rows_copy, parts_copy = far_copy(step, source, source)
        rows_copy.wait_send()
        rows_copy.wait_recv()
        pass_on(place, source, has_right, has_left)
        parts_copy.wait_send()
        parts_copy.wait_recv()
        return carry

    lax.fori_loop(1, groups, far_finish, 0)
    own_part.wait()
    own_parts = pltpu.make_async_copy(far_parts, near_parts.at[place], local_sem.at[2])
    own_parts.start()

    def near_parts_copy(step, slot):
        return pltpu.make_async_remote_copy(
            src_ref=far_parts, dst_ref=near_parts.at[slot],
            send_sem=near_psend.at[step], recv_sem=near_precv.at[step],
            device_id=near_member(lax.rem(place + step, shards)),
            device_id_type=pl.DeviceIdType.MESH)

    for step in range(1, shards):
        near_parts_copy(step, place).start()

    for distance in range(1, shards):
        def relay(slab, carry, distance=distance):
            from_left = place - distance
            from_right = place + distance

            @pl.when(from_left >= 0)
            def _():
                chain_copy(0, from_left, slab).wait_recv()
                pass_on(from_left, slab, has_right, False)

            @pl.when(from_right < shards)
            def _():
                chain_copy(1, from_right, slab).wait_recv()
                pass_on(from_right, slab, False, has_left)

            return carry

        lax.fori_loop(0, groups, relay, 0)

    for origin in range(shards):
        def drain(slab, carry, origin=origin):
            @pl.when((origin <= place) & has_right)
            def _():
                chain_copy(0, origin, slab).wait_send()

            @pl.when((origin >= place) & has_left)
            def _():
                chain_copy(1, origin, slab).wait_send()

            return carry

        lax.fori_loop(0, groups, drain, 0)

    def parts_finish(step, carry):
        parts_copy = near_parts_copy(step, lax.rem(place - step + shards, shards))
        parts_copy.wait_send()
        parts_copy.wait_recv()
        return carry

    lax.fori_loop(1, shards, parts_finish, 0)
    own_parts.wait()

    def lane_finish(step, carry):
        source = lax.rem(lane_me - step + lanes, lanes)
        for which in range(3):
            copy = lane_copy(which, step, source, source)
            copy.wait_send()
            copy.wait_recv()
        return carry

    lax.fori_loop(1, lanes, lane_finish, 0)
    for copy in own_weights:
        copy.wait()


def outbound(slabs, parts, weights, groups, shards, lanes, collective_id):
    rows_shape = (shards,) + slabs.shape
    parts_shape = (shards, groups) + parts.shape
    weight_shapes = [jax.ShapeDtypeStruct((lanes,) + w.shape, w.dtype) for w in weights]
    return pl.pallas_call(
        functools.partial(outbound_kernel, groups, shards, lanes),
        out_shape=[jax.ShapeDtypeStruct(rows_shape, slabs.dtype),
                   jax.ShapeDtypeStruct(parts_shape, parts.dtype)] + weight_shapes,
        in_specs=[pl.BlockSpec(memory_space=pltpu.VMEM)] * 5,
        out_specs=[pl.BlockSpec(memory_space=pltpu.VMEM)] * 5,
        scratch_shapes=[pltpu.VMEM((groups,) + parts.shape, parts.dtype)]
        + [pltpu.SemaphoreType.DMA((groups,))] * 4
        + [pltpu.SemaphoreType.DMA((2, shards, groups)), pltpu.SemaphoreType.DMA((shards, groups))]
        + [pltpu.SemaphoreType.DMA((shards,))] * 2
        + [pltpu.SemaphoreType.DMA((8,))]
        + [pltpu.SemaphoreType.DMA((3, lanes))] * 2,
        compiler_params=pltpu.CompilerParams(collective_id=collective_id, has_side_effects=True),
    )(slabs, parts, *weights)


def merge_softmax(stacked, rows, width):
    slot_max = stacked[:, rows, :width]
    slot_sum = stacked[:, rows + 1, :width]
    joint_max = jnp.max(slot_max, axis=0)
    slot_scale = jnp.exp(slot_max - joint_max[None])
    joint_sum = jnp.sum(slot_sum * slot_scale, axis=0)
    lane_scale = jnp.repeat(slot_scale.reshape(slot_scale.shape[0], rows, -1), HD, axis=2)
    joint_acc = jnp.sum(stacked[:, :rows, :] * lane_scale, axis=0)
    return joint_max, joint_sum, joint_acc


def pack_softmax(joint_max, joint_sum, joint_acc):
    rows, lanes = joint_acc.shape
    stats = jnp.stack([joint_max, joint_sum])
    return jnp.concatenate([joint_acc, jnp.pad(stats, ((0, 2), (0, lanes - stats.shape[1])))], axis=0)


def rms_scale(hidden, norm_gain):
    values = hidden.astype(jnp.float32)
    meansq = jnp.mean(values * values, axis=-1, keepdims=True)
    return (values * lax.rsqrt(meansq + 1e-06) * norm_gain).astype(jnp.bfloat16)


def route_slots(route_rows, capacity):
    flat_routes = route_rows.reshape(-1)
    onehot = (flat_routes[:, None] == jnp.arange(EXPERTS, dtype=jnp.int32)[None, :]).astype(
        jnp.int32
    )
    earlier = jnp.cumsum(onehot, axis=0) - onehot
    slot_rank = jnp.sum(earlier * onehot, axis=1)
    return flat_routes * capacity + slot_rank


def expert_block(row_block, weights):
    gate_full, up_full, down_full = weights
    gate_pre = jnp.dot(row_block, gate_full, preferred_element_type=jnp.float32)
    up_pre = jnp.dot(row_block, up_full, preferred_element_type=jnp.float32)
    act = (jax.nn.gelu(gate_pre, approximate=True) * up_pre).astype(jnp.bfloat16)
    return jnp.dot(act, down_full, preferred_element_type=jnp.float32).astype(jnp.bfloat16)


def body(
    queries,
    keys_new,
    values_new,
    key_cache,
    value_cache,
    buckets,
    lengths,
    bias_table,
    out_proj,
    decode_in,
    prefill_in,
    routes,
    gates,
    dec_routes,
    dec_gates,
    norm_gain,
    w_gate,
    w_up,
    w_down,
):
    seq_count = lax.axis_size("seq")
    seq_index = lax.axis_index("seq")
    tp_index = lax.axis_index("tp")
    shards = seq_count // EXPERTS
    normed_pre = rms_scale(prefill_in, norm_gain)
    request_count, heads_width = queries.shape
    heads_here = heads_width // HD
    ctx_local = key_cache.shape[1]
    score_scale = 1.0 / math.sqrt(HD)
    query_rows = queries.reshape(request_count, heads_here, HD)
    key_rows = key_cache.reshape(request_count, ctx_local, heads_here, HD)
    value_rows = value_cache.reshape(request_count, ctx_local, heads_here, HD).astype(jnp.float32)
    bias_here = lax.dynamic_slice_in_dim(bias_table, tp_index * heads_here, heads_here, 1)
    bucket_hot = (
        buckets[..., None] == jnp.arange(bias_table.shape[0], dtype=jnp.int32)[None, None, :]
    ).astype(jnp.float32)
    bias_rows = jnp.einsum("rcn,nh->rhc", bucket_hot, bias_here, precision=lax.Precision.HIGHEST)
    cache_scores = (
        jnp.einsum("rhd,rchd->rhc", query_rows, key_rows, preferred_element_type=jnp.float32)
        * score_scale
        + bias_rows
    )
    positions = seq_index * ctx_local + jnp.arange(ctx_local, dtype=jnp.int32)
    valid_mask = (positions[None, :] < lengths[:, None])[:, None, :]
    cache_scores = jnp.where(valid_mask, cache_scores, -1e30)
    local_max = jnp.max(cache_scores, axis=-1)
    local_weights = jnp.where(valid_mask, jnp.exp(cache_scores - local_max[..., None]), 0.0)
    local_sum = jnp.sum(local_weights, axis=-1)
    local_acc = jnp.einsum(
        "rhc,rchd->rhd", local_weights, value_rows, precision=lax.Precision.HIGHEST
    )
    tp_count = lax.axis_size("tp")
    flat_width = request_count * heads_here
    packed_parts = pack_softmax(
        local_max.reshape(-1), local_sum.reshape(-1), local_acc.reshape(request_count, heads_here * HD)
    )
    flat_index = route_slots(routes, CAP)
    feature_width = normed_pre.shape[1]
    slabs = (
        jnp.zeros((EXPERTS * CAP, feature_width), jnp.bfloat16)
        .at[flat_index]
        .set(jnp.repeat(normed_pre, TOP, axis=0))
        .reshape(EXPERTS, CAP, feature_width)
    )
    group_count = seq_count // shards
    block_rows, block_parts, gate_all, up_all, down_all = outbound(
        slabs, packed_parts, (w_gate, w_up, w_down), group_count, shards, tp_count, 1
    )
    weights = (
        gate_all.reshape(-1, gate_all.shape[-1]),
        up_all.reshape(-1, up_all.shape[-1]),
        jnp.transpose(down_all, (1, 0, 2)).reshape(down_all.shape[1], -1),
    )
    stage = merge_softmax(
        block_parts.reshape((-1,) + packed_parts.shape), request_count, flat_width
    )
    part_max = stage[0].reshape(request_count, heads_here)
    part_sum = stage[1].reshape(request_count, heads_here)
    part_acc = stage[2].reshape(request_count, heads_here, HD)
    own_key = keys_new.reshape(request_count, heads_here, HD).astype(jnp.float32)
    own_value = values_new.reshape(request_count, heads_here, HD).astype(jnp.float32)
    own_score = (
        jnp.sum(query_rows.astype(jnp.float32) * own_key, axis=-1) * score_scale
        + bias_here[0][None, :]
    )
    row_peak = jnp.maximum(part_max, own_score)
    keep_scale = jnp.exp(part_max - row_peak)
    own_weight = jnp.exp(own_score - row_peak)
    weight_total = part_sum * keep_scale + own_weight
    weighted = part_acc * keep_scale[..., None] + own_weight[..., None] * own_value
    mixed_rows = (
        (weighted / weight_total[..., None])
        .astype(jnp.bfloat16)
        .reshape(request_count, heads_width)
    )
    head_terms = jnp.dot(mixed_rows, out_proj, preferred_element_type=jnp.float32)
    (head_all,) = axis_share([head_terms], [False], "tp", tp_count, 1, 3)
    attended = jnp.sum(head_all, axis=0)
    decode_hidden = (decode_in.astype(jnp.float32) + attended).astype(jnp.bfloat16)
    normed_dec = rms_scale(decode_hidden, norm_gain)
    block_count = block_rows.shape[0] * block_rows.shape[1] * block_rows.shape[2]
    all_rows = jnp.concatenate([block_rows.reshape(block_count, feature_width), normed_dec], axis=0)
    all_out = expert_block(all_rows, weights)
    block_out = all_out[:block_count].reshape(block_rows.shape)
    dec_part = all_out[block_count:]
    part_rows, dec_block = axis_share(
        [block_out, dec_part], [True, False], "seq", shards, 1, 4
    )
    summed = jnp.zeros(part_rows.shape[1:], jnp.float32)
    dec_expert = jnp.zeros(dec_block.shape[1:], jnp.float32)
    for part in range(shards):
        summed = summed + part_rows[part].astype(jnp.float32)
        dec_expert = dec_expert + dec_block[part].astype(jnp.float32)
    my_expert = seq_index // shards
    gate_here = jnp.sum(jnp.where(dec_routes == my_expert, dec_gates, 0.0), axis=1)
    returned, dec_all = axis_share(
        [summed, gate_here[:, None] * dec_expert], [True, False], "seq", group_count, shards, 5, twisted=True
    )
    dec_terms = jnp.sum(dec_all, axis=0)
    decode_out = (decode_hidden.astype(jnp.float32) + dec_terms).astype(jnp.bfloat16)
    picked = jnp.take(returned.reshape(EXPERTS * CAP, -1), flat_index, axis=0)
    picked = picked.reshape(-1, TOP, picked.shape[-1])
    prefill_out = (
        prefill_in.astype(jnp.float32) + jnp.sum(gates[..., None] * picked, axis=1)
    ).astype(jnp.bfloat16)
    return (decode_out, prefill_out)


def solution(mesh):
    placed = (
        P(None, "tp"),
        P(None, "tp"),
        P(None, "tp"),
        P(None, "seq", "tp"),
        P(None, "seq", "tp"),
        P(None, "seq"),
        P(),
        P(),
        P("tp", None),
        P(),
        P(("seq", "tp"), None),
        P(("seq", "tp"), None),
        P(("seq", "tp"), None),
        P(),
        P(),
        P(),
        P("tp", "seq"),
        P("tp", "seq"),
        P("seq", "tp"),
    )
    return jax.shard_map(
        body, mesh=mesh, in_specs=placed, out_specs=(P(), P(("seq", "tp"), None)), check_vma=False
    )
```

```python
import functools
import math

import jax
import jax.numpy as jnp
from jax import lax
from jax.experimental import pallas as pl
from jax.experimental.pallas import tpu as pltpu
from jax.sharding import PartitionSpec as P

HD = 64
EXPERTS = 16
TOP = 2
CAP = 10


def peer_device(axis, peer):
    if axis == "seq":
        return (peer, lax.axis_index("tp"))
    return (lax.axis_index("seq"), peer)


def share_kernel(axis, count, stride, modes, *refs):
    width = len(modes)
    sources = refs[:width]
    landed = refs[width : 2 * width]
    send_sems = refs[2 * width : 3 * width]
    recv_sems = refs[3 * width :]
    index = lax.axis_index(axis)
    me = lax.rem(index // stride, count)
    base = index - me * stride

    def member(slot):
        return peer_device(axis, base + slot * stride)

    def piece(which, slot):
        return sources[which].at[slot] if modes[which] else sources[which]

    barrier = pltpu.get_barrier_semaphore()

    def greet(step, carry):
        pl.semaphore_signal(
            barrier,
            inc=1,
            device_id=member(lax.rem(me + step, count)),
            device_id_type=pl.DeviceIdType.MESH,
        )
        return carry

    lax.fori_loop(1, count, greet, 0)
    pl.semaphore_wait(barrier, count - 1)

    def outgoing(which, step):
        target = lax.rem(me + step, count)
        return pltpu.make_async_remote_copy(
            src_ref=piece(which, target),
            dst_ref=landed[which].at[me],
            send_sem=send_sems[which].at[step],
            recv_sem=recv_sems[which].at[step],
            device_id=member(target),
            device_id_type=pl.DeviceIdType.MESH,
        )

    def incoming(which, step):
        source = lax.rem(me - step + count, count)
        return pltpu.make_async_remote_copy(
            src_ref=piece(which, source),
            dst_ref=landed[which].at[source],
            send_sem=send_sems[which].at[step],
            recv_sem=recv_sems[which].at[step],
            device_id=member(source),
            device_id_type=pl.DeviceIdType.MESH,
        )

    def launch(step, carry):
        for which in range(width):
            outgoing(which, step).start()
        return carry

    lax.fori_loop(1, count, launch, 0)
    for which in range(width):
        landed[which][me] = piece(which, me)[...]

    def finish(step, carry):
        for which in range(width):
            outgoing(which, step).wait_send()
            incoming(which, step).wait_recv()
        return carry

    lax.fori_loop(1, count, finish, 0)


def axis_share(payloads, modes, axis, count, stride, collective_id):
    shapes = [x.shape if mode else (count,) + x.shape for x, mode in zip(payloads, modes)]
    width = len(payloads)
    return pl.pallas_call(
        functools.partial(share_kernel, axis, count, stride, tuple(modes)),
        out_shape=[jax.ShapeDtypeStruct(s, x.dtype) for s, x in zip(shapes, payloads)],
        in_specs=[pl.BlockSpec(memory_space=pltpu.VMEM)] * width,
        out_specs=[pl.BlockSpec(memory_space=pltpu.VMEM)] * width,
        scratch_shapes=[pltpu.SemaphoreType.DMA((count,))] * (2 * width),
        compiler_params=pltpu.CompilerParams(collective_id=collective_id, has_side_effects=True),
    )(*payloads)


def outbound_kernel(groups, shards, lanes, slab_ref, part_ref, gate_ref, up_ref, down_ref,
                    near_rows, near_parts, gate_all, up_all, down_all, far_parts,
                    far_send, far_recv, far_psend, far_precv,
                    near_send, near_recv, near_psend, near_precv, local_sem,
                    lane_send, lane_recv):
    index = lax.axis_index("seq")
    far_me = lax.rem(index // shards, groups)
    far_base = index - far_me * shards
    place = lax.rem(index, shards)
    near_base = index - place
    has_right = place < shards - 1
    has_left = place > 0

    def far_member(slot):
        return peer_device("seq", far_base + slot * shards)

    def near_member(slot):
        return peer_device("seq", near_base + slot)

    barrier = pltpu.get_barrier_semaphore()

    def greet_far(step, carry):
        pl.semaphore_signal(barrier, inc=1, device_id=far_member(lax.rem(far_me + step, groups)),
                            device_id_type=pl.DeviceIdType.MESH)
        return carry

    def greet_near(step, carry):
        pl.semaphore_signal(barrier, inc=1, device_id=near_member(lax.rem(place + step, shards)),
                            device_id_type=pl.DeviceIdType.MESH)
        return carry

    lane_me = lax.axis_index("tp")

    def lane_member(slot):
        return peer_device("tp", slot)

    def greet_lane(step, carry):
        pl.semaphore_signal(barrier, inc=1, device_id=lane_member(lax.rem(lane_me + step, lanes)),
                            device_id_type=pl.DeviceIdType.MESH)
        return carry

    lax.fori_loop(1, groups, greet_far, 0)
    lax.fori_loop(1, shards, greet_near, 0)
    lax.fori_loop(1, lanes, greet_lane, 0)
    pl.semaphore_wait(barrier, groups + shards + lanes - 3)
    weight_refs = ((gate_ref, gate_all), (up_ref, up_all), (down_ref, down_all))

    def lane_copy(which, step, slot, landed_slot):
        source_ref, landed_ref = weight_refs[which]
        return pltpu.make_async_remote_copy(
            src_ref=source_ref, dst_ref=landed_ref.at[landed_slot],
            send_sem=lane_send.at[which, step], recv_sem=lane_recv.at[which, step],
            device_id=lane_member(slot), device_id_type=pl.DeviceIdType.MESH)

    def lane_start(step, carry):
        for which in range(3):
            lane_copy(which, step, lax.rem(lane_me + step, lanes), lane_me).start()
        return carry


    def far_copy(step, slot, landed_slot):
        return (
            pltpu.make_async_remote_copy(
                src_ref=slab_ref.at[slot], dst_ref=near_rows.at[place, landed_slot],
                send_sem=far_send.at[step], recv_sem=far_recv.at[step],
                device_id=far_member(slot), device_id_type=pl.DeviceIdType.MESH),
            pltpu.make_async_remote_copy(
                src_ref=part_ref, dst_ref=far_parts.at[landed_slot],
                send_sem=far_psend.at[step], recv_sem=far_precv.at[step],
                device_id=far_member(slot), device_id_type=pl.DeviceIdType.MESH),
        )

    def far_start(step, carry):
        for copy in far_copy(step, lax.rem(far_me + step, groups), far_me):
            copy.start()
        return carry

    lax.fori_loop(1, groups, far_start, 0)
    own_slab = pltpu.make_async_copy(slab_ref.at[far_me], near_rows.at[place, far_me], local_sem.at[0])
    own_part = pltpu.make_async_copy(part_ref, far_parts.at[far_me], local_sem.at[1])
    own_slab.start()
    own_part.start()
    lax.fori_loop(1, lanes, lane_start, 0)
    own_weights = [
        pltpu.make_async_copy(source_ref, landed_ref.at[lane_me], local_sem.at[3 + which])
        for which, (source_ref, landed_ref) in enumerate(weight_refs)
    ]
    for copy in own_weights:
        copy.start()

    def chain_copy(direction, origin, slab):
        return pltpu.make_async_remote_copy(
            src_ref=near_rows.at[origin, slab], dst_ref=near_rows.at[origin, slab],
            send_sem=near_send.at[direction, origin, slab], recv_sem=near_recv.at[origin, slab],
            device_id=near_member(place + 1 - 2 * direction), device_id_type=pl.DeviceIdType.MESH)

    def pass_on(origin, slab, to_right, to_left):
        @pl.when(to_right)
        def _():
            chain_copy(0, origin, slab).start()

        @pl.when(to_left)
        def _():
            chain_copy(1, origin, slab).start()

    own_slab.wait()
    pass_on(place, far_me, has_right, has_left)

    def far_finish(step, carry):
        source = lax.rem(far_me - step + groups, groups)
        rows_copy, parts_copy = far_copy(step, source, source)
        rows_copy.wait_send()
        rows_copy.wait_recv()
        pass_on(place, source, has_right, has_left)
        parts_copy.wait_send()
        parts_copy.wait_recv()
        return carry

    lax.fori_loop(1, groups, far_finish, 0)
    own_part.wait()
    own_parts = pltpu.make_async_copy(far_parts, near_parts.at[place], local_sem.at[2])
    own_parts.start()

    def near_parts_copy(step, slot):
        return pltpu.make_async_remote_copy(
            src_ref=far_parts, dst_ref=near_parts.at[slot],
            send_sem=near_psend.at[step], recv_sem=near_precv.at[step],
            device_id=near_member(lax.rem(place + step, shards)),
            device_id_type=pl.DeviceIdType.MESH)

    for step in range(1, shards):
        near_parts_copy(step, place).start()

    for distance in range(1, shards):
        def relay(slab, carry, distance=distance):
            from_left = place - distance
            from_right = place + distance

            @pl.when(from_left >= 0)
            def _():
                chain_copy(0, from_left, slab).wait_recv()
                pass_on(from_left, slab, has_right, False)

            @pl.when(from_right < shards)
            def _():
                chain_copy(1, from_right, slab).wait_recv()
                pass_on(from_right, slab, False, has_left)

            return carry

        lax.fori_loop(0, groups, relay, 0)

    for origin in range(shards):
        def drain(slab, carry, origin=origin):
            @pl.when((origin <= place) & has_right)
            def _():
                chain_copy(0, origin, slab).wait_send()

            @pl.when((origin >= place) & has_left)
            def _():
                chain_copy(1, origin, slab).wait_send()

            return carry

        lax.fori_loop(0, groups, drain, 0)

    def parts_finish(step, carry):
        parts_copy = near_parts_copy(step, lax.rem(place - step + shards, shards))
        parts_copy.wait_send()
        parts_copy.wait_recv()
        return carry

    lax.fori_loop(1, shards, parts_finish, 0)
    own_parts.wait()

    def lane_finish(step, carry):
        source = lax.rem(lane_me - step + lanes, lanes)
        for which in range(3):
            copy = lane_copy(which, step, source, source)
            copy.wait_send()
            copy.wait_recv()
        return carry

    lax.fori_loop(1, lanes, lane_finish, 0)
    for copy in own_weights:
        copy.wait()


def outbound(slabs, parts, weights, groups, shards, lanes, collective_id):
    rows_shape = (shards,) + slabs.shape
    parts_shape = (shards, groups) + parts.shape
    weight_shapes = [jax.ShapeDtypeStruct((lanes,) + w.shape, w.dtype) for w in weights]
    return pl.pallas_call(
        functools.partial(outbound_kernel, groups, shards, lanes),
        out_shape=[jax.ShapeDtypeStruct(rows_shape, slabs.dtype),
                   jax.ShapeDtypeStruct(parts_shape, parts.dtype)] + weight_shapes,
        in_specs=[pl.BlockSpec(memory_space=pltpu.VMEM)] * 5,
        out_specs=[pl.BlockSpec(memory_space=pltpu.VMEM)] * 5,
        scratch_shapes=[pltpu.VMEM((groups,) + parts.shape, parts.dtype)]
        + [pltpu.SemaphoreType.DMA((groups,))] * 4
        + [pltpu.SemaphoreType.DMA((2, shards, groups)), pltpu.SemaphoreType.DMA((shards, groups))]
        + [pltpu.SemaphoreType.DMA((shards,))] * 2
        + [pltpu.SemaphoreType.DMA((8,))]
        + [pltpu.SemaphoreType.DMA((3, lanes))] * 2,
        compiler_params=pltpu.CompilerParams(collective_id=collective_id, has_side_effects=True),
    )(slabs, parts, *weights)


def merge_softmax(stacked, rows, width):
    slot_max = stacked[:, rows, :width]
    slot_sum = stacked[:, rows + 1, :width]
    joint_max = jnp.max(slot_max, axis=0)
    slot_scale = jnp.exp(slot_max - joint_max[None])
    joint_sum = jnp.sum(slot_sum * slot_scale, axis=0)
    lane_scale = jnp.repeat(slot_scale.reshape(slot_scale.shape[0], rows, -1), HD, axis=2)
    joint_acc = jnp.sum(stacked[:, :rows, :] * lane_scale, axis=0)
    return joint_max, joint_sum, joint_acc


def pack_softmax(joint_max, joint_sum, joint_acc):
    rows, lanes = joint_acc.shape
    stats = jnp.stack([joint_max, joint_sum])
    return jnp.concatenate([joint_acc, jnp.pad(stats, ((0, 2), (0, lanes - stats.shape[1])))], axis=0)


def rms_scale(hidden, norm_gain):
    values = hidden.astype(jnp.float32)
    meansq = jnp.mean(values * values, axis=-1, keepdims=True)
    return (values * lax.rsqrt(meansq + 1e-06) * norm_gain).astype(jnp.bfloat16)


def route_slots(route_rows, capacity):
    flat_routes = route_rows.reshape(-1)
    onehot = (flat_routes[:, None] == jnp.arange(EXPERTS, dtype=jnp.int32)[None, :]).astype(
        jnp.int32
    )
    earlier = jnp.cumsum(onehot, axis=0) - onehot
    slot_rank = jnp.sum(earlier * onehot, axis=1)
    return flat_routes * capacity + slot_rank


def expert_block(row_block, weights):
    gate_full, up_full, down_full = weights
    gate_pre = jnp.dot(row_block, gate_full, preferred_element_type=jnp.float32)
    up_pre = jnp.dot(row_block, up_full, preferred_element_type=jnp.float32)
    act = (jax.nn.gelu(gate_pre, approximate=True) * up_pre).astype(jnp.bfloat16)
    return jnp.dot(act, down_full, preferred_element_type=jnp.float32).astype(jnp.bfloat16)


def body(
    queries,
    keys_new,
    values_new,
    key_cache,
    value_cache,
    buckets,
    lengths,
    bias_table,
    out_proj,
    decode_in,
    prefill_in,
    routes,
    gates,
    dec_routes,
    dec_gates,
    norm_gain,
    w_gate,
    w_up,
    w_down,
):
    seq_count = lax.axis_size("seq")
    seq_index = lax.axis_index("seq")
    tp_index = lax.axis_index("tp")
    shards = seq_count // EXPERTS
    normed_pre = rms_scale(prefill_in, norm_gain)
    request_count, heads_width = queries.shape
    heads_here = heads_width // HD
    ctx_local = key_cache.shape[1]
    score_scale = 1.0 / math.sqrt(HD)
    query_rows = queries.reshape(request_count, heads_here, HD)
    key_rows = key_cache.reshape(request_count, ctx_local, heads_here, HD)
    value_rows = value_cache.reshape(request_count, ctx_local, heads_here, HD).astype(jnp.float32)
    bias_here = lax.dynamic_slice_in_dim(bias_table, tp_index * heads_here, heads_here, 1)
    bucket_hot = (
        buckets[..., None] == jnp.arange(bias_table.shape[0], dtype=jnp.int32)[None, None, :]
    ).astype(jnp.float32)
    bias_rows = jnp.einsum("rcn,nh->rhc", bucket_hot, bias_here, precision=lax.Precision.HIGHEST)
    cache_scores = (
        jnp.einsum("rhd,rchd->rhc", query_rows, key_rows, preferred_element_type=jnp.float32)
        * score_scale
        + bias_rows
    )
    positions = seq_index * ctx_local + jnp.arange(ctx_local, dtype=jnp.int32)
    valid_mask = (positions[None, :] < lengths[:, None])[:, None, :]
    cache_scores = jnp.where(valid_mask, cache_scores, -1e30)
    local_max = jnp.max(cache_scores, axis=-1)
    local_weights = jnp.where(valid_mask, jnp.exp(cache_scores - local_max[..., None]), 0.0)
    local_sum = jnp.sum(local_weights, axis=-1)
    local_acc = jnp.einsum(
        "rhc,rchd->rhd", local_weights, value_rows, precision=lax.Precision.HIGHEST
    )
    tp_count = lax.axis_size("tp")
    flat_width = request_count * heads_here
    packed_parts = pack_softmax(
        local_max.reshape(-1), local_sum.reshape(-1), local_acc.reshape(request_count, heads_here * HD)
    )
    flat_index = route_slots(routes, CAP)
    feature_width = normed_pre.shape[1]
    slabs = (
        jnp.zeros((EXPERTS * CAP, feature_width), jnp.bfloat16)
        .at[flat_index]
        .set(jnp.repeat(normed_pre, TOP, axis=0))
        .reshape(EXPERTS, CAP, feature_width)
    )
    group_count = seq_count // shards
    block_rows, block_parts, gate_all, up_all, down_all = outbound(
        slabs, packed_parts, (w_gate, w_up, w_down), group_count, shards, tp_count, 1
    )
    weights = (
        gate_all.reshape(-1, gate_all.shape[-1]),
        up_all.reshape(-1, up_all.shape[-1]),
        jnp.transpose(down_all, (1, 0, 2)).reshape(down_all.shape[1], -1),
    )
    stage = merge_softmax(
        block_parts.reshape((-1,) + packed_parts.shape), request_count, flat_width
    )
    part_max = stage[0].reshape(request_count, heads_here)
    part_sum = stage[1].reshape(request_count, heads_here)
    part_acc = stage[2].reshape(request_count, heads_here, HD)
    own_key = keys_new.reshape(request_count, heads_here, HD).astype(jnp.float32)
    own_value = values_new.reshape(request_count, heads_here, HD).astype(jnp.float32)
    own_score = (
        jnp.sum(query_rows.astype(jnp.float32) * own_key, axis=-1) * score_scale
        + bias_here[0][None, :]
    )
    row_peak = jnp.maximum(part_max, own_score)
    keep_scale = jnp.exp(part_max - row_peak)
    own_weight = jnp.exp(own_score - row_peak)
    weight_total = part_sum * keep_scale + own_weight
    weighted = part_acc * keep_scale[..., None] + own_weight[..., None] * own_value
    mixed_rows = (
        (weighted / weight_total[..., None])
        .astype(jnp.bfloat16)
        .reshape(request_count, heads_width)
    )
    head_terms = jnp.dot(mixed_rows, out_proj, preferred_element_type=jnp.float32)
    (head_all,) = axis_share([head_terms], [False], "tp", tp_count, 1, 3)
    attended = jnp.sum(head_all, axis=0)
    decode_hidden = (decode_in.astype(jnp.float32) + attended).astype(jnp.bfloat16)
    normed_dec = rms_scale(decode_hidden, norm_gain)
    block_count = block_rows.shape[0] * block_rows.shape[1] * block_rows.shape[2]
    all_rows = jnp.concatenate([block_rows.reshape(block_count, feature_width), normed_dec], axis=0)
    all_out = expert_block(all_rows, weights)
    block_out = all_out[:block_count].reshape(block_rows.shape)
    dec_part = all_out[block_count:]
    part_rows, dec_block = axis_share(
        [block_out, dec_part], [True, False], "seq", shards, 1, 4
    )
    summed = jnp.zeros(part_rows.shape[1:], jnp.float32)
    dec_expert = jnp.zeros(dec_block.shape[1:], jnp.float32)
    for part in range(shards):
        summed = summed + part_rows[part].astype(jnp.float32)
        dec_expert = dec_expert + dec_block[part].astype(jnp.float32)
    my_expert = seq_index // shards
    gate_here = jnp.sum(jnp.where(dec_routes == my_expert, dec_gates, 0.0), axis=1)
    returned, dec_all = axis_share(
        [summed, gate_here[:, None] * dec_expert], [True, False], "seq", group_count, shards, 5
    )
    dec_terms = jnp.sum(dec_all, axis=0)
    decode_out = (decode_hidden.astype(jnp.float32) + dec_terms).astype(jnp.bfloat16)
    picked = jnp.take(returned.reshape(EXPERTS * CAP, -1), flat_index, axis=0)
    picked = picked.reshape(-1, TOP, picked.shape[-1])
    prefill_out = (
        prefill_in.astype(jnp.float32) + jnp.sum(gates[..., None] * picked, axis=1)
    ).astype(jnp.bfloat16)
    return (decode_out, prefill_out)


def solution(mesh):
    placed = (
        P(None, "tp"),
        P(None, "tp"),
        P(None, "tp"),
        P(None, "seq", "tp"),
        P(None, "seq", "tp"),
        P(None, "seq"),
        P(),
        P(),
        P("tp", None),
        P(),
        P(("seq", "tp"), None),
        P(("seq", "tp"), None),
        P(("seq", "tp"), None),
        P(),
        P(),
        P(),
        P("tp", "seq"),
        P("tp", "seq"),
        P("seq", "tp"),
    )
    return jax.shard_map(
        body, mesh=mesh, in_specs=placed, out_specs=(P(), P(("seq", "tp"), None)), check_vma=False
    )
```

```python
import functools
import math

import jax
import jax.numpy as jnp
from jax import lax
from jax.experimental import pallas as pl
from jax.experimental.pallas import tpu as pltpu
from jax.sharding import PartitionSpec as P

HD = 64
EXPERTS = 16
TOP = 2
CAP = 10


def spread(turn, count):
    odd = turn % 2
    return odd * ((turn + 1) // 2) + (1 - odd) * (count - turn // 2)


def peer_device(axis, peer):
    if axis == "seq":
        return (peer, lax.axis_index("tp"))
    return (lax.axis_index("seq"), peer)


def share_kernel(axis, count, stride, modes, *refs):
    width = len(modes)
    sources = refs[:width]
    landed = refs[width : 2 * width]
    send_sems = refs[2 * width : 3 * width]
    recv_sems = refs[3 * width :]
    index = lax.axis_index(axis)
    me = lax.rem(index // stride, count)
    base = index - me * stride

    def member(slot):
        return peer_device(axis, base + slot * stride)

    def piece(which, slot):
        return sources[which].at[slot] if modes[which] else sources[which]

    barrier = pltpu.get_barrier_semaphore()

    def greet(step, carry):
        pl.semaphore_signal(
            barrier,
            inc=1,
            device_id=member(lax.rem(me + step, count)),
            device_id_type=pl.DeviceIdType.MESH,
        )
        return carry

    lax.fori_loop(1, count, greet, 0)
    pl.semaphore_wait(barrier, count - 1)

    def outgoing(which, step):
        target = lax.rem(me + step, count)
        return pltpu.make_async_remote_copy(
            src_ref=piece(which, target),
            dst_ref=landed[which].at[me],
            send_sem=send_sems[which].at[step],
            recv_sem=recv_sems[which].at[step],
            device_id=member(target),
            device_id_type=pl.DeviceIdType.MESH,
        )

    def incoming(which, step):
        source = lax.rem(me - step + count, count)
        return pltpu.make_async_remote_copy(
            src_ref=piece(which, source),
            dst_ref=landed[which].at[source],
            send_sem=send_sems[which].at[step],
            recv_sem=recv_sems[which].at[step],
            device_id=member(source),
            device_id_type=pl.DeviceIdType.MESH,
        )

    def launch(turn, carry):
        step = spread(turn, count)
        for which in range(width):
            outgoing(which, step).start()
        return carry

    lax.fori_loop(1, count, launch, 0)
    for which in range(width):
        landed[which][me] = piece(which, me)[...]

    def finish(step, carry):
        for which in range(width):
            outgoing(which, step).wait_send()
            incoming(which, step).wait_recv()
        return carry

    lax.fori_loop(1, count, finish, 0)


def axis_share(payloads, modes, axis, count, stride, collective_id):
    shapes = [x.shape if mode else (count,) + x.shape for x, mode in zip(payloads, modes)]
    width = len(payloads)
    return pl.pallas_call(
        functools.partial(share_kernel, axis, count, stride, tuple(modes)),
        out_shape=[jax.ShapeDtypeStruct(s, x.dtype) for s, x in zip(shapes, payloads)],
        in_specs=[pl.BlockSpec(memory_space=pltpu.VMEM)] * width,
        out_specs=[pl.BlockSpec(memory_space=pltpu.VMEM)] * width,
        scratch_shapes=[pltpu.SemaphoreType.DMA((count,))] * (2 * width),
        compiler_params=pltpu.CompilerParams(collective_id=collective_id, has_side_effects=True),
    )(*payloads)


def outbound_kernel(groups, shards, lanes, slab_ref, part_ref, gate_ref, up_ref, down_ref,
                    near_rows, near_parts, gate_all, up_all, down_all, far_parts,
                    far_send, far_recv, far_psend, far_precv,
                    near_send, near_recv, near_psend, near_precv, local_sem,
                    lane_send, lane_recv):
    index = lax.axis_index("seq")
    far_me = lax.rem(index // shards, groups)
    far_base = index - far_me * shards
    place = lax.rem(index, shards)
    near_base = index - place
    has_right = place < shards - 1
    has_left = place > 0

    def far_member(slot):
        return peer_device("seq", far_base + slot * shards)

    def near_member(slot):
        return peer_device("seq", near_base + slot)

    barrier = pltpu.get_barrier_semaphore()

    def greet_far(step, carry):
        pl.semaphore_signal(barrier, inc=1, device_id=far_member(lax.rem(far_me + step, groups)),
                            device_id_type=pl.DeviceIdType.MESH)
        return carry

    def greet_near(step, carry):
        pl.semaphore_signal(barrier, inc=1, device_id=near_member(lax.rem(place + step, shards)),
                            device_id_type=pl.DeviceIdType.MESH)
        return carry

    lane_me = lax.axis_index("tp")

    def lane_member(slot):
        return peer_device("tp", slot)

    def greet_lane(step, carry):
        pl.semaphore_signal(barrier, inc=1, device_id=lane_member(lax.rem(lane_me + step, lanes)),
                            device_id_type=pl.DeviceIdType.MESH)
        return carry

    lax.fori_loop(1, groups, greet_far, 0)
    lax.fori_loop(1, shards, greet_near, 0)
    lax.fori_loop(1, lanes, greet_lane, 0)
    pl.semaphore_wait(barrier, groups + shards + lanes - 3)
    weight_refs = ((gate_ref, gate_all), (up_ref, up_all), (down_ref, down_all))

    def lane_copy(which, step, slot, landed_slot):
        source_ref, landed_ref = weight_refs[which]
        return pltpu.make_async_remote_copy(
            src_ref=source_ref, dst_ref=landed_ref.at[landed_slot],
            send_sem=lane_send.at[which, step], recv_sem=lane_recv.at[which, step],
            device_id=lane_member(slot), device_id_type=pl.DeviceIdType.MESH)

    def lane_start(turn, carry):
        step = spread(turn, lanes)
        for which in range(3):
            lane_copy(which, step, lax.rem(lane_me + step, lanes), lane_me).start()
        return carry


    def far_copy(step, slot, landed_slot):
        return (
            pltpu.make_async_remote_copy(
                src_ref=slab_ref.at[slot], dst_ref=near_rows.at[place, landed_slot],
                send_sem=far_send.at[step], recv_sem=far_recv.at[step],
                device_id=far_member(slot), device_id_type=pl.DeviceIdType.MESH),
            pltpu.make_async_remote_copy(
                src_ref=part_ref, dst_ref=far_parts.at[landed_slot],
                send_sem=far_psend.at[step], recv_sem=far_precv.at[step],
                device_id=far_member(slot), device_id_type=pl.DeviceIdType.MESH),
        )

    def far_start(turn, carry):
        step = spread(turn, groups)
        for copy in far_copy(step, lax.rem(far_me + step, groups), far_me):
            copy.start()
        return carry

    lax.fori_loop(1, groups, far_start, 0)
    own_slab = pltpu.make_async_copy(slab_ref.at[far_me], near_rows.at[place, far_me], local_sem.at[0])
    own_part = pltpu.make_async_copy(part_ref, far_parts.at[far_me], local_sem.at[1])
    own_slab.start()
    own_part.start()
    lax.fori_loop(1, lanes, lane_start, 0)
    own_weights = [
        pltpu.make_async_copy(source_ref, landed_ref.at[lane_me], local_sem.at[3 + which])
        for which, (source_ref, landed_ref) in enumerate(weight_refs)
    ]
    for copy in own_weights:
        copy.start()

    def chain_copy(direction, origin, slab):
        return pltpu.make_async_remote_copy(
            src_ref=near_rows.at[origin, slab], dst_ref=near_rows.at[origin, slab],
            send_sem=near_send.at[direction, origin, slab], recv_sem=near_recv.at[origin, slab],
            device_id=near_member(place + 1 - 2 * direction), device_id_type=pl.DeviceIdType.MESH)

    def pass_on(origin, slab, to_right, to_left):
        @pl.when(to_right)
        def _():
            chain_copy(0, origin, slab).start()

        @pl.when(to_left)
        def _():
            chain_copy(1, origin, slab).start()

    own_slab.wait()
    pass_on(place, far_me, has_right, has_left)

    def far_finish(step, carry):
        source = lax.rem(far_me - step + groups, groups)
        rows_copy, parts_copy = far_copy(step, source, source)
        rows_copy.wait_send()
        rows_copy.wait_recv()
        pass_on(place, source, has_right, has_left)
        parts_copy.wait_send()
        parts_copy.wait_recv()
        return carry

    lax.fori_loop(1, groups, far_finish, 0)
    own_part.wait()
    own_parts = pltpu.make_async_copy(far_parts, near_parts.at[place], local_sem.at[2])
    own_parts.start()

    def near_parts_copy(step, slot):
        return pltpu.make_async_remote_copy(
            src_ref=far_parts, dst_ref=near_parts.at[slot],
            send_sem=near_psend.at[step], recv_sem=near_precv.at[step],
            device_id=near_member(lax.rem(place + step, shards)),
            device_id_type=pl.DeviceIdType.MESH)

    for step in range(1, shards):
        near_parts_copy(step, place).start()

    for distance in range(1, shards):
        def relay(slab, carry, distance=distance):
            from_left = place - distance
            from_right = place + distance

            @pl.when(from_left >= 0)
            def _():
                chain_copy(0, from_left, slab).wait_recv()
                pass_on(from_left, slab, has_right, False)

            @pl.when(from_right < shards)
            def _():
                chain_copy(1, from_right, slab).wait_recv()
                pass_on(from_right, slab, False, has_left)

            return carry

        lax.fori_loop(0, groups, relay, 0)

    for origin in range(shards):
        def drain(slab, carry, origin=origin):
            @pl.when((origin <= place) & has_right)
            def _():
                chain_copy(0, origin, slab).wait_send()

            @pl.when((origin >= place) & has_left)
            def _():
                chain_copy(1, origin, slab).wait_send()

            return carry

        lax.fori_loop(0, groups, drain, 0)

    def parts_finish(step, carry):
        parts_copy = near_parts_copy(step, lax.rem(place - step + shards, shards))
        parts_copy.wait_send()
        parts_copy.wait_recv()
        return carry

    lax.fori_loop(1, shards, parts_finish, 0)
    own_parts.wait()

    def lane_finish(step, carry):
        source = lax.rem(lane_me - step + lanes, lanes)
        for which in range(3):
            copy = lane_copy(which, step, source, source)
            copy.wait_send()
            copy.wait_recv()
        return carry

    lax.fori_loop(1, lanes, lane_finish, 0)
    for copy in own_weights:
        copy.wait()


def outbound(slabs, parts, weights, groups, shards, lanes, collective_id):
    rows_shape = (shards,) + slabs.shape
    parts_shape = (shards, groups) + parts.shape
    weight_shapes = [jax.ShapeDtypeStruct((lanes,) + w.shape, w.dtype) for w in weights]
    return pl.pallas_call(
        functools.partial(outbound_kernel, groups, shards, lanes),
        out_shape=[jax.ShapeDtypeStruct(rows_shape, slabs.dtype),
                   jax.ShapeDtypeStruct(parts_shape, parts.dtype)] + weight_shapes,
        in_specs=[pl.BlockSpec(memory_space=pltpu.VMEM)] * 5,
        out_specs=[pl.BlockSpec(memory_space=pltpu.VMEM)] * 5,
        scratch_shapes=[pltpu.VMEM((groups,) + parts.shape, parts.dtype)]
        + [pltpu.SemaphoreType.DMA((groups,))] * 4
        + [pltpu.SemaphoreType.DMA((2, shards, groups)), pltpu.SemaphoreType.DMA((shards, groups))]
        + [pltpu.SemaphoreType.DMA((shards,))] * 2
        + [pltpu.SemaphoreType.DMA((8,))]
        + [pltpu.SemaphoreType.DMA((3, lanes))] * 2,
        compiler_params=pltpu.CompilerParams(collective_id=collective_id, has_side_effects=True),
    )(slabs, parts, *weights)


def merge_softmax(stacked, rows, width):
    slot_max = stacked[:, rows, :width]
    slot_sum = stacked[:, rows + 1, :width]
    joint_max = jnp.max(slot_max, axis=0)
    slot_scale = jnp.exp(slot_max - joint_max[None])
    joint_sum = jnp.sum(slot_sum * slot_scale, axis=0)
    lane_scale = jnp.repeat(slot_scale.reshape(slot_scale.shape[0], rows, -1), HD, axis=2)
    joint_acc = jnp.sum(stacked[:, :rows, :] * lane_scale, axis=0)
    return joint_max, joint_sum, joint_acc


def pack_softmax(joint_max, joint_sum, joint_acc):
    rows, lanes = joint_acc.shape
    stats = jnp.stack([joint_max, joint_sum])
    return jnp.concatenate([joint_acc, jnp.pad(stats, ((0, 2), (0, lanes - stats.shape[1])))], axis=0)


def rms_scale(hidden, norm_gain):
    values = hidden.astype(jnp.float32)
    meansq = jnp.mean(values * values, axis=-1, keepdims=True)
    return (values * lax.rsqrt(meansq + 1e-06) * norm_gain).astype(jnp.bfloat16)


def route_slots(route_rows, capacity):
    flat_routes = route_rows.reshape(-1)
    onehot = (flat_routes[:, None] == jnp.arange(EXPERTS, dtype=jnp.int32)[None, :]).astype(
        jnp.int32
    )
    earlier = jnp.cumsum(onehot, axis=0) - onehot
    slot_rank = jnp.sum(earlier * onehot, axis=1)
    return flat_routes * capacity + slot_rank


def expert_block(row_block, weights):
    gate_full, up_full, down_full = weights
    gate_pre = jnp.dot(row_block, gate_full, preferred_element_type=jnp.float32)
    up_pre = jnp.dot(row_block, up_full, preferred_element_type=jnp.float32)
    act = (jax.nn.gelu(gate_pre, approximate=True) * up_pre).astype(jnp.bfloat16)
    return jnp.dot(act, down_full, preferred_element_type=jnp.float32).astype(jnp.bfloat16)


def body(
    queries,
    keys_new,
    values_new,
    key_cache,
    value_cache,
    buckets,
    lengths,
    bias_table,
    out_proj,
    decode_in,
    prefill_in,
    routes,
    gates,
    dec_routes,
    dec_gates,
    norm_gain,
    w_gate,
    w_up,
    w_down,
):
    seq_count = lax.axis_size("seq")
    seq_index = lax.axis_index("seq")
    tp_index = lax.axis_index("tp")
    shards = seq_count // EXPERTS
    normed_pre = rms_scale(prefill_in, norm_gain)
    request_count, heads_width = queries.shape
    heads_here = heads_width // HD
    ctx_local = key_cache.shape[1]
    score_scale = 1.0 / math.sqrt(HD)
    query_rows = queries.reshape(request_count, heads_here, HD)
    key_rows = key_cache.reshape(request_count, ctx_local, heads_here, HD)
    value_rows = value_cache.reshape(request_count, ctx_local, heads_here, HD).astype(jnp.float32)
    bias_here = lax.dynamic_slice_in_dim(bias_table, tp_index * heads_here, heads_here, 1)
    bucket_hot = (
        buckets[..., None] == jnp.arange(bias_table.shape[0], dtype=jnp.int32)[None, None, :]
    ).astype(jnp.float32)
    bias_rows = jnp.einsum("rcn,nh->rhc", bucket_hot, bias_here, precision=lax.Precision.HIGHEST)
    cache_scores = (
        jnp.einsum("rhd,rchd->rhc", query_rows, key_rows, preferred_element_type=jnp.float32)
        * score_scale
        + bias_rows
    )
    positions = seq_index * ctx_local + jnp.arange(ctx_local, dtype=jnp.int32)
    valid_mask = (positions[None, :] < lengths[:, None])[:, None, :]
    cache_scores = jnp.where(valid_mask, cache_scores, -1e30)
    local_max = jnp.max(cache_scores, axis=-1)
    local_weights = jnp.where(valid_mask, jnp.exp(cache_scores - local_max[..., None]), 0.0)
    local_sum = jnp.sum(local_weights, axis=-1)
    local_acc = jnp.einsum(
        "rhc,rchd->rhd", local_weights, value_rows, precision=lax.Precision.HIGHEST
    )
    tp_count = lax.axis_size("tp")
    flat_width = request_count * heads_here
    packed_parts = pack_softmax(
        local_max.reshape(-1), local_sum.reshape(-1), local_acc.reshape(request_count, heads_here * HD)
    )
    flat_index = route_slots(routes, CAP)
    feature_width = normed_pre.shape[1]
    slabs = (
        jnp.zeros((EXPERTS * CAP, feature_width), jnp.bfloat16)
        .at[flat_index]
        .set(jnp.repeat(normed_pre, TOP, axis=0))
        .reshape(EXPERTS, CAP, feature_width)
    )
    group_count = seq_count // shards
    block_rows, block_parts, gate_all, up_all, down_all = outbound(
        slabs, packed_parts, (w_gate, w_up, w_down), group_count, shards, tp_count, 1
    )
    weights = (
        gate_all.reshape(-1, gate_all.shape[-1]),
        up_all.reshape(-1, up_all.shape[-1]),
        jnp.transpose(down_all, (1, 0, 2)).reshape(down_all.shape[1], -1),
    )
    stage = merge_softmax(
        block_parts.reshape((-1,) + packed_parts.shape), request_count, flat_width
    )
    part_max = stage[0].reshape(request_count, heads_here)
    part_sum = stage[1].reshape(request_count, heads_here)
    part_acc = stage[2].reshape(request_count, heads_here, HD)
    own_key = keys_new.reshape(request_count, heads_here, HD).astype(jnp.float32)
    own_value = values_new.reshape(request_count, heads_here, HD).astype(jnp.float32)
    own_score = (
        jnp.sum(query_rows.astype(jnp.float32) * own_key, axis=-1) * score_scale
        + bias_here[0][None, :]
    )
    row_peak = jnp.maximum(part_max, own_score)
    keep_scale = jnp.exp(part_max - row_peak)
    own_weight = jnp.exp(own_score - row_peak)
    weight_total = part_sum * keep_scale + own_weight
    weighted = part_acc * keep_scale[..., None] + own_weight[..., None] * own_value
    mixed_rows = (
        (weighted / weight_total[..., None])
        .astype(jnp.bfloat16)
        .reshape(request_count, heads_width)
    )
    head_terms = jnp.dot(mixed_rows, out_proj, preferred_element_type=jnp.float32)
    (head_all,) = axis_share([head_terms], [False], "tp", tp_count, 1, 3)
    attended = jnp.sum(head_all, axis=0)
    decode_hidden = (decode_in.astype(jnp.float32) + attended).astype(jnp.bfloat16)
    normed_dec = rms_scale(decode_hidden, norm_gain)
    block_count = block_rows.shape[0] * block_rows.shape[1] * block_rows.shape[2]
    all_rows = jnp.concatenate([block_rows.reshape(block_count, feature_width), normed_dec], axis=0)
    all_out = expert_block(all_rows, weights)
    block_out = all_out[:block_count].reshape(block_rows.shape)
    dec_part = all_out[block_count:]
    part_rows, dec_block = axis_share(
        [block_out, dec_part], [True, False], "seq", shards, 1, 4
    )
    summed = jnp.zeros(part_rows.shape[1:], jnp.float32)
    dec_expert = jnp.zeros(dec_block.shape[1:], jnp.float32)
    for part in range(shards):
        summed = summed + part_rows[part].astype(jnp.float32)
        dec_expert = dec_expert + dec_block[part].astype(jnp.float32)
    my_expert = seq_index // shards
    gate_here = jnp.sum(jnp.where(dec_routes == my_expert, dec_gates, 0.0), axis=1)
    returned, dec_all = axis_share(
        [summed, gate_here[:, None] * dec_expert], [True, False], "seq", group_count, shards, 5
    )
    dec_terms = jnp.sum(dec_all, axis=0)
    decode_out = (decode_hidden.astype(jnp.float32) + dec_terms).astype(jnp.bfloat16)
    picked = jnp.take(returned.reshape(EXPERTS * CAP, -1), flat_index, axis=0)
    picked = picked.reshape(-1, TOP, picked.shape[-1])
    prefill_out = (
        prefill_in.astype(jnp.float32) + jnp.sum(gates[..., None] * picked, axis=1)
    ).astype(jnp.bfloat16)
    return (decode_out, prefill_out)


def solution(mesh):
    placed = (
        P(None, "tp"),
        P(None, "tp"),
        P(None, "tp"),
        P(None, "seq", "tp"),
        P(None, "seq", "tp"),
        P(None, "seq"),
        P(),
        P(),
        P("tp", None),
        P(),
        P(("seq", "tp"), None),
        P(("seq", "tp"), None),
        P(("seq", "tp"), None),
        P(),
        P(),
        P(),
        P("tp", "seq"),
        P("tp", "seq"),
        P("seq", "tp"),
    )
    return jax.shard_map(
        body, mesh=mesh, in_specs=placed, out_specs=(P(), P(("seq", "tp"), None)), check_vma=False
    )
```

```python
import functools
import math

import jax
import jax.numpy as jnp
from jax import lax
from jax.experimental import pallas as pl
from jax.experimental.pallas import tpu as pltpu
from jax.sharding import PartitionSpec as P

HD = 64
EXPERTS = 16
TOP = 2
CAP = 10


def peer_device(axis, peer):
    if axis == "seq":
        return (peer, lax.axis_index("tp"))
    return (lax.axis_index("seq"), peer)


def share_kernel(axis, count, stride, modes, *refs):
    width = len(modes)
    sources = refs[:width]
    landed = refs[width : 2 * width]
    send_sems = refs[2 * width : 3 * width]
    recv_sems = refs[3 * width :]
    index = lax.axis_index(axis)
    me = lax.rem(index // stride, count)
    base = index - me * stride

    def member(slot):
        return peer_device(axis, base + slot * stride)

    def piece(which, slot):
        return sources[which].at[slot] if modes[which] else sources[which]

    barrier = pltpu.get_barrier_semaphore()

    def greet(step, carry):
        pl.semaphore_signal(
            barrier,
            inc=1,
            device_id=member(lax.rem(me + step, count)),
            device_id_type=pl.DeviceIdType.MESH,
        )
        return carry

    lax.fori_loop(1, count, greet, 0)
    pl.semaphore_wait(barrier, count - 1)

    def outgoing(which, step):
        target = lax.rem(me + step, count)
        return pltpu.make_async_remote_copy(
            src_ref=piece(which, target),
            dst_ref=landed[which].at[me],
            send_sem=send_sems[which].at[step],
            recv_sem=recv_sems[which].at[step],
            device_id=member(target),
            device_id_type=pl.DeviceIdType.MESH,
        )

    def incoming(which, step):
        source = lax.rem(me - step + count, count)
        return pltpu.make_async_remote_copy(
            src_ref=piece(which, source),
            dst_ref=landed[which].at[source],
            send_sem=send_sems[which].at[step],
            recv_sem=recv_sems[which].at[step],
            device_id=member(source),
            device_id_type=pl.DeviceIdType.MESH,
        )

    def launch(step, carry):
        for which in range(width):
            outgoing(which, step).start()
        return carry

    lax.fori_loop(1, count, launch, 0)
    for which in range(width):
        landed[which][me] = piece(which, me)[...]

    def finish(step, carry):
        for which in range(width):
            outgoing(which, step).wait_send()
            incoming(which, step).wait_recv()
        return carry

    lax.fori_loop(1, count, finish, 0)


def axis_share(payloads, modes, axis, count, stride, collective_id):
    shapes = [x.shape if mode else (count,) + x.shape for x, mode in zip(payloads, modes)]
    width = len(payloads)
    return pl.pallas_call(
        functools.partial(share_kernel, axis, count, stride, tuple(modes)),
        out_shape=[jax.ShapeDtypeStruct(s, x.dtype) for s, x in zip(shapes, payloads)],
        in_specs=[pl.BlockSpec(memory_space=pltpu.VMEM)] * width,
        out_specs=[pl.BlockSpec(memory_space=pltpu.VMEM)] * width,
        scratch_shapes=[pltpu.SemaphoreType.DMA((count,))] * (2 * width),
        compiler_params=pltpu.CompilerParams(collective_id=collective_id, has_side_effects=True),
    )(*payloads)


def outbound_kernel(groups, shards, lanes, slab_ref, part_ref, gate_ref, up_ref, down_ref,
                    near_rows, near_parts, gate_all, up_all, down_all, far_parts,
                    far_send, far_recv, far_psend, far_precv,
                    near_send, near_recv, near_psend, near_precv, local_sem,
                    lane_send, lane_recv):
    index = lax.axis_index("seq")
    far_me = lax.rem(index // shards, groups)
    far_base = index - far_me * shards
    place = lax.rem(index, shards)
    near_base = index - place
    has_right = place < shards - 1
    has_left = place > 0

    def far_member(slot):
        return peer_device("seq", far_base + slot * shards)

    def near_member(slot):
        return peer_device("seq", near_base + slot)

    barrier = pltpu.get_barrier_semaphore()

    def greet_far(step, carry):
        pl.semaphore_signal(barrier, inc=1, device_id=far_member(lax.rem(far_me + step, groups)),
                            device_id_type=pl.DeviceIdType.MESH)
        return carry

    def greet_near(step, carry):
        pl.semaphore_signal(barrier, inc=1, device_id=near_member(lax.rem(place + step, shards)),
                            device_id_type=pl.DeviceIdType.MESH)
        return carry

    lane_me = lax.axis_index("tp")

    def lane_member(slot):
        return peer_device("tp", slot)

    def greet_lane(step, carry):
        pl.semaphore_signal(barrier, inc=1, device_id=lane_member(lax.rem(lane_me + step, lanes)),
                            device_id_type=pl.DeviceIdType.MESH)
        return carry

    lax.fori_loop(1, groups, greet_far, 0)
    lax.fori_loop(1, shards, greet_near, 0)
    lax.fori_loop(1, lanes, greet_lane, 0)
    pl.semaphore_wait(barrier, groups + shards + lanes - 3)
    weight_refs = ((gate_ref, gate_all), (up_ref, up_all), (down_ref, down_all))

    def lane_target(which, landed_slot):
        source_ref, landed_ref = weight_refs[which]
        if which == 2:
            return landed_ref.at[landed_slot]
        width = source_ref.shape[1]
        return landed_ref.at[:, pl.ds(pl.multiple_of(landed_slot * width, width), width)]

    def lane_copy(which, step, slot, landed_slot):
        source_ref, landed_ref = weight_refs[which]
        return pltpu.make_async_remote_copy(
            src_ref=source_ref, dst_ref=lane_target(which, landed_slot),
            send_sem=lane_send.at[which, step], recv_sem=lane_recv.at[which, step],
            device_id=lane_member(slot), device_id_type=pl.DeviceIdType.MESH)

    def lane_start(step, carry):
        for which in range(3):
            lane_copy(which, step, lax.rem(lane_me + step, lanes), lane_me).start()
        return carry


    def far_copy(step, slot, landed_slot):
        return (
            pltpu.make_async_remote_copy(
                src_ref=slab_ref.at[slot], dst_ref=near_rows.at[place, landed_slot],
                send_sem=far_send.at[step], recv_sem=far_recv.at[step],
                device_id=far_member(slot), device_id_type=pl.DeviceIdType.MESH),
            pltpu.make_async_remote_copy(
                src_ref=part_ref, dst_ref=far_parts.at[landed_slot],
                send_sem=far_psend.at[step], recv_sem=far_precv.at[step],
                device_id=far_member(slot), device_id_type=pl.DeviceIdType.MESH),
        )

    def far_start(step, carry):
        for copy in far_copy(step, lax.rem(far_me + step, groups), far_me):
            copy.start()
        return carry

    lax.fori_loop(1, groups, far_start, 0)
    own_slab = pltpu.make_async_copy(slab_ref.at[far_me], near_rows.at[place, far_me], local_sem.at[0])
    own_part = pltpu.make_async_copy(part_ref, far_parts.at[far_me], local_sem.at[1])
    own_slab.start()
    own_part.start()
    lax.fori_loop(1, lanes, lane_start, 0)
    own_weights = [
        pltpu.make_async_copy(source_ref, lane_target(which, lane_me), local_sem.at[3 + which])
        for which, (source_ref, landed_ref) in enumerate(weight_refs)
    ]
    for copy in own_weights:
        copy.start()

    def chain_copy(direction, origin, slab):
        return pltpu.make_async_remote_copy(
            src_ref=near_rows.at[origin, slab], dst_ref=near_rows.at[origin, slab],
            send_sem=near_send.at[direction, origin, slab], recv_sem=near_recv.at[origin, slab],
            device_id=near_member(place + 1 - 2 * direction), device_id_type=pl.DeviceIdType.MESH)

    def pass_on(origin, slab, to_right, to_left):
        @pl.when(to_right)
        def _():
            chain_copy(0, origin, slab).start()

        @pl.when(to_left)
        def _():
            chain_copy(1, origin, slab).start()

    own_slab.wait()
    pass_on(place, far_me, has_right, has_left)

    def far_finish(step, carry):
        source = lax.rem(far_me - step + groups, groups)
        rows_copy, parts_copy = far_copy(step, source, source)
        rows_copy.wait_send()
        rows_copy.wait_recv()
        pass_on(place, source, has_right, has_left)
        parts_copy.wait_send()
        parts_copy.wait_recv()
        return carry

    lax.fori_loop(1, groups, far_finish, 0)
    own_part.wait()
    own_parts = pltpu.make_async_copy(far_parts, near_parts.at[place], local_sem.at[2])
    own_parts.start()

    def near_parts_copy(step, slot):
        return pltpu.make_async_remote_copy(
            src_ref=far_parts, dst_ref=near_parts.at[slot],
            send_sem=near_psend.at[step], recv_sem=near_precv.at[step],
            device_id=near_member(lax.rem(place + step, shards)),
            device_id_type=pl.DeviceIdType.MESH)

    for step in range(1, shards):
        near_parts_copy(step, place).start()

    for distance in range(1, shards):
        def relay(slab, carry, distance=distance):
            from_left = place - distance
            from_right = place + distance

            @pl.when(from_left >= 0)
            def _():
                chain_copy(0, from_left, slab).wait_recv()
                pass_on(from_left, slab, has_right, False)

            @pl.when(from_right < shards)
            def _():
                chain_copy(1, from_right, slab).wait_recv()
                pass_on(from_right, slab, False, has_left)

            return carry

        lax.fori_loop(0, groups, relay, 0)

    for origin in range(shards):
        def drain(slab, carry, origin=origin):
            @pl.when((origin <= place) & has_right)
            def _():
                chain_copy(0, origin, slab).wait_send()

            @pl.when((origin >= place) & has_left)
            def _():
                chain_copy(1, origin, slab).wait_send()

            return carry

        lax.fori_loop(0, groups, drain, 0)

    def parts_finish(step, carry):
        parts_copy = near_parts_copy(step, lax.rem(place - step + shards, shards))
        parts_copy.wait_send()
        parts_copy.wait_recv()
        return carry

    lax.fori_loop(1, shards, parts_finish, 0)
    own_parts.wait()

    def lane_finish(step, carry):
        source = lax.rem(lane_me - step + lanes, lanes)
        for which in range(3):
            copy = lane_copy(which, step, source, source)
            copy.wait_send()
            copy.wait_recv()
        return carry

    lax.fori_loop(1, lanes, lane_finish, 0)
    for copy in own_weights:
        copy.wait()


def outbound(slabs, parts, weights, groups, shards, lanes, collective_id):
    rows_shape = (shards,) + slabs.shape
    parts_shape = (shards, groups) + parts.shape
    weight_shapes = [
        jax.ShapeDtypeStruct((w.shape[0], lanes * w.shape[1]), w.dtype) for w in weights[:2]
    ] + [jax.ShapeDtypeStruct((lanes,) + weights[2].shape, weights[2].dtype)]
    return pl.pallas_call(
        functools.partial(outbound_kernel, groups, shards, lanes),
        out_shape=[jax.ShapeDtypeStruct(rows_shape, slabs.dtype),
                   jax.ShapeDtypeStruct(parts_shape, parts.dtype)] + weight_shapes,
        in_specs=[pl.BlockSpec(memory_space=pltpu.VMEM)] * 5,
        out_specs=[pl.BlockSpec(memory_space=pltpu.VMEM)] * 5,
        scratch_shapes=[pltpu.VMEM((groups,) + parts.shape, parts.dtype)]
        + [pltpu.SemaphoreType.DMA((groups,))] * 4
        + [pltpu.SemaphoreType.DMA((2, shards, groups)), pltpu.SemaphoreType.DMA((shards, groups))]
        + [pltpu.SemaphoreType.DMA((shards,))] * 2
        + [pltpu.SemaphoreType.DMA((8,))]
        + [pltpu.SemaphoreType.DMA((3, lanes))] * 2,
        compiler_params=pltpu.CompilerParams(collective_id=collective_id, has_side_effects=True),
    )(slabs, parts, *weights)


def merge_softmax(stacked, rows, width):
    slot_max = stacked[:, rows, :width]
    slot_sum = stacked[:, rows + 1, :width]
    joint_max = jnp.max(slot_max, axis=0)
    slot_scale = jnp.exp(slot_max - joint_max[None])
    joint_sum = jnp.sum(slot_sum * slot_scale, axis=0)
    lane_scale = jnp.repeat(slot_scale.reshape(slot_scale.shape[0], rows, -1), HD, axis=2)
    joint_acc = jnp.sum(stacked[:, :rows, :] * lane_scale, axis=0)
    return joint_max, joint_sum, joint_acc


def pack_softmax(joint_max, joint_sum, joint_acc):
    rows, lanes = joint_acc.shape
    stats = jnp.stack([joint_max, joint_sum])
    return jnp.concatenate([joint_acc, jnp.pad(stats, ((0, 2), (0, lanes - stats.shape[1])))], axis=0)


def rms_scale(hidden, norm_gain):
    values = hidden.astype(jnp.float32)
    meansq = jnp.mean(values * values, axis=-1, keepdims=True)
    return (values * lax.rsqrt(meansq + 1e-06) * norm_gain).astype(jnp.bfloat16)


def route_slots(route_rows, capacity):
    flat_routes = route_rows.reshape(-1)
    onehot = (flat_routes[:, None] == jnp.arange(EXPERTS, dtype=jnp.int32)[None, :]).astype(
        jnp.int32
    )
    earlier = jnp.cumsum(onehot, axis=0) - onehot
    slot_rank = jnp.sum(earlier * onehot, axis=1)
    return flat_routes * capacity + slot_rank


def expert_block(row_block, weights):
    gate_full, up_full, down_full = weights
    gate_pre = jnp.dot(row_block, gate_full, preferred_element_type=jnp.float32)
    up_pre = jnp.dot(row_block, up_full, preferred_element_type=jnp.float32)
    act = (jax.nn.gelu(gate_pre, approximate=True) * up_pre).astype(jnp.bfloat16)
    return jnp.dot(act, down_full, preferred_element_type=jnp.float32).astype(jnp.bfloat16)


def body(
    queries,
    keys_new,
    values_new,
    key_cache,
    value_cache,
    buckets,
    lengths,
    bias_table,
    out_proj,
    decode_in,
    prefill_in,
    routes,
    gates,
    dec_routes,
    dec_gates,
    norm_gain,
    w_gate,
    w_up,
    w_down,
):
    seq_count = lax.axis_size("seq")
    seq_index = lax.axis_index("seq")
    tp_index = lax.axis_index("tp")
    shards = seq_count // EXPERTS
    normed_pre = rms_scale(prefill_in, norm_gain)
    request_count, heads_width = queries.shape
    heads_here = heads_width // HD
    ctx_local = key_cache.shape[1]
    score_scale = 1.0 / math.sqrt(HD)
    query_rows = queries.reshape(request_count, heads_here, HD)
    key_rows = key_cache.reshape(request_count, ctx_local, heads_here, HD)
    value_rows = value_cache.reshape(request_count, ctx_local, heads_here, HD).astype(jnp.float32)
    bias_here = lax.dynamic_slice_in_dim(bias_table, tp_index * heads_here, heads_here, 1)
    bucket_hot = (
        buckets[..., None] == jnp.arange(bias_table.shape[0], dtype=jnp.int32)[None, None, :]
    ).astype(jnp.float32)
    bias_rows = jnp.einsum("rcn,nh->rhc", bucket_hot, bias_here, precision=lax.Precision.HIGHEST)
    cache_scores = (
        jnp.einsum("rhd,rchd->rhc", query_rows, key_rows, preferred_element_type=jnp.float32)
        * score_scale
        + bias_rows
    )
    positions = seq_index * ctx_local + jnp.arange(ctx_local, dtype=jnp.int32)
    valid_mask = (positions[None, :] < lengths[:, None])[:, None, :]
    cache_scores = jnp.where(valid_mask, cache_scores, -1e30)
    local_max = jnp.max(cache_scores, axis=-1)
    local_weights = jnp.where(valid_mask, jnp.exp(cache_scores - local_max[..., None]), 0.0)
    local_sum = jnp.sum(local_weights, axis=-1)
    local_acc = jnp.einsum(
        "rhc,rchd->rhd", local_weights, value_rows, precision=lax.Precision.HIGHEST
    )
    tp_count = lax.axis_size("tp")
    flat_width = request_count * heads_here
    packed_parts = pack_softmax(
        local_max.reshape(-1), local_sum.reshape(-1), local_acc.reshape(request_count, heads_here * HD)
    )
    flat_index = route_slots(routes, CAP)
    feature_width = normed_pre.shape[1]
    slabs = (
        jnp.zeros((EXPERTS * CAP, feature_width), jnp.bfloat16)
        .at[flat_index]
        .set(jnp.repeat(normed_pre, TOP, axis=0))
        .reshape(EXPERTS, CAP, feature_width)
    )
    group_count = seq_count // shards
    block_rows, block_parts, gate_all, up_all, down_all = outbound(
        slabs, packed_parts, (w_gate.T, w_up.T, w_down), group_count, shards, tp_count, 1
    )
    weights = (
        gate_all.T,
        up_all.T,
        jnp.transpose(down_all, (1, 0, 2)).reshape(down_all.shape[1], -1),
    )
    stage = merge_softmax(
        block_parts.reshape((-1,) + packed_parts.shape), request_count, flat_width
    )
    part_max = stage[0].reshape(request_count, heads_here)
    part_sum = stage[1].reshape(request_count, heads_here)
    part_acc = stage[2].reshape(request_count, heads_here, HD)
    own_key = keys_new.reshape(request_count, heads_here, HD).astype(jnp.float32)
    own_value = values_new.reshape(request_count, heads_here, HD).astype(jnp.float32)
    own_score = (
        jnp.sum(query_rows.astype(jnp.float32) * own_key, axis=-1) * score_scale
        + bias_here[0][None, :]
    )
    row_peak = jnp.maximum(part_max, own_score)
    keep_scale = jnp.exp(part_max - row_peak)
    own_weight = jnp.exp(own_score - row_peak)
    weight_total = part_sum * keep_scale + own_weight
    weighted = part_acc * keep_scale[..., None] + own_weight[..., None] * own_value
    mixed_rows = (
        (weighted / weight_total[..., None])
        .astype(jnp.bfloat16)
        .reshape(request_count, heads_width)
    )
    head_terms = jnp.dot(mixed_rows, out_proj, preferred_element_type=jnp.float32)
    (head_all,) = axis_share([head_terms], [False], "tp", tp_count, 1, 3)
    attended = jnp.sum(head_all, axis=0)
    decode_hidden = (decode_in.astype(jnp.float32) + attended).astype(jnp.bfloat16)
    normed_dec = rms_scale(decode_hidden, norm_gain)
    block_count = block_rows.shape[0] * block_rows.shape[1] * block_rows.shape[2]
    all_rows = jnp.concatenate([block_rows.reshape(block_count, feature_width), normed_dec], axis=0)
    all_out = expert_block(all_rows, weights)
    block_out = all_out[:block_count].reshape(block_rows.shape)
    dec_part = all_out[block_count:]
    part_rows, dec_block = axis_share(
        [block_out, dec_part], [True, False], "seq", shards, 1, 4
    )
    summed = jnp.zeros(part_rows.shape[1:], jnp.float32)
    dec_expert = jnp.zeros(dec_block.shape[1:], jnp.float32)
    for part in range(shards):
        summed = summed + part_rows[part].astype(jnp.float32)
        dec_expert = dec_expert + dec_block[part].astype(jnp.float32)
    my_expert = seq_index // shards
    gate_here = jnp.sum(jnp.where(dec_routes == my_expert, dec_gates, 0.0), axis=1)
    returned, dec_all = axis_share(
        [summed, gate_here[:, None] * dec_expert], [True, False], "seq", group_count, shards, 5
    )
    dec_terms = jnp.sum(dec_all, axis=0)
    decode_out = (decode_hidden.astype(jnp.float32) + dec_terms).astype(jnp.bfloat16)
    picked = jnp.take(returned.reshape(EXPERTS * CAP, -1), flat_index, axis=0)
    picked = picked.reshape(-1, TOP, picked.shape[-1])
    prefill_out = (
        prefill_in.astype(jnp.float32) + jnp.sum(gates[..., None] * picked, axis=1)
    ).astype(jnp.bfloat16)
    return (decode_out, prefill_out)


def solution(mesh):
    placed = (
        P(None, "tp"),
        P(None, "tp"),
        P(None, "tp"),
        P(None, "seq", "tp"),
        P(None, "seq", "tp"),
        P(None, "seq"),
        P(),
        P(),
        P("tp", None),
        P(),
        P(("seq", "tp"), None),
        P(("seq", "tp"), None),
        P(("seq", "tp"), None),
        P(),
        P(),
        P(),
        P("tp", "seq"),
        P("tp", "seq"),
        P("seq", "tp"),
    )
    return jax.shard_map(
        body, mesh=mesh, in_specs=placed, out_specs=(P(), P(("seq", "tp"), None)), check_vma=False
    )
```

```python
import functools
import math

import jax
import jax.numpy as jnp
from jax import lax
from jax.experimental import pallas as pl
from jax.experimental.pallas import tpu as pltpu
from jax.sharding import PartitionSpec as P

HD = 64
EXPERTS = 16
TOP = 2
CAP = 10


def peer_device(axis, peer):
    if axis == "seq":
        return (peer, lax.axis_index("tp"))
    return (lax.axis_index("seq"), peer)


def share_kernel(axis, count, stride, modes, *refs):
    width = len(modes)
    sources = refs[:width]
    landed = refs[width : 2 * width]
    send_sems = refs[2 * width : 3 * width]
    recv_sems = refs[3 * width :]
    index = lax.axis_index(axis)
    me = lax.rem(index // stride, count)
    base = index - me * stride

    def member(slot):
        return peer_device(axis, base + slot * stride)

    def piece(which, slot):
        return sources[which].at[slot] if modes[which] else sources[which]

    barrier = pltpu.get_barrier_semaphore()

    def greet(step, carry):
        pl.semaphore_signal(
            barrier,
            inc=1,
            device_id=member(lax.rem(me + step, count)),
            device_id_type=pl.DeviceIdType.MESH,
        )
        return carry

    lax.fori_loop(1, count, greet, 0)
    pl.semaphore_wait(barrier, count - 1)

    def outgoing(which, step):
        target = lax.rem(me + step, count)
        return pltpu.make_async_remote_copy(
            src_ref=piece(which, target),
            dst_ref=landed[which].at[me],
            send_sem=send_sems[which].at[step],
            recv_sem=recv_sems[which].at[step],
            device_id=member(target),
            device_id_type=pl.DeviceIdType.MESH,
        )

    def incoming(which, step):
        source = lax.rem(me - step + count, count)
        return pltpu.make_async_remote_copy(
            src_ref=piece(which, source),
            dst_ref=landed[which].at[source],
            send_sem=send_sems[which].at[step],
            recv_sem=recv_sems[which].at[step],
            device_id=member(source),
            device_id_type=pl.DeviceIdType.MESH,
        )

    def launch(step, carry):
        for which in range(width):
            outgoing(which, step).start()
        return carry

    lax.fori_loop(1, count, launch, 0)
    for which in range(width):
        landed[which][me] = piece(which, me)[...]

    def finish(step, carry):
        for which in range(width):
            outgoing(which, step).wait_send()
            incoming(which, step).wait_recv()
        return carry

    lax.fori_loop(1, count, finish, 0)


def axis_share(payloads, modes, axis, count, stride, collective_id):
    shapes = [x.shape if mode else (count,) + x.shape for x, mode in zip(payloads, modes)]
    width = len(payloads)
    return pl.pallas_call(
        functools.partial(share_kernel, axis, count, stride, tuple(modes)),
        out_shape=[jax.ShapeDtypeStruct(s, x.dtype) for s, x in zip(shapes, payloads)],
        in_specs=[pl.BlockSpec(memory_space=pltpu.VMEM)] * width,
        out_specs=[pl.BlockSpec(memory_space=pltpu.VMEM)] * width,
        scratch_shapes=[pltpu.SemaphoreType.DMA((count,))] * (2 * width),
        compiler_params=pltpu.CompilerParams(collective_id=collective_id, has_side_effects=True),
    )(*payloads)


def outbound_kernel(groups, shards, lanes, slab_ref, part_ref, gate_ref, up_ref, down_ref,
                    near_rows, near_parts, gate_all, up_all, down_all, far_parts,
                    far_send, far_recv, far_psend, far_precv,
                    near_send, near_recv, near_psend, near_precv, local_sem,
                    lane_send, lane_recv):
    index = lax.axis_index("seq")
    far_me = lax.rem(index // shards, groups)
    far_base = index - far_me * shards
    place = lax.rem(index, shards)
    near_base = index - place
    has_right = place < shards - 1
    has_left = place > 0

    def far_member(slot):
        return peer_device("seq", far_base + slot * shards)

    def near_member(slot):
        return peer_device("seq", near_base + slot)

    barrier = pltpu.get_barrier_semaphore()

    def greet_far(step, carry):
        pl.semaphore_signal(barrier, inc=1, device_id=far_member(lax.rem(far_me + step, groups)),
                            device_id_type=pl.DeviceIdType.MESH)
        return carry

    def greet_near(step, carry):
        pl.semaphore_signal(barrier, inc=1, device_id=near_member(lax.rem(place + step, shards)),
                            device_id_type=pl.DeviceIdType.MESH)
        return carry

    lane_me = lax.axis_index("tp")

    def lane_member(slot):
        return peer_device("tp", slot)

    def greet_lane(step, carry):
        pl.semaphore_signal(barrier, inc=1, device_id=lane_member(lax.rem(lane_me + step, lanes)),
                            device_id_type=pl.DeviceIdType.MESH)
        return carry

    lax.fori_loop(1, groups, greet_far, 0)
    lax.fori_loop(1, shards, greet_near, 0)
    lax.fori_loop(1, lanes, greet_lane, 0)
    pl.semaphore_wait(barrier, groups + shards + lanes - 3)
    weight_refs = ((gate_ref, gate_all), (up_ref, up_all), (down_ref, down_all))

    def lane_target(which, landed_slot):
        source_ref, landed_ref = weight_refs[which]
        if which == 2:
            return landed_ref.at[landed_slot]
        width = source_ref.shape[1]
        return landed_ref.at[:, pl.ds(pl.multiple_of(landed_slot * width, width), width)]

    def lane_copy(which, step, slot, landed_slot):
        source_ref, landed_ref = weight_refs[which]
        return pltpu.make_async_remote_copy(
            src_ref=source_ref, dst_ref=lane_target(which, landed_slot),
            send_sem=lane_send.at[which, step], recv_sem=lane_recv.at[which, step],
            device_id=lane_member(slot), device_id_type=pl.DeviceIdType.MESH)

    def lane_start(step, carry):
        for which in range(3):
            lane_copy(which, step, lax.rem(lane_me + step, lanes), lane_me).start()
        return carry


    def far_copy(step, slot, landed_slot):
        return (
            pltpu.make_async_remote_copy(
                src_ref=slab_ref.at[slot], dst_ref=near_rows.at[place, landed_slot],
                send_sem=far_send.at[step], recv_sem=far_recv.at[step],
                device_id=far_member(slot), device_id_type=pl.DeviceIdType.MESH),
            pltpu.make_async_remote_copy(
                src_ref=part_ref, dst_ref=far_parts.at[landed_slot],
                send_sem=far_psend.at[step], recv_sem=far_precv.at[step],
                device_id=far_member(slot), device_id_type=pl.DeviceIdType.MESH),
        )

    def far_start(step, carry):
        for copy in far_copy(step, lax.rem(far_me + step, groups), far_me):
            copy.start()
        return carry

    lax.fori_loop(1, groups, far_start, 0)
    own_slab = pltpu.make_async_copy(slab_ref.at[far_me], near_rows.at[place, far_me], local_sem.at[0])
    own_part = pltpu.make_async_copy(part_ref, far_parts.at[far_me], local_sem.at[1])
    own_slab.start()
    own_part.start()
    lax.fori_loop(1, lanes, lane_start, 0)
    own_weights = [
        pltpu.make_async_copy(source_ref, lane_target(which, lane_me), local_sem.at[3 + which])
        for which, (source_ref, landed_ref) in enumerate(weight_refs)
    ]
    for copy in own_weights:
        copy.start()

    def chain_copy(direction, origin, slab):
        return pltpu.make_async_remote_copy(
            src_ref=near_rows.at[origin, slab], dst_ref=near_rows.at[origin, slab],
            send_sem=near_send.at[direction, origin, slab], recv_sem=near_recv.at[origin, slab],
            device_id=near_member(place + 1 - 2 * direction), device_id_type=pl.DeviceIdType.MESH)

    def pass_on(origin, slab, to_right, to_left):
        @pl.when(to_right)
        def _():
            chain_copy(0, origin, slab).start()

        @pl.when(to_left)
        def _():
            chain_copy(1, origin, slab).start()

    own_slab.wait()
    pass_on(place, far_me, has_right, has_left)

    def far_finish(step, carry):
        source = lax.rem(far_me - step + groups, groups)
        rows_copy, parts_copy = far_copy(step, source, source)
        rows_copy.wait_send()
        rows_copy.wait_recv()
        pass_on(place, source, has_right, has_left)
        parts_copy.wait_send()
        parts_copy.wait_recv()
        return carry

    lax.fori_loop(1, groups, far_finish, 0)
    own_part.wait()
    own_parts = pltpu.make_async_copy(far_parts, near_parts.at[place], local_sem.at[2])
    own_parts.start()

    def near_parts_copy(step, slot):
        return pltpu.make_async_remote_copy(
            src_ref=far_parts, dst_ref=near_parts.at[slot],
            send_sem=near_psend.at[step], recv_sem=near_precv.at[step],
            device_id=near_member(lax.rem(place + step, shards)),
            device_id_type=pl.DeviceIdType.MESH)

    for step in range(1, shards):
        near_parts_copy(step, place).start()

    for distance in range(1, shards):
        def relay(slab, carry, distance=distance):
            from_left = place - distance
            from_right = place + distance

            @pl.when(from_left >= 0)
            def _():
                chain_copy(0, from_left, slab).wait_recv()
                pass_on(from_left, slab, has_right, False)

            @pl.when(from_right < shards)
            def _():
                chain_copy(1, from_right, slab).wait_recv()
                pass_on(from_right, slab, False, has_left)

            return carry

        lax.fori_loop(0, groups, relay, 0)

    for origin in range(shards):
        def drain(slab, carry, origin=origin):
            @pl.when((origin <= place) & has_right)
            def _():
                chain_copy(0, origin, slab).wait_send()

            @pl.when((origin >= place) & has_left)
            def _():
                chain_copy(1, origin, slab).wait_send()

            return carry

        lax.fori_loop(0, groups, drain, 0)

    def parts_finish(step, carry):
        parts_copy = near_parts_copy(step, lax.rem(place - step + shards, shards))
        parts_copy.wait_send()
        parts_copy.wait_recv()
        return carry

    lax.fori_loop(1, shards, parts_finish, 0)
    own_parts.wait()

    def lane_finish(step, carry):
        source = lax.rem(lane_me - step + lanes, lanes)
        for which in range(3):
            copy = lane_copy(which, step, source, source)
            copy.wait_send()
            copy.wait_recv()
        return carry

    lax.fori_loop(1, lanes, lane_finish, 0)
    for copy in own_weights:
        copy.wait()


def outbound(slabs, parts, weights, groups, shards, lanes, collective_id):
    rows_shape = (shards,) + slabs.shape
    parts_shape = (shards, groups) + parts.shape
    weight_shapes = [
        jax.ShapeDtypeStruct((w.shape[0], lanes * w.shape[1]), w.dtype) for w in weights[:2]
    ] + [jax.ShapeDtypeStruct((lanes,) + weights[2].shape, weights[2].dtype)]
    return pl.pallas_call(
        functools.partial(outbound_kernel, groups, shards, lanes),
        out_shape=[jax.ShapeDtypeStruct(rows_shape, slabs.dtype),
                   jax.ShapeDtypeStruct(parts_shape, parts.dtype)] + weight_shapes,
        in_specs=[pl.BlockSpec(memory_space=pltpu.VMEM)] * 5,
        out_specs=[pl.BlockSpec(memory_space=pltpu.VMEM)] * 2
        + [pl.BlockSpec(memory_space=pl.ANY)] * 3,
        scratch_shapes=[pltpu.VMEM((groups,) + parts.shape, parts.dtype)]
        + [pltpu.SemaphoreType.DMA((groups,))] * 4
        + [pltpu.SemaphoreType.DMA((2, shards, groups)), pltpu.SemaphoreType.DMA((shards, groups))]
        + [pltpu.SemaphoreType.DMA((shards,))] * 2
        + [pltpu.SemaphoreType.DMA((8,))]
        + [pltpu.SemaphoreType.DMA((3, lanes))] * 2,
        compiler_params=pltpu.CompilerParams(collective_id=collective_id, has_side_effects=True),
    )(slabs, parts, *weights)


def merge_softmax(stacked, rows, width):
    slot_max = stacked[:, rows, :width]
    slot_sum = stacked[:, rows + 1, :width]
    joint_max = jnp.max(slot_max, axis=0)
    slot_scale = jnp.exp(slot_max - joint_max[None])
    joint_sum = jnp.sum(slot_sum * slot_scale, axis=0)
    lane_scale = jnp.repeat(slot_scale.reshape(slot_scale.shape[0], rows, -1), HD, axis=2)
    joint_acc = jnp.sum(stacked[:, :rows, :] * lane_scale, axis=0)
    return joint_max, joint_sum, joint_acc


def pack_softmax(joint_max, joint_sum, joint_acc):
    rows, lanes = joint_acc.shape
    stats = jnp.stack([joint_max, joint_sum])
    return jnp.concatenate([joint_acc, jnp.pad(stats, ((0, 2), (0, lanes - stats.shape[1])))], axis=0)


def rms_scale(hidden, norm_gain):
    values = hidden.astype(jnp.float32)
    meansq = jnp.mean(values * values, axis=-1, keepdims=True)
    return (values * lax.rsqrt(meansq + 1e-06) * norm_gain).astype(jnp.bfloat16)


def route_slots(route_rows, capacity):
    flat_routes = route_rows.reshape(-1)
    onehot = (flat_routes[:, None] == jnp.arange(EXPERTS, dtype=jnp.int32)[None, :]).astype(
        jnp.int32
    )
    earlier = jnp.cumsum(onehot, axis=0) - onehot
    slot_rank = jnp.sum(earlier * onehot, axis=1)
    return flat_routes * capacity + slot_rank


def expert_block(row_block, weights):
    gate_full, up_full, down_full = weights
    gate_pre = jnp.dot(row_block, gate_full, preferred_element_type=jnp.float32)
    up_pre = jnp.dot(row_block, up_full, preferred_element_type=jnp.float32)
    act = (jax.nn.gelu(gate_pre, approximate=True) * up_pre).astype(jnp.bfloat16)
    return jnp.dot(act, down_full, preferred_element_type=jnp.float32).astype(jnp.bfloat16)


def body(
    queries,
    keys_new,
    values_new,
    key_cache,
    value_cache,
    buckets,
    lengths,
    bias_table,
    out_proj,
    decode_in,
    prefill_in,
    routes,
    gates,
    dec_routes,
    dec_gates,
    norm_gain,
    w_gate,
    w_up,
    w_down,
):
    seq_count = lax.axis_size("seq")
    seq_index = lax.axis_index("seq")
    tp_index = lax.axis_index("tp")
    shards = seq_count // EXPERTS
    normed_pre = rms_scale(prefill_in, norm_gain)
    request_count, heads_width = queries.shape
    heads_here = heads_width // HD
    ctx_local = key_cache.shape[1]
    score_scale = 1.0 / math.sqrt(HD)
    query_rows = queries.reshape(request_count, heads_here, HD)
    key_rows = key_cache.reshape(request_count, ctx_local, heads_here, HD)
    value_rows = value_cache.reshape(request_count, ctx_local, heads_here, HD).astype(jnp.float32)
    bias_here = lax.dynamic_slice_in_dim(bias_table, tp_index * heads_here, heads_here, 1)
    bucket_hot = (
        buckets[..., None] == jnp.arange(bias_table.shape[0], dtype=jnp.int32)[None, None, :]
    ).astype(jnp.float32)
    bias_rows = jnp.einsum("rcn,nh->rhc", bucket_hot, bias_here, precision=lax.Precision.HIGHEST)
    cache_scores = (
        jnp.einsum("rhd,rchd->rhc", query_rows, key_rows, preferred_element_type=jnp.float32)
        * score_scale
        + bias_rows
    )
    positions = seq_index * ctx_local + jnp.arange(ctx_local, dtype=jnp.int32)
    valid_mask = (positions[None, :] < lengths[:, None])[:, None, :]
    cache_scores = jnp.where(valid_mask, cache_scores, -1e30)
    local_max = jnp.max(cache_scores, axis=-1)
    local_weights = jnp.where(valid_mask, jnp.exp(cache_scores - local_max[..., None]), 0.0)
    local_sum = jnp.sum(local_weights, axis=-1)
    local_acc = jnp.einsum(
        "rhc,rchd->rhd", local_weights, value_rows, precision=lax.Precision.HIGHEST
    )
    tp_count = lax.axis_size("tp")
    flat_width = request_count * heads_here
    packed_parts = pack_softmax(
        local_max.reshape(-1), local_sum.reshape(-1), local_acc.reshape(request_count, heads_here * HD)
    )
    flat_index = route_slots(routes, CAP)
    feature_width = normed_pre.shape[1]
    slabs = (
        jnp.zeros((EXPERTS * CAP, feature_width), jnp.bfloat16)
        .at[flat_index]
        .set(jnp.repeat(normed_pre, TOP, axis=0))
        .reshape(EXPERTS, CAP, feature_width)
    )
    group_count = seq_count // shards
    block_rows, block_parts, gate_all, up_all, down_all = outbound(
        slabs, packed_parts, (w_gate.T, w_up.T, w_down), group_count, shards, tp_count, 1
    )
    weights = (
        gate_all.T,
        up_all.T,
        jnp.transpose(down_all, (1, 0, 2)).reshape(down_all.shape[1], -1),
    )
    stage = merge_softmax(
        block_parts.reshape((-1,) + packed_parts.shape), request_count, flat_width
    )
    part_max = stage[0].reshape(request_count, heads_here)
    part_sum = stage[1].reshape(request_count, heads_here)
    part_acc = stage[2].reshape(request_count, heads_here, HD)
    own_key = keys_new.reshape(request_count, heads_here, HD).astype(jnp.float32)
    own_value = values_new.reshape(request_count, heads_here, HD).astype(jnp.float32)
    own_score = (
        jnp.sum(query_rows.astype(jnp.float32) * own_key, axis=-1) * score_scale
        + bias_here[0][None, :]
    )
    row_peak = jnp.maximum(part_max, own_score)
    keep_scale = jnp.exp(part_max - row_peak)
    own_weight = jnp.exp(own_score - row_peak)
    weight_total = part_sum * keep_scale + own_weight
    weighted = part_acc * keep_scale[..., None] + own_weight[..., None] * own_value
    mixed_rows = (
        (weighted / weight_total[..., None])
        .astype(jnp.bfloat16)
        .reshape(request_count, heads_width)
    )
    head_terms = jnp.dot(mixed_rows, out_proj, preferred_element_type=jnp.float32)
    (head_all,) = axis_share([head_terms], [False], "tp", tp_count, 1, 3)
    attended = jnp.sum(head_all, axis=0)
    decode_hidden = (decode_in.astype(jnp.float32) + attended).astype(jnp.bfloat16)
    normed_dec = rms_scale(decode_hidden, norm_gain)
    block_count = block_rows.shape[0] * block_rows.shape[1] * block_rows.shape[2]
    all_rows = jnp.concatenate([block_rows.reshape(block_count, feature_width), normed_dec], axis=0)
    all_out = expert_block(all_rows, weights)
    block_out = all_out[:block_count].reshape(block_rows.shape)
    dec_part = all_out[block_count:]
    part_rows, dec_block = axis_share(
        [block_out, dec_part], [True, False], "seq", shards, 1, 4
    )
    summed = jnp.zeros(part_rows.shape[1:], jnp.float32)
    dec_expert = jnp.zeros(dec_block.shape[1:], jnp.float32)
    for part in range(shards):
        summed = summed + part_rows[part].astype(jnp.float32)
        dec_expert = dec_expert + dec_block[part].astype(jnp.float32)
    my_expert = seq_index // shards
    gate_here = jnp.sum(jnp.where(dec_routes == my_expert, dec_gates, 0.0), axis=1)
    returned, dec_all = axis_share(
        [summed, gate_here[:, None] * dec_expert], [True, False], "seq", group_count, shards, 5
    )
    dec_terms = jnp.sum(dec_all, axis=0)
    decode_out = (decode_hidden.astype(jnp.float32) + dec_terms).astype(jnp.bfloat16)
    picked = jnp.take(returned.reshape(EXPERTS * CAP, -1), flat_index, axis=0)
    picked = picked.reshape(-1, TOP, picked.shape[-1])
    prefill_out = (
        prefill_in.astype(jnp.float32) + jnp.sum(gates[..., None] * picked, axis=1)
    ).astype(jnp.bfloat16)
    return (decode_out, prefill_out)


def solution(mesh):
    placed = (
        P(None, "tp"),
        P(None, "tp"),
        P(None, "tp"),
        P(None, "seq", "tp"),
        P(None, "seq", "tp"),
        P(None, "seq"),
        P(),
        P(),
        P("tp", None),
        P(),
        P(("seq", "tp"), None),
        P(("seq", "tp"), None),
        P(("seq", "tp"), None),
        P(),
        P(),
        P(),
        P("tp", "seq"),
        P("tp", "seq"),
        P("seq", "tp"),
    )
    return jax.shard_map(
        body, mesh=mesh, in_specs=placed, out_specs=(P(), P(("seq", "tp"), None)), check_vma=False
    )
```

```python
import functools
import math

import jax
import jax.numpy as jnp
from jax import lax
from jax.experimental import pallas as pl
from jax.experimental.pallas import tpu as pltpu
from jax.sharding import PartitionSpec as P

HD = 64
EXPERTS = 16
TOP = 2
CAP = 10


def peer_device(axis, peer):
    if axis == "seq":
        return (peer, lax.axis_index("tp"))
    return (lax.axis_index("seq"), peer)


def share_kernel(axis, count, stride, modes, *refs):
    width = len(modes)
    sources = refs[:width]
    landed = refs[width : 2 * width]
    send_sems = refs[2 * width : 3 * width]
    recv_sems = refs[3 * width : 4 * width]
    own_sem = refs[4 * width]
    index = lax.axis_index(axis)
    me = lax.rem(index // stride, count)
    base = index - me * stride

    def member(slot):
        return peer_device(axis, base + slot * stride)

    def piece(which, slot):
        return sources[which].at[slot] if modes[which] else sources[which]

    barrier = pltpu.get_barrier_semaphore()

    def greet(step, carry):
        pl.semaphore_signal(
            barrier,
            inc=1,
            device_id=member(lax.rem(me + step, count)),
            device_id_type=pl.DeviceIdType.MESH,
        )
        return carry

    lax.fori_loop(1, count, greet, 0)
    pl.semaphore_wait(barrier, count - 1)

    def outgoing(which, step):
        target = lax.rem(me + step, count)
        return pltpu.make_async_remote_copy(
            src_ref=piece(which, target),
            dst_ref=landed[which].at[me],
            send_sem=send_sems[which].at[step],
            recv_sem=recv_sems[which].at[step],
            device_id=member(target),
            device_id_type=pl.DeviceIdType.MESH,
        )

    def incoming(which, step):
        source = lax.rem(me - step + count, count)
        return pltpu.make_async_remote_copy(
            src_ref=piece(which, source),
            dst_ref=landed[which].at[source],
            send_sem=send_sems[which].at[step],
            recv_sem=recv_sems[which].at[step],
            device_id=member(source),
            device_id_type=pl.DeviceIdType.MESH,
        )

    def launch(step, carry):
        for which in range(width):
            outgoing(which, step).start()
        return carry

    lax.fori_loop(1, count, launch, 0)
    own_copies = [
        pltpu.make_async_copy(piece(which, me), landed[which].at[me], own_sem.at[which])
        for which in range(width)
    ]
    for copy in own_copies:
        copy.start()

    def finish(step, carry):
        for which in range(width):
            outgoing(which, step).wait_send()
            incoming(which, step).wait_recv()
        return carry

    lax.fori_loop(1, count, finish, 0)
    for copy in own_copies:
        copy.wait()


def axis_share(payloads, modes, axis, count, stride, collective_id):
    shapes = [x.shape if mode else (count,) + x.shape for x, mode in zip(payloads, modes)]
    width = len(payloads)
    return pl.pallas_call(
        functools.partial(share_kernel, axis, count, stride, tuple(modes)),
        out_shape=[jax.ShapeDtypeStruct(s, x.dtype) for s, x in zip(shapes, payloads)],
        in_specs=[pl.BlockSpec(memory_space=pltpu.VMEM)] * width,
        out_specs=[pl.BlockSpec(memory_space=pl.ANY)] * width,
        scratch_shapes=[pltpu.SemaphoreType.DMA((count,))] * (2 * width)
        + [pltpu.SemaphoreType.DMA((width,))],
        compiler_params=pltpu.CompilerParams(collective_id=collective_id, has_side_effects=True),
    )(*payloads)


def outbound_kernel(groups, shards, lanes, slab_ref, part_ref, gate_ref, up_ref, down_ref,
                    near_rows, near_parts, gate_all, up_all, down_all, far_parts,
                    far_send, far_recv, far_psend, far_precv,
                    near_send, near_recv, near_psend, near_precv, local_sem,
                    lane_send, lane_recv):
    index = lax.axis_index("seq")
    far_me = lax.rem(index // shards, groups)
    far_base = index - far_me * shards
    place = lax.rem(index, shards)
    near_base = index - place
    has_right = place < shards - 1
    has_left = place > 0

    def far_member(slot):
        return peer_device("seq", far_base + slot * shards)

    def near_member(slot):
        return peer_device("seq", near_base + slot)

    barrier = pltpu.get_barrier_semaphore()

    def greet_far(step, carry):
        pl.semaphore_signal(barrier, inc=1, device_id=far_member(lax.rem(far_me + step, groups)),
                            device_id_type=pl.DeviceIdType.MESH)
        return carry

    def greet_near(step, carry):
        pl.semaphore_signal(barrier, inc=1, device_id=near_member(lax.rem(place + step, shards)),
                            device_id_type=pl.DeviceIdType.MESH)
        return carry

    lane_me = lax.axis_index("tp")

    def lane_member(slot):
        return peer_device("tp", slot)

    def greet_lane(step, carry):
        pl.semaphore_signal(barrier, inc=1, device_id=lane_member(lax.rem(lane_me + step, lanes)),
                            device_id_type=pl.DeviceIdType.MESH)
        return carry

    lax.fori_loop(1, groups, greet_far, 0)
    lax.fori_loop(1, shards, greet_near, 0)
    lax.fori_loop(1, lanes, greet_lane, 0)
    pl.semaphore_wait(barrier, groups + shards + lanes - 3)
    weight_refs = ((gate_ref, gate_all), (up_ref, up_all), (down_ref, down_all))

    def lane_target(which, landed_slot):
        source_ref, landed_ref = weight_refs[which]
        if which == 2:
            return landed_ref.at[landed_slot]
        width = source_ref.shape[1]
        return landed_ref.at[:, pl.ds(pl.multiple_of(landed_slot * width, width), width)]

    def lane_copy(which, step, slot, landed_slot):
        source_ref, landed_ref = weight_refs[which]
        return pltpu.make_async_remote_copy(
            src_ref=source_ref, dst_ref=lane_target(which, landed_slot),
            send_sem=lane_send.at[which, step], recv_sem=lane_recv.at[which, step],
            device_id=lane_member(slot), device_id_type=pl.DeviceIdType.MESH)

    def lane_start(step, carry):
        for which in range(3):
            lane_copy(which, step, lax.rem(lane_me + step, lanes), lane_me).start()
        return carry


    def far_copy(step, slot, landed_slot):
        return (
            pltpu.make_async_remote_copy(
                src_ref=slab_ref.at[slot], dst_ref=near_rows.at[place, landed_slot],
                send_sem=far_send.at[step], recv_sem=far_recv.at[step],
                device_id=far_member(slot), device_id_type=pl.DeviceIdType.MESH),
            pltpu.make_async_remote_copy(
                src_ref=part_ref, dst_ref=far_parts.at[landed_slot],
                send_sem=far_psend.at[step], recv_sem=far_precv.at[step],
                device_id=far_member(slot), device_id_type=pl.DeviceIdType.MESH),
        )

    def far_start(step, carry):
        for copy in far_copy(step, lax.rem(far_me + step, groups), far_me):
            copy.start()
        return carry

    lax.fori_loop(1, groups, far_start, 0)
    own_slab = pltpu.make_async_copy(slab_ref.at[far_me], near_rows.at[place, far_me], local_sem.at[0])
    own_part = pltpu.make_async_copy(part_ref, far_parts.at[far_me], local_sem.at[1])
    own_slab.start()
    own_part.start()
    lax.fori_loop(1, lanes, lane_start, 0)
    own_weights = [
        pltpu.make_async_copy(source_ref, lane_target(which, lane_me), local_sem.at[3 + which])
        for which, (source_ref, landed_ref) in enumerate(weight_refs)
    ]
    for copy in own_weights:
        copy.start()

    def chain_copy(direction, origin, slab):
        return pltpu.make_async_remote_copy(
            src_ref=near_rows.at[origin, slab], dst_ref=near_rows.at[origin, slab],
            send_sem=near_send.at[direction, origin, slab], recv_sem=near_recv.at[origin, slab],
            device_id=near_member(place + 1 - 2 * direction), device_id_type=pl.DeviceIdType.MESH)

    def pass_on(origin, slab, to_right, to_left):
        @pl.when(to_right)
        def _():
            chain_copy(0, origin, slab).start()

        @pl.when(to_left)
        def _():
            chain_copy(1, origin, slab).start()

    own_slab.wait()
    pass_on(place, far_me, has_right, has_left)

    def far_finish(step, carry):
        source = lax.rem(far_me - step + groups, groups)
        rows_copy, parts_copy = far_copy(step, source, source)
        rows_copy.wait_send()
        rows_copy.wait_recv()
        pass_on(place, source, has_right, has_left)
        parts_copy.wait_send()
        parts_copy.wait_recv()
        return carry

    lax.fori_loop(1, groups, far_finish, 0)
    own_part.wait()
    own_parts = pltpu.make_async_copy(far_parts, near_parts.at[place], local_sem.at[2])
    own_parts.start()

    def near_parts_copy(step, slot):
        return pltpu.make_async_remote_copy(
            src_ref=far_parts, dst_ref=near_parts.at[slot],
            send_sem=near_psend.at[step], recv_sem=near_precv.at[step],
            device_id=near_member(lax.rem(place + step, shards)),
            device_id_type=pl.DeviceIdType.MESH)

    for step in range(1, shards):
        near_parts_copy(step, place).start()

    for distance in range(1, shards):
        def relay(slab, carry, distance=distance):
            from_left = place - distance
            from_right = place + distance

            @pl.when(from_left >= 0)
            def _():
                chain_copy(0, from_left, slab).wait_recv()
                pass_on(from_left, slab, has_right, False)

            @pl.when(from_right < shards)
            def _():
                chain_copy(1, from_right, slab).wait_recv()
                pass_on(from_right, slab, False, has_left)

            return carry

        lax.fori_loop(0, groups, relay, 0)

    for origin in range(shards):
        def drain(slab, carry, origin=origin):
            @pl.when((origin <= place) & has_right)
            def _():
                chain_copy(0, origin, slab).wait_send()

            @pl.when((origin >= place) & has_left)
            def _():
                chain_copy(1, origin, slab).wait_send()

            return carry

        lax.fori_loop(0, groups, drain, 0)

    def parts_finish(step, carry):
        parts_copy = near_parts_copy(step, lax.rem(place - step + shards, shards))
        parts_copy.wait_send()
        parts_copy.wait_recv()
        return carry

    lax.fori_loop(1, shards, parts_finish, 0)
    own_parts.wait()

    def lane_finish(step, carry):
        source = lax.rem(lane_me - step + lanes, lanes)
        for which in range(3):
            copy = lane_copy(which, step, source, source)
            copy.wait_send()
            copy.wait_recv()
        return carry

    lax.fori_loop(1, lanes, lane_finish, 0)
    for copy in own_weights:
        copy.wait()


def outbound(slabs, parts, weights, groups, shards, lanes, collective_id):
    rows_shape = (shards,) + slabs.shape
    parts_shape = (shards, groups) + parts.shape
    weight_shapes = [
        jax.ShapeDtypeStruct((w.shape[0], lanes * w.shape[1]), w.dtype) for w in weights[:2]
    ] + [jax.ShapeDtypeStruct((lanes,) + weights[2].shape, weights[2].dtype)]
    return pl.pallas_call(
        functools.partial(outbound_kernel, groups, shards, lanes),
        out_shape=[jax.ShapeDtypeStruct(rows_shape, slabs.dtype),
                   jax.ShapeDtypeStruct(parts_shape, parts.dtype)] + weight_shapes,
        in_specs=[pl.BlockSpec(memory_space=pltpu.VMEM)] * 5,
        out_specs=[pl.BlockSpec(memory_space=pltpu.VMEM)] * 2
        + [pl.BlockSpec(memory_space=pl.ANY)] * 3,
        scratch_shapes=[pltpu.VMEM((groups,) + parts.shape, parts.dtype)]
        + [pltpu.SemaphoreType.DMA((groups,))] * 4
        + [pltpu.SemaphoreType.DMA((2, shards, groups)), pltpu.SemaphoreType.DMA((shards, groups))]
        + [pltpu.SemaphoreType.DMA((shards,))] * 2
        + [pltpu.SemaphoreType.DMA((8,))]
        + [pltpu.SemaphoreType.DMA((3, lanes))] * 2,
        compiler_params=pltpu.CompilerParams(collective_id=collective_id, has_side_effects=True),
    )(slabs, parts, *weights)


def merge_softmax(stacked, rows, width):
    slot_max = stacked[:, rows, :width]
    slot_sum = stacked[:, rows + 1, :width]
    joint_max = jnp.max(slot_max, axis=0)
    slot_scale = jnp.exp(slot_max - joint_max[None])
    joint_sum = jnp.sum(slot_sum * slot_scale, axis=0)
    lane_scale = jnp.repeat(slot_scale.reshape(slot_scale.shape[0], rows, -1), HD, axis=2)
    joint_acc = jnp.sum(stacked[:, :rows, :] * lane_scale, axis=0)
    return joint_max, joint_sum, joint_acc


def pack_softmax(joint_max, joint_sum, joint_acc):
    rows, lanes = joint_acc.shape
    stats = jnp.stack([joint_max, joint_sum])
    return jnp.concatenate([joint_acc, jnp.pad(stats, ((0, 2), (0, lanes - stats.shape[1])))], axis=0)


def rms_scale(hidden, norm_gain):
    values = hidden.astype(jnp.float32)
    meansq = jnp.mean(values * values, axis=-1, keepdims=True)
    return (values * lax.rsqrt(meansq + 1e-06) * norm_gain).astype(jnp.bfloat16)


def route_slots(route_rows, capacity):
    flat_routes = route_rows.reshape(-1)
    onehot = (flat_routes[:, None] == jnp.arange(EXPERTS, dtype=jnp.int32)[None, :]).astype(
        jnp.int32
    )
    earlier = jnp.cumsum(onehot, axis=0) - onehot
    slot_rank = jnp.sum(earlier * onehot, axis=1)
    return flat_routes * capacity + slot_rank


def expert_block(row_block, weights):
    gate_full, up_full, down_full = weights
    gate_pre = jnp.dot(row_block, gate_full, preferred_element_type=jnp.float32)
    up_pre = jnp.dot(row_block, up_full, preferred_element_type=jnp.float32)
    act = (jax.nn.gelu(gate_pre, approximate=True) * up_pre).astype(jnp.bfloat16)
    return jnp.dot(act, down_full, preferred_element_type=jnp.float32).astype(jnp.bfloat16)


def body(
    queries,
    keys_new,
    values_new,
    key_cache,
    value_cache,
    buckets,
    lengths,
    bias_table,
    out_proj,
    decode_in,
    prefill_in,
    routes,
    gates,
    dec_routes,
    dec_gates,
    norm_gain,
    w_gate,
    w_up,
    w_down,
):
    seq_count = lax.axis_size("seq")
    seq_index = lax.axis_index("seq")
    tp_index = lax.axis_index("tp")
    shards = seq_count // EXPERTS
    normed_pre = rms_scale(prefill_in, norm_gain)
    request_count, heads_width = queries.shape
    heads_here = heads_width // HD
    ctx_local = key_cache.shape[1]
    score_scale = 1.0 / math.sqrt(HD)
    query_rows = queries.reshape(request_count, heads_here, HD)
    key_rows = key_cache.reshape(request_count, ctx_local, heads_here, HD)
    value_rows = value_cache.reshape(request_count, ctx_local, heads_here, HD).astype(jnp.float32)
    bias_here = lax.dynamic_slice_in_dim(bias_table, tp_index * heads_here, heads_here, 1)
    bucket_hot = (
        buckets[..., None] == jnp.arange(bias_table.shape[0], dtype=jnp.int32)[None, None, :]
    ).astype(jnp.float32)
    bias_rows = jnp.einsum("rcn,nh->rhc", bucket_hot, bias_here, precision=lax.Precision.HIGHEST)
    cache_scores = (
        jnp.einsum("rhd,rchd->rhc", query_rows, key_rows, preferred_element_type=jnp.float32)
        * score_scale
        + bias_rows
    )
    positions = seq_index * ctx_local + jnp.arange(ctx_local, dtype=jnp.int32)
    valid_mask = (positions[None, :] < lengths[:, None])[:, None, :]
    cache_scores = jnp.where(valid_mask, cache_scores, -1e30)
    local_max = jnp.max(cache_scores, axis=-1)
    local_weights = jnp.where(valid_mask, jnp.exp(cache_scores - local_max[..., None]), 0.0)
    local_sum = jnp.sum(local_weights, axis=-1)
    local_acc = jnp.einsum(
        "rhc,rchd->rhd", local_weights, value_rows, precision=lax.Precision.HIGHEST
    )
    tp_count = lax.axis_size("tp")
    flat_width = request_count * heads_here
    packed_parts = pack_softmax(
        local_max.reshape(-1), local_sum.reshape(-1), local_acc.reshape(request_count, heads_here * HD)
    )
    flat_index = route_slots(routes, CAP)
    feature_width = normed_pre.shape[1]
    slabs = (
        jnp.zeros((EXPERTS * CAP, feature_width), jnp.bfloat16)
        .at[flat_index]
        .set(jnp.repeat(normed_pre, TOP, axis=0))
        .reshape(EXPERTS, CAP, feature_width)
    )
    group_count = seq_count // shards
    block_rows, block_parts, gate_all, up_all, down_all = outbound(
        slabs, packed_parts, (w_gate.T, w_up.T, w_down), group_count, shards, tp_count, 1
    )
    weights = (
        gate_all.T,
        up_all.T,
        jnp.transpose(down_all, (1, 0, 2)).reshape(down_all.shape[1], -1),
    )
    stage = merge_softmax(
        block_parts.reshape((-1,) + packed_parts.shape), request_count, flat_width
    )
    part_max = stage[0].reshape(request_count, heads_here)
    part_sum = stage[1].reshape(request_count, heads_here)
    part_acc = stage[2].reshape(request_count, heads_here, HD)
    own_key = keys_new.reshape(request_count, heads_here, HD).astype(jnp.float32)
    own_value = values_new.reshape(request_count, heads_here, HD).astype(jnp.float32)
    own_score = (
        jnp.sum(query_rows.astype(jnp.float32) * own_key, axis=-1) * score_scale
        + bias_here[0][None, :]
    )
    row_peak = jnp.maximum(part_max, own_score)
    keep_scale = jnp.exp(part_max - row_peak)
    own_weight = jnp.exp(own_score - row_peak)
    weight_total = part_sum * keep_scale + own_weight
    weighted = part_acc * keep_scale[..., None] + own_weight[..., None] * own_value
    mixed_rows = (
        (weighted / weight_total[..., None])
        .astype(jnp.bfloat16)
        .reshape(request_count, heads_width)
    )
    head_terms = jnp.dot(mixed_rows, out_proj, preferred_element_type=jnp.float32)
    (head_all,) = axis_share([head_terms], [False], "tp", tp_count, 1, 3)
    attended = jnp.sum(head_all, axis=0)
    decode_hidden = (decode_in.astype(jnp.float32) + attended).astype(jnp.bfloat16)
    normed_dec = rms_scale(decode_hidden, norm_gain)
    block_count = block_rows.shape[0] * block_rows.shape[1] * block_rows.shape[2]
    all_rows = jnp.concatenate([block_rows.reshape(block_count, feature_width), normed_dec], axis=0)
    all_out = expert_block(all_rows, weights)
    block_out = all_out[:block_count].reshape(block_rows.shape)
    dec_part = all_out[block_count:]
    part_rows, dec_block = axis_share(
        [block_out, dec_part], [True, False], "seq", shards, 1, 4
    )
    summed = jnp.zeros(part_rows.shape[1:], jnp.float32)
    dec_expert = jnp.zeros(dec_block.shape[1:], jnp.float32)
    for part in range(shards):
        summed = summed + part_rows[part].astype(jnp.float32)
        dec_expert = dec_expert + dec_block[part].astype(jnp.float32)
    my_expert = seq_index // shards
    gate_here = jnp.sum(jnp.where(dec_routes == my_expert, dec_gates, 0.0), axis=1)
    returned, dec_all = axis_share(
        [summed, gate_here[:, None] * dec_expert], [True, False], "seq", group_count, shards, 5
    )
    dec_terms = jnp.sum(dec_all, axis=0)
    decode_out = (decode_hidden.astype(jnp.float32) + dec_terms).astype(jnp.bfloat16)
    picked = jnp.take(returned.reshape(EXPERTS * CAP, -1), flat_index, axis=0)
    picked = picked.reshape(-1, TOP, picked.shape[-1])
    prefill_out = (
        prefill_in.astype(jnp.float32) + jnp.sum(gates[..., None] * picked, axis=1)
    ).astype(jnp.bfloat16)
    return (decode_out, prefill_out)


def solution(mesh):
    placed = (
        P(None, "tp"),
        P(None, "tp"),
        P(None, "tp"),
        P(None, "seq", "tp"),
        P(None, "seq", "tp"),
        P(None, "seq"),
        P(),
        P(),
        P("tp", None),
        P(),
        P(("seq", "tp"), None),
        P(("seq", "tp"), None),
        P(("seq", "tp"), None),
        P(),
        P(),
        P(),
        P("tp", "seq"),
        P("tp", "seq"),
        P("seq", "tp"),
    )
    return jax.shard_map(
        body, mesh=mesh, in_specs=placed, out_specs=(P(), P(("seq", "tp"), None)), check_vma=False
    )
```

```python
import functools
import math

import jax
import jax.numpy as jnp
from jax import lax
from jax.experimental import pallas as pl
from jax.experimental.pallas import tpu as pltpu
from jax.sharding import PartitionSpec as P

HD = 64
EXPERTS = 16
TOP = 2
CAP = 10


def peer_device(axis, peer):
    if axis == "seq":
        return (peer, lax.axis_index("tp"))
    return (lax.axis_index("seq"), peer)


def share_kernel(axis, count, stride, modes, *refs):
    width = len(modes)
    sources = refs[:width]
    landed = refs[width : 2 * width]
    send_sems = refs[2 * width : 3 * width]
    recv_sems = refs[3 * width : 4 * width]
    own_sem = refs[4 * width]
    index = lax.axis_index(axis)
    me = lax.rem(index // stride, count)
    base = index - me * stride

    def member(slot):
        return peer_device(axis, base + slot * stride)

    def piece(which, slot):
        return sources[which].at[slot] if modes[which] else sources[which]

    barrier = pltpu.get_barrier_semaphore()

    def greet(step, carry):
        pl.semaphore_signal(
            barrier,
            inc=1,
            device_id=member(lax.rem(me + step, count)),
            device_id_type=pl.DeviceIdType.MESH,
        )
        return carry

    lax.fori_loop(1, count, greet, 0)
    pl.semaphore_wait(barrier, count - 1)

    def outgoing(which, step):
        target = lax.rem(me + step, count)
        return pltpu.make_async_remote_copy(
            src_ref=piece(which, target),
            dst_ref=landed[which].at[me],
            send_sem=send_sems[which].at[step],
            recv_sem=recv_sems[which].at[step],
            device_id=member(target),
            device_id_type=pl.DeviceIdType.MESH,
        )

    def incoming(which, step):
        source = lax.rem(me - step + count, count)
        return pltpu.make_async_remote_copy(
            src_ref=piece(which, source),
            dst_ref=landed[which].at[source],
            send_sem=send_sems[which].at[step],
            recv_sem=recv_sems[which].at[step],
            device_id=member(source),
            device_id_type=pl.DeviceIdType.MESH,
        )

    def launch(step, carry):
        for which in range(width):
            outgoing(which, step).start()
        return carry

    lax.fori_loop(1, count, launch, 0)
    own_copies = [
        pltpu.make_async_copy(piece(which, me), landed[which].at[me], own_sem.at[which])
        for which in range(width)
    ]
    for copy in own_copies:
        copy.start()

    def finish(step, carry):
        for which in range(width):
            outgoing(which, step).wait_send()
            incoming(which, step).wait_recv()
        return carry

    lax.fori_loop(1, count, finish, 0)
    for copy in own_copies:
        copy.wait()


def axis_share(payloads, modes, axis, count, stride, collective_id):
    shapes = [x.shape if mode else (count,) + x.shape for x, mode in zip(payloads, modes)]
    width = len(payloads)
    return pl.pallas_call(
        functools.partial(share_kernel, axis, count, stride, tuple(modes)),
        out_shape=[jax.ShapeDtypeStruct(s, x.dtype) for s, x in zip(shapes, payloads)],
        in_specs=[pl.BlockSpec(memory_space=pltpu.VMEM)] * width,
        out_specs=[pl.BlockSpec(memory_space=pl.ANY)] * width,
        scratch_shapes=[pltpu.SemaphoreType.DMA((count,))] * (2 * width)
        + [pltpu.SemaphoreType.DMA((width,))],
        compiler_params=pltpu.CompilerParams(collective_id=collective_id, has_side_effects=True),
    )(*payloads)


def outbound_kernel(groups, shards, lanes, slab_ref, part_ref, gate_ref, up_ref, down_ref,
                    near_rows, near_parts, gate_all, up_all, down_all, far_parts,
                    far_send, far_recv, far_psend, far_precv,
                    near_send, near_recv, near_psend, near_precv, local_sem,
                    lane_send, lane_recv):
    index = lax.axis_index("seq")
    far_me = lax.rem(index // shards, groups)
    far_base = index - far_me * shards
    place = lax.rem(index, shards)
    near_base = index - place
    has_right = place < shards - 1
    has_left = place > 0

    def far_member(slot):
        return peer_device("seq", far_base + slot * shards)

    def near_member(slot):
        return peer_device("seq", near_base + slot)

    barrier = pltpu.get_barrier_semaphore()

    def greet_far(step, carry):
        pl.semaphore_signal(barrier, inc=1, device_id=far_member(lax.rem(far_me + step, groups)),
                            device_id_type=pl.DeviceIdType.MESH)
        return carry

    def greet_near(step, carry):
        pl.semaphore_signal(barrier, inc=1, device_id=near_member(lax.rem(place + step, shards)),
                            device_id_type=pl.DeviceIdType.MESH)
        return carry

    lane_me = lax.axis_index("tp")

    def lane_member(slot):
        return peer_device("tp", slot)

    def greet_lane(step, carry):
        pl.semaphore_signal(barrier, inc=1, device_id=lane_member(lax.rem(lane_me + step, lanes)),
                            device_id_type=pl.DeviceIdType.MESH)
        return carry

    lax.fori_loop(1, groups, greet_far, 0)
    lax.fori_loop(1, shards, greet_near, 0)
    lax.fori_loop(1, lanes, greet_lane, 0)
    pl.semaphore_wait(barrier, groups + shards + lanes - 3)
    weight_refs = ((gate_ref, gate_all), (up_ref, up_all), (down_ref, down_all))

    def lane_target(which, landed_slot):
        source_ref, landed_ref = weight_refs[which]
        if which == 2:
            return landed_ref.at[landed_slot]
        width = source_ref.shape[1]
        return landed_ref.at[:, pl.ds(pl.multiple_of(landed_slot * width, width), width)]

    def lane_copy(which, step, slot, landed_slot):
        source_ref, landed_ref = weight_refs[which]
        return pltpu.make_async_remote_copy(
            src_ref=source_ref, dst_ref=lane_target(which, landed_slot),
            send_sem=lane_send.at[which, step], recv_sem=lane_recv.at[which, step],
            device_id=lane_member(slot), device_id_type=pl.DeviceIdType.MESH)

    def lane_start(step, carry):
        for which in range(3):
            lane_copy(which, step, lax.rem(lane_me + step, lanes), lane_me).start()
        return carry


    def far_copy(step, slot, landed_slot):
        return (
            pltpu.make_async_remote_copy(
                src_ref=slab_ref.at[slot], dst_ref=near_rows.at[place, landed_slot],
                send_sem=far_send.at[step], recv_sem=far_recv.at[step],
                device_id=far_member(slot), device_id_type=pl.DeviceIdType.MESH),
            pltpu.make_async_remote_copy(
                src_ref=part_ref, dst_ref=far_parts.at[landed_slot],
                send_sem=far_psend.at[step], recv_sem=far_precv.at[step],
                device_id=far_member(slot), device_id_type=pl.DeviceIdType.MESH),
        )

    def far_start(step, carry):
        for copy in far_copy(step, lax.rem(far_me + step, groups), far_me):
            copy.start()
        return carry

    lax.fori_loop(1, groups, far_start, 0)
    own_slab = pltpu.make_async_copy(slab_ref.at[far_me], near_rows.at[place, far_me], local_sem.at[0])
    own_part = pltpu.make_async_copy(part_ref, far_parts.at[far_me], local_sem.at[1])
    own_slab.start()
    own_part.start()
    lax.fori_loop(1, lanes, lane_start, 0)
    own_weights = [
        pltpu.make_async_copy(source_ref, lane_target(which, lane_me), local_sem.at[3 + which])
        for which, (source_ref, landed_ref) in enumerate(weight_refs)
    ]
    for copy in own_weights:
        copy.start()

    def chain_copy(direction, origin, slab):
        return pltpu.make_async_remote_copy(
            src_ref=near_rows.at[origin, slab], dst_ref=near_rows.at[origin, slab],
            send_sem=near_send.at[direction, origin, slab], recv_sem=near_recv.at[origin, slab],
            device_id=near_member(place + 1 - 2 * direction), device_id_type=pl.DeviceIdType.MESH)

    def pass_on(origin, slab, to_right, to_left):
        @pl.when(to_right)
        def _():
            chain_copy(0, origin, slab).start()

        @pl.when(to_left)
        def _():
            chain_copy(1, origin, slab).start()

    own_slab.wait()
    pass_on(place, far_me, has_right, has_left)

    def far_finish(step, carry):
        source = lax.rem(far_me - step + groups, groups)
        rows_copy, parts_copy = far_copy(step, source, source)
        rows_copy.wait_send()
        rows_copy.wait_recv()
        pass_on(place, source, has_right, has_left)
        parts_copy.wait_send()
        parts_copy.wait_recv()
        return carry

    lax.fori_loop(1, groups, far_finish, 0)
    own_part.wait()
    own_parts = pltpu.make_async_copy(far_parts, near_parts.at[place], local_sem.at[2])
    own_parts.start()

    def near_parts_copy(step, slot):
        return pltpu.make_async_remote_copy(
            src_ref=far_parts, dst_ref=near_parts.at[slot],
            send_sem=near_psend.at[step], recv_sem=near_precv.at[step],
            device_id=near_member(lax.rem(place + step, shards)),
            device_id_type=pl.DeviceIdType.MESH)

    for step in range(1, shards):
        near_parts_copy(step, place).start()

    for distance in range(1, shards):
        def relay(slab, carry, distance=distance):
            from_left = place - distance
            from_right = place + distance

            @pl.when(from_left >= 0)
            def _():
                chain_copy(0, from_left, slab).wait_recv()
                pass_on(from_left, slab, has_right, False)

            @pl.when(from_right < shards)
            def _():
                chain_copy(1, from_right, slab).wait_recv()
                pass_on(from_right, slab, False, has_left)

            return carry

        lax.fori_loop(0, groups, relay, 0)

    for origin in range(shards):
        def drain(slab, carry, origin=origin):
            @pl.when((origin <= place) & has_right)
            def _():
                chain_copy(0, origin, slab).wait_send()

            @pl.when((origin >= place) & has_left)
            def _():
                chain_copy(1, origin, slab).wait_send()

            return carry

        lax.fori_loop(0, groups, drain, 0)

    def parts_finish(step, carry):
        parts_copy = near_parts_copy(step, lax.rem(place - step + shards, shards))
        parts_copy.wait_send()
        parts_copy.wait_recv()
        return carry

    lax.fori_loop(1, shards, parts_finish, 0)
    own_parts.wait()

    def lane_finish(step, carry):
        source = lax.rem(lane_me - step + lanes, lanes)
        for which in range(3):
            copy = lane_copy(which, step, source, source)
            copy.wait_send()
            copy.wait_recv()
        return carry

    lax.fori_loop(1, lanes, lane_finish, 0)
    for copy in own_weights:
        copy.wait()


def outbound(slabs, parts, weights, groups, shards, lanes, collective_id):
    rows_shape = (shards,) + slabs.shape
    parts_shape = (shards, groups) + parts.shape
    weight_shapes = [
        jax.ShapeDtypeStruct((w.shape[0], lanes * w.shape[1]), w.dtype) for w in weights[:2]
    ] + [jax.ShapeDtypeStruct((lanes,) + weights[2].shape, weights[2].dtype)]
    return pl.pallas_call(
        functools.partial(outbound_kernel, groups, shards, lanes),
        out_shape=[jax.ShapeDtypeStruct(rows_shape, slabs.dtype),
                   jax.ShapeDtypeStruct(parts_shape, parts.dtype)] + weight_shapes,
        in_specs=[pl.BlockSpec(memory_space=pltpu.VMEM)] * 5,
        out_specs=[pl.BlockSpec(memory_space=pl.ANY)] * 5,
        scratch_shapes=[pltpu.VMEM((groups,) + parts.shape, parts.dtype)]
        + [pltpu.SemaphoreType.DMA((groups,))] * 4
        + [pltpu.SemaphoreType.DMA((2, shards, groups)), pltpu.SemaphoreType.DMA((shards, groups))]
        + [pltpu.SemaphoreType.DMA((shards,))] * 2
        + [pltpu.SemaphoreType.DMA((8,))]
        + [pltpu.SemaphoreType.DMA((3, lanes))] * 2,
        compiler_params=pltpu.CompilerParams(collective_id=collective_id, has_side_effects=True),
    )(slabs, parts, *weights)


def merge_softmax(stacked, rows, width):
    slot_max = stacked[:, rows, :width]
    slot_sum = stacked[:, rows + 1, :width]
    joint_max = jnp.max(slot_max, axis=0)
    slot_scale = jnp.exp(slot_max - joint_max[None])
    joint_sum = jnp.sum(slot_sum * slot_scale, axis=0)
    lane_scale = jnp.repeat(slot_scale.reshape(slot_scale.shape[0], rows, -1), HD, axis=2)
    joint_acc = jnp.sum(stacked[:, :rows, :] * lane_scale, axis=0)
    return joint_max, joint_sum, joint_acc


def pack_softmax(joint_max, joint_sum, joint_acc):
    rows, lanes = joint_acc.shape
    stats = jnp.stack([joint_max, joint_sum])
    return jnp.concatenate([joint_acc, jnp.pad(stats, ((0, 2), (0, lanes - stats.shape[1])))], axis=0)


def rms_scale(hidden, norm_gain):
    values = hidden.astype(jnp.float32)
    meansq = jnp.mean(values * values, axis=-1, keepdims=True)
    return (values * lax.rsqrt(meansq + 1e-06) * norm_gain).astype(jnp.bfloat16)


def route_slots(route_rows, capacity):
    flat_routes = route_rows.reshape(-1)
    onehot = (flat_routes[:, None] == jnp.arange(EXPERTS, dtype=jnp.int32)[None, :]).astype(
        jnp.int32
    )
    earlier = jnp.cumsum(onehot, axis=0) - onehot
    slot_rank = jnp.sum(earlier * onehot, axis=1)
    return flat_routes * capacity + slot_rank


def expert_block(row_block, weights):
    gate_full, up_full, down_full = weights
    gate_pre = jnp.dot(row_block, gate_full, preferred_element_type=jnp.float32)
    up_pre = jnp.dot(row_block, up_full, preferred_element_type=jnp.float32)
    act = (jax.nn.gelu(gate_pre, approximate=True) * up_pre).astype(jnp.bfloat16)
    return jnp.dot(act, down_full, preferred_element_type=jnp.float32).astype(jnp.bfloat16)


def body(
    queries,
    keys_new,
    values_new,
    key_cache,
    value_cache,
    buckets,
    lengths,
    bias_table,
    out_proj,
    decode_in,
    prefill_in,
    routes,
    gates,
    dec_routes,
    dec_gates,
    norm_gain,
    w_gate,
    w_up,
    w_down,
):
    seq_count = lax.axis_size("seq")
    seq_index = lax.axis_index("seq")
    tp_index = lax.axis_index("tp")
    shards = seq_count // EXPERTS
    normed_pre = rms_scale(prefill_in, norm_gain)
    request_count, heads_width = queries.shape
    heads_here = heads_width // HD
    ctx_local = key_cache.shape[1]
    score_scale = 1.0 / math.sqrt(HD)
    query_rows = queries.reshape(request_count, heads_here, HD)
    key_rows = key_cache.reshape(request_count, ctx_local, heads_here, HD)
    value_rows = value_cache.reshape(request_count, ctx_local, heads_here, HD).astype(jnp.float32)
    bias_here = lax.dynamic_slice_in_dim(bias_table, tp_index * heads_here, heads_here, 1)
    bucket_hot = (
        buckets[..., None] == jnp.arange(bias_table.shape[0], dtype=jnp.int32)[None, None, :]
    ).astype(jnp.float32)
    bias_rows = jnp.einsum("rcn,nh->rhc", bucket_hot, bias_here, precision=lax.Precision.HIGHEST)
    cache_scores = (
        jnp.einsum("rhd,rchd->rhc", query_rows, key_rows, preferred_element_type=jnp.float32)
        * score_scale
        + bias_rows
    )
    positions = seq_index * ctx_local + jnp.arange(ctx_local, dtype=jnp.int32)
    valid_mask = (positions[None, :] < lengths[:, None])[:, None, :]
    cache_scores = jnp.where(valid_mask, cache_scores, -1e30)
    local_max = jnp.max(cache_scores, axis=-1)
    local_weights = jnp.where(valid_mask, jnp.exp(cache_scores - local_max[..., None]), 0.0)
    local_sum = jnp.sum(local_weights, axis=-1)
    local_acc = jnp.einsum(
        "rhc,rchd->rhd", local_weights, value_rows, precision=lax.Precision.HIGHEST
    )
    tp_count = lax.axis_size("tp")
    flat_width = request_count * heads_here
    packed_parts = pack_softmax(
        local_max.reshape(-1), local_sum.reshape(-1), local_acc.reshape(request_count, heads_here * HD)
    )
    flat_index = route_slots(routes, CAP)
    feature_width = normed_pre.shape[1]
    slabs = (
        jnp.zeros((EXPERTS * CAP, feature_width), jnp.bfloat16)
        .at[flat_index]
        .set(jnp.repeat(normed_pre, TOP, axis=0))
        .reshape(EXPERTS, CAP, feature_width)
    )
    group_count = seq_count // shards
    block_rows, block_parts, gate_all, up_all, down_all = outbound(
        slabs, packed_parts, (w_gate.T, w_up.T, w_down), group_count, shards, tp_count, 1
    )
    weights = (
        gate_all.T,
        up_all.T,
        jnp.transpose(down_all, (1, 0, 2)).reshape(down_all.shape[1], -1),
    )
    stage = merge_softmax(
        block_parts.reshape((-1,) + packed_parts.shape), request_count, flat_width
    )
    part_max = stage[0].reshape(request_count, heads_here)
    part_sum = stage[1].reshape(request_count, heads_here)
    part_acc = stage[2].reshape(request_count, heads_here, HD)
    own_key = keys_new.reshape(request_count, heads_here, HD).astype(jnp.float32)
    own_value = values_new.reshape(request_count, heads_here, HD).astype(jnp.float32)
    own_score = (
        jnp.sum(query_rows.astype(jnp.float32) * own_key, axis=-1) * score_scale
        + bias_here[0][None, :]
    )
    row_peak = jnp.maximum(part_max, own_score)
    keep_scale = jnp.exp(part_max - row_peak)
    own_weight = jnp.exp(own_score - row_peak)
    weight_total = part_sum * keep_scale + own_weight
    weighted = part_acc * keep_scale[..., None] + own_weight[..., None] * own_value
    mixed_rows = (
        (weighted / weight_total[..., None])
        .astype(jnp.bfloat16)
        .reshape(request_count, heads_width)
    )
    head_terms = jnp.dot(mixed_rows, out_proj, preferred_element_type=jnp.float32)
    (head_all,) = axis_share([head_terms], [False], "tp", tp_count, 1, 3)
    attended = jnp.sum(head_all, axis=0)
    decode_hidden = (decode_in.astype(jnp.float32) + attended).astype(jnp.bfloat16)
    normed_dec = rms_scale(decode_hidden, norm_gain)
    block_count = block_rows.shape[0] * block_rows.shape[1] * block_rows.shape[2]
    all_rows = jnp.concatenate([block_rows.reshape(block_count, feature_width), normed_dec], axis=0)
    all_out = expert_block(all_rows, weights)
    block_out = all_out[:block_count].reshape(block_rows.shape)
    dec_part = all_out[block_count:]
    part_rows, dec_block = axis_share(
        [block_out, dec_part], [True, False], "seq", shards, 1, 4
    )
    summed = jnp.zeros(part_rows.shape[1:], jnp.float32)
    dec_expert = jnp.zeros(dec_block.shape[1:], jnp.float32)
    for part in range(shards):
        summed = summed + part_rows[part].astype(jnp.float32)
        dec_expert = dec_expert + dec_block[part].astype(jnp.float32)
    my_expert = seq_index // shards
    gate_here = jnp.sum(jnp.where(dec_routes == my_expert, dec_gates, 0.0), axis=1)
    returned, dec_all = axis_share(
        [summed, gate_here[:, None] * dec_expert], [True, False], "seq", group_count, shards, 5
    )
    dec_terms = jnp.sum(dec_all, axis=0)
    decode_out = (decode_hidden.astype(jnp.float32) + dec_terms).astype(jnp.bfloat16)
    picked = jnp.take(returned.reshape(EXPERTS * CAP, -1), flat_index, axis=0)
    picked = picked.reshape(-1, TOP, picked.shape[-1])
    prefill_out = (
        prefill_in.astype(jnp.float32) + jnp.sum(gates[..., None] * picked, axis=1)
    ).astype(jnp.bfloat16)
    return (decode_out, prefill_out)


def solution(mesh):
    placed = (
        P(None, "tp"),
        P(None, "tp"),
        P(None, "tp"),
        P(None, "seq", "tp"),
        P(None, "seq", "tp"),
        P(None, "seq"),
        P(),
        P(),
        P("tp", None),
        P(),
        P(("seq", "tp"), None),
        P(("seq", "tp"), None),
        P(("seq", "tp"), None),
        P(),
        P(),
        P(),
        P("tp", "seq"),
        P("tp", "seq"),
        P("seq", "tp"),
    )
    return jax.shard_map(
        body, mesh=mesh, in_specs=placed, out_specs=(P(), P(("seq", "tp"), None)), check_vma=False
    )
```
